32 devices in a mesh: row: 4 (over x, core), col: 8 (over z, y).
Axes of the slice: x: 2, y: 2, z: 4, core: 2. Of those that a mesh axis runs over, the one named last changes fastest.
Arguments:
- activations: bfloat16 [64, 9216], P('row', 'col'), may hold values from -0.75 to 0.75
- cotangent: bfloat16 [64, 9216], P('col', 'row'), may hold values from -6 to 6
- weight: bfloat16 [9216, 9216], P('row', 'col'), may hold values from -0.0625 to 0.0625
- momentum: float32 [9216, 9216], P('row', 'col'), may hold values from -500 to 500
- right_factor: float32 [9216, 256], P('col'), may hold values from -6 to 6
Outputs:
- input_grad: bfloat16 [64, 9216], P('row', 'col')
- momentum_next: float32 [9216, 9216], P('row', 'col')
- right_next: float32 [9216, 256], P('col')
- weight_step: bfloat16 [9216, 9216], P('row', 'col')
The draws below stay inside these ranges and needn't reach their ends.
All inputs are finite; a program needn't handle non-finite values.
Results may differ from the reference program's by a relative error of at most 0.0011.
Values may be sent and summed in bfloat16 or wider, within the bound.
A program may use at most 128 MiB of HBM per device.

```python
import math
import jax
import jax.numpy as jnp
from jax import lax

DOUT = 9216
DIN = 9216
RANK = 256
TOKENS = 64


def draw_momentum(key, part):
    base_key, row_key, col_key = jax.random.split(jax.random.fold_in(key, 11), 3)
    values = jnp.clip(jax.random.normal(base_key, (DOUT, DIN), jnp.float32), -5.0, 5.0)
    half_span = 0.5 * math.log(10.0)
    row_scale = 3.0 ** (jnp.arange(DOUT, dtype=jnp.float32) / DOUT)
    row_scale = row_scale * jnp.exp(jax.random.uniform(row_key, (DOUT,), jnp.float32, -half_span, half_span))
    col_scale = 3.0 ** (jnp.arange(DIN, dtype=jnp.float32) / DIN)
    col_scale = col_scale * jnp.exp(jax.random.uniform(col_key, (DIN,), jnp.float32, -half_span, half_span))
    return (values * row_scale[:, None] * col_scale[None, :]).astype(jnp.float32)


def block_scale(rng, shape, shards, smallest, top_value):
    def one(position, shards_of):
        draws = jax.random.uniform(jax.random.fold_in(jax.random.fold_in(rng, 6), position), (shards_of,), jnp.float32, smallest / len(shards), top_value / len(shards))
        return jnp.repeat(jnp.exp(draws), shape[position] // shards_of).reshape((-1,) + (1,) * (len(shape) - position - 1))

    level = one(*shards[0])
    for cut in shards[1:]:
        level = level * one(*cut)
    return level


def noise(rng, extent, width, bound, shards=(), kind=jnp.bfloat16):
    array = jax.random.normal(rng, extent, jnp.float32) * width
    if len(shards) > 0:
        array = block_scale(rng, extent, shards, -0.22, 0.18) * array
    return jnp.clip(array, min=-bound, max=bound).astype(kind)


def setup_inputs(seed: int = 0) -> dict:
    seeds = jax.random.split(jax.random.key(seed), 6)
    return {
        "activations": noise(seeds[0], (TOKENS, DIN), TOKENS ** -0.5, 0.75, ((0, 4), (1, 8))),
        "cotangent": noise(seeds[1], (TOKENS, DOUT), 1.0, 6.0, ((0, 8), (1, 4))),
        "weight": noise(seeds[2], (DOUT, DIN), DOUT ** -0.5, 0.0625, ((0, 4), (1, 8))),
        "momentum": draw_momentum(jax.random.fold_in(seeds[5], 71), 0),
        "right_factor": noise(seeds[4], (DIN, RANK), 1.0, 6.0, ((0, 8),), jnp.float32),
    }


momentum_decay = 0.6
ridge_weight = 0.001

def reference(activations, cotangent, weight, momentum, right_factor):
    highest = lax.Precision.HIGHEST
    input_grad = jnp.dot(cotangent.astype(jnp.float32), weight.astype(jnp.float32), preferred_element_type=jnp.float32).astype(jnp.bfloat16)
    weight_grad = jnp.dot(cotangent.T.astype(jnp.float32), activations.astype(jnp.float32), preferred_element_type=jnp.float32)
    buffer = momentum + weight_grad
    left = jnp.dot(buffer, right_factor, precision=highest) / jnp.sqrt(jnp.float32(DIN))
    gram_matrix = jnp.dot(left.T, left, precision=highest) + ridge_weight * DOUT * jnp.eye(RANK, dtype=jnp.float32)
    factor_low = jnp.linalg.cholesky(gram_matrix)
    orthonormal = jax.scipy.linalg.solve_triangular(factor_low, left.T, lower=True).T
    right = jnp.dot(buffer.T, orthonormal, precision=highest)
    squares = lax.optimization_barrier(jnp.sum(right * right, axis=0))
    right_next = right * lax.rsqrt(squares / DIN + 1e-06)
    momentum_next = buffer - (1.0 - momentum_decay) * jnp.dot(orthonormal, right.T, precision=highest)
    step_scale = jnp.sqrt(jnp.float32(DOUT) / RANK)
    weight_step = (step_scale * jnp.dot(orthonormal, right_next.T, precision=highest)).astype(jnp.bfloat16)
    return (input_grad, momentum_next, right_next, weight_step)
```

```python
import functools

import jax
import jax.numpy as jnp
from jax import lax
from jax.experimental import pallas as pl
from jax.experimental.pallas import tpu as pltpu
from jax.sharding import PartitionSpec as P

momentum_decay = 0.6
ridge_weight = 0.001

HIGHEST = lax.Precision.HIGHEST
HIGH = lax.Precision.HIGH
SUBLANES = 8
LANES = 128
MESH = pl.DeviceIdType.MESH


def contract(left_side, right_side, left_dim, right_dim, precision=None):
    return lax.dot_general(
        left_side,
        right_side,
        (((left_dim,), (right_dim,)), ((), ())),
        precision=precision,
        preferred_element_type=jnp.float32,
    )


def identity(size):
    shape = (size, size)
    same = lax.broadcasted_iota(jnp.int32, shape, 0) == lax.broadcasted_iota(jnp.int32, shape, 1)
    return jnp.where(same, 1.0, 0.0).astype(jnp.float32)


def two_stages(size):
    inner = max(k for k in range(1, size + 1) if size % k == 0 and k * k <= size)
    return inner, size // inner


def split(value):
    high = value.astype(jnp.bfloat16)
    return high, (value - high.astype(jnp.float32)).astype(jnp.bfloat16)


def contract_split(left_pair, right_pair, left_dim, right_dim):
    total = contract(left_pair[0], right_pair[0], left_dim, right_dim)
    total = total + contract(left_pair[1], right_pair[0], left_dim, right_dim)
    return total + contract(left_pair[0], right_pair[1], left_dim, right_dim)


def inverse_factor_body(block, ridge, gram_ref, inverse_ref, work, corner):
    size = gram_ref.shape[0]
    work[:, :size] = gram_ref[...] + ridge * identity(size)
    work[:, size:] = identity(size)
    row_in_group = lax.broadcasted_iota(jnp.int32, (SUBLANES, 2 * block), 0)
    for low in range(0, size, block):
        high = low + block
        corner[:, :block] = work[low:high, low:high]
        corner[:, block:] = identity(block)
        groups = [corner[g : g + SUBLANES, :] for g in range(0, block, SUBLANES)]
        for k in range(block):
            own, inside = divmod(k, SUBLANES)
            pivot_row = groups[own][inside : inside + 1, :]
            scaled = pivot_row / pivot_row[:, k : k + 1]
            for g in range(own, len(groups)):
                factor = groups[g][:, k : k + 1]
                change = factor * scaled
                if g == own:
                    change = jnp.where(row_in_group > inside, change, 0.0)
                groups[g] = groups[g] - change
        for g, rows in enumerate(groups):
            corner[g * SUBLANES : (g + 1) * SUBLANES, :] = rows
        pivots = jnp.sum(corner[:, :block] * identity(block), axis=1, keepdims=True)
        corner_inverse = corner[:, block:] * (1.0 / jnp.sqrt(pivots))
        panel = contract(corner_inverse, work[low:high, :], 1, 0, HIGHEST)
        inverse_ref[low:high, :] = panel[:, size:]
        if high < size:
            update = contract(panel[:, :size], panel, 0, 0, HIGHEST)
            work[high:, :] = work[high:, :] - update[high:, :]


def inverse_factor(gram_matrix, ridge):
    size = gram_matrix.shape[0]
    block = min(64, size)
    return pl.pallas_call(
        functools.partial(inverse_factor_body, block, ridge),
        out_shape=jax.ShapeDtypeStruct((size, size), jnp.float32),
        in_specs=[pl.BlockSpec(memory_space=pltpu.VMEM)],
        out_specs=pl.BlockSpec(memory_space=pltpu.VMEM),
        scratch_shapes=[
            pltpu.VMEM((size, 2 * size), jnp.float32),
            pltpu.VMEM((block, 2 * block), jnp.float32),
        ],
        cost_estimate=pl.CostEstimate(flops=20_000_000_000, bytes_accessed=8 * size * size, transcendentals=0),
        name="inverse_factor",
    )(gram_matrix)


def plain_shards(rows_of, cols_of, activations, cotangent, weight, momentum, right_factor):
    dout = momentum.shape[0] * rows_of
    din = momentum.shape[1] * cols_of
    rank = right_factor.shape[1]
    cot_tokens = lax.all_gather(cotangent, "col", axis=0, tiled=True)
    act_tokens = lax.all_gather(activations, "row", axis=0, tiled=True)
    held_part = contract(momentum, right_factor, 1, 0, HIGH)
    act_part = contract(act_tokens.astype(jnp.float32), right_factor, 1, 0, HIGH)
    grad_part = contract(cot_tokens.astype(jnp.float32), act_part, 0, 0, HIGH)
    left_part = (held_part + grad_part) / jnp.sqrt(jnp.float32(din))
    left_piece = lax.psum_scatter(left_part, "col", scatter_dimension=0, tiled=True)
    input_part = jnp.dot(cot_tokens, weight, preferred_element_type=jnp.float32)
    buffer = momentum + contract(cot_tokens, act_tokens, 0, 0, None)
    left_block = lax.all_gather(left_piece, "col", axis=0, tiled=True)
    gram_matrix = lax.psum(contract(left_block, left_block, 0, 0, HIGHEST), "row")
    projected_part = contract(buffer, left_block, 0, 0, HIGH)
    gram_matrix, projected_part = lax.optimization_barrier((gram_matrix, projected_part))
    projected = lax.psum(projected_part, "row")
    projected, input_part = lax.optimization_barrier((projected, input_part))
    input_sums = lax.psum_scatter(input_part, "row", scatter_dimension=0, tiled=True)
    inverse = inverse_factor(gram_matrix, ridge_weight * dout)
    orthonormal = contract(left_block, inverse, 1, 1, HIGHEST)
    right = contract(projected, inverse, 1, 1, HIGHEST)
    squares = lax.psum(jnp.sum(right * right, axis=0), "col")
    momentum_next = buffer - (1.0 - momentum_decay) * contract(orthonormal, right, 1, 1, HIGH)
    right_next = right * lax.rsqrt(squares / din + 1e-06)
    step_scale = jnp.sqrt(jnp.float32(dout) / rank)
    weight_step = (step_scale * contract(orthonormal, right_next, 1, 1, HIGH)).astype(jnp.bfloat16)
    return (input_sums.astype(jnp.bfloat16), momentum_next, right_next, weight_step)


def remote(source, target, send_sem, recv_sem, device):
    return pltpu.make_async_remote_copy(
        src_ref=source,
        dst_ref=target,
        send_sem=send_sem,
        recv_sem=recv_sem,
        device_id=device,
        device_id_type=MESH,
    )


def greet(devices):
    barrier = pltpu.get_barrier_semaphore()
    for device in devices:
        pl.semaphore_signal(barrier, inc=1, device_id=device, device_id_type=MESH)
    pl.semaphore_wait(barrier, len(devices))


def left_kernel(
    n_row,
    n_col,
    act_ref,
    cot_ref,
    weight_hbm,
    momentum_hbm,
    factor_ref,
    left_ref,
    projected_ref,
    gram_ref,
    input_ref,
    buffer_hbm,
    act_all,
    cot_all,
    cot_flat,
    cot_turned,
    chunks,
    chunk_high,
    chunk_low,
    weight,
    factor_high,
    factor_low,
    send_inner,
    recv_inner,
    totals,
    recv_outer,
    input_send,
    input_recv,
    load_sem,
    store_sem,
    weight_sem,
    act_sem,
    cot_sem,
    inner_sem,
    outer_sem,
    gather_outer_sem,
    gather_inner_sem,
    input_sem,
):
    inner, outer = two_stages(n_col)
    row, col = lax.axis_index("row"), lax.axis_index("col")
    me_in, me_out = lax.rem(col, inner), lax.div(col, inner)
    piece, cols = chunks.shape[1], chunks.shape[2]
    din = cols * n_col
    act_rows = act_ref.shape[0]
    tokens = act_rows * n_row

    def outer_id(k):
        return lax.rem(me_out + 1 + k, outer)

    def chunk_at(j):
        d, k = divmod(j, outer) if isinstance(j, int) else (lax.div(j, outer), lax.rem(j, outer))
        return outer_id(k) * inner + lax.rem(me_in + 1 + d, inner)

    def load(j):
        q = chunk_at(j)
        return pltpu.make_async_copy(
            momentum_hbm.at[pl.ds(pl.multiple_of(q * piece, SUBLANES), piece), :], chunks.at[j], load_sem.at[j]
        )

    def store(j):
        q = chunk_at(j)
        return pltpu.make_async_copy(
            chunks.at[j], buffer_hbm.at[pl.ds(pl.multiple_of(q * piece, SUBLANES), piece), :], store_sem.at[j]
        )

    for j in range(n_col):
        load(j).start()
    weight_copy = pltpu.make_async_copy(weight_hbm, weight, weight_sem)
    weight_copy.start()

    row_peers = [lax.rem(row + d, n_row) for d in range(1, n_row)]
    col_peers = [lax.rem(col + d, n_col) for d in range(1, n_col)]
    greet([(peer, col) for peer in row_peers] + [(row, peer) for peer in col_peers])

    cot_copies = [
        remote(cot_ref, cot_all.at[col], cot_sem.at[0, d], cot_sem.at[1, d], (row, peer))
        for d, peer in enumerate(col_peers)
    ]
    act_copies = [
        remote(act_ref, act_all.at[row], act_sem.at[0, d], act_sem.at[1, d], (peer, col))
        for d, peer in enumerate(row_peers)
    ]
    for copy in cot_copies + act_copies:
        copy.start()
    act_all[row] = act_ref[...]
    cot_all[col] = cot_ref[...]
    factor_high[...], factor_low[...] = split(factor_ref[...])
    for copy in act_copies + cot_copies:
        copy.wait()

    def turn(b, carry):
        lanes = pl.ds(pl.multiple_of(b * LANES, LANES), LANES)
        slab = cot_all[:, :, lanes].astype(jnp.float32).reshape(tokens, LANES)
        cot_flat[:, lanes] = slab.astype(jnp.bfloat16)
        cot_turned[lanes, :] = slab.T.astype(jnp.bfloat16)
        return carry

    lax.fori_loop(0, cot_ref.shape[1] // LANES, turn, 0)

    def partial(j):
        q = chunk_at(j)
        load(j).wait()
        turned = cot_turned[pl.ds(pl.multiple_of(q * piece, 2 * SUBLANES), piece), :]
        value = chunks[j] + contract(turned, act_all[...].reshape(tokens, cols), 1, 0)
        chunks[j] = value
        high, low = split(value)
        chunk_high[j] = high
        chunk_low[j] = low
        return contract_split((high, low), (factor_high[...], factor_low[...]), 1, 0)

    def inner_copy(d, k):
        peer = me_out * inner + lax.rem(me_in + 1 + d, inner)
        return remote(
            send_inner.at[d, k], recv_inner.at[d, k], inner_sem.at[0, d, k], inner_sem.at[1, d, k], (row, peer)
        )

    def outer_copy(k):
        peer = outer_id(k) * inner + me_in
        return remote(totals.at[k], recv_outer.at[k], outer_sem.at[0, k], outer_sem.at[1, k], (row, peer))

    for d in range(inner - 1):

        def push(k, carry, d=d):
            send_inner[d, k] = partial(d * outer + k)
            inner_copy(d, k).start()
            return carry

        lax.fori_loop(0, outer, push, 0)

    def keep(k, carry):
        totals[k] = partial((inner - 1) * outer + k)
        return carry

    lax.fori_loop(0, outer, keep, 0)

    for j in range(n_col):
        store(j).start()

    weight_copy.wait()
    input_part = contract(cot_flat[...], weight[...], 1, 0)
    input_send[...] = input_part.reshape(n_row, act_rows, cols)
    input_copies = [
        remote(input_send.at[peer], input_recv.at[d], input_sem.at[0, d], input_sem.at[1, d], (peer, col))
        for d, peer in enumerate(row_peers)
    ]
    for copy in input_copies:
        copy.start()

    for k in range(outer):
        total = totals[k]
        for d in range(inner - 1):
            inner_copy(d, k).wait()
            total = total + recv_inner[d, k]
        totals[k] = total
        if k < outer - 1:
            outer_copy(k).start()
    mine = totals[outer - 1]
    for k in range(outer - 1):
        outer_copy(k).wait()
        mine = mine + recv_outer[k]
    left_ref[col] = mine / jnp.sqrt(jnp.float32(din))

    def gather_outer(k):
        peer = outer_id(k) * inner + me_in
        return remote(
            left_ref.at[col], left_ref.at[col], gather_outer_sem.at[0, k], gather_outer_sem.at[1, k], (row, peer)
        )

    def source_outer(k):
        return lax.rem(me_out + outer - k, outer)

    def gather_inner(d, k):
        q = source_outer(k) * inner + me_in
        peer = me_out * inner + lax.rem(me_in + 1 + d, inner)
        return remote(
            left_ref.at[q], left_ref.at[q], gather_inner_sem.at[0, d, k], gather_inner_sem.at[1, d, k], (row, peer)
        )

    for k in range(outer - 1):
        gather_outer(k).start()
    for d in range(inner - 1):
        gather_inner(d, 0).start()

    def place(q):
        d = lax.rem(lax.rem(q, inner) - me_in - 1 + 2 * inner, inner)
        k = lax.rem(lax.div(q, inner) - me_out - 1 + 2 * outer, outer)
        return d * outer + k

    def absorb(q, first):
        value = left_ref[q]
        pair = split(value)
        j = place(q)
        gram = contract(value, value, 0, 0, HIGHEST)
        projected = contract_split(pair, (chunk_high[j], chunk_low[j]), 0, 0)
        if first:
            gram_ref[...] = gram
            projected_ref[...] = projected
        else:
            gram_ref[...] = gram_ref[...] + gram
            projected_ref[...] = projected_ref[...] + projected

    absorb(col, True)
    for k in range(1, outer):
        gather_outer(k - 1).wait()
        for d in range(inner - 1):
            gather_inner(d, k).start()
        absorb(source_outer(k) * inner + me_in, False)
        for d in range(inner - 1):
            gather_inner(d, k - 1).wait()
            absorb(source_outer(k - 1) * inner + lax.rem(me_in - 1 - d + inner, inner), False)
    for d in range(inner - 1):
        gather_inner(d, outer - 1).wait()
        absorb(source_outer(outer - 1) * inner + lax.rem(me_in - 1 - d + inner, inner), False)

    total = input_send[row]
    for d, copy in enumerate(input_copies):
        copy.wait()
        total = total + input_recv[d]
    input_ref[...] = total.astype(jnp.bfloat16)
    for j in range(n_col):
        store(j).wait()


def left_call(n_row, n_col, activations, cotangent, weight, momentum, right_factor):
    inner, outer = two_stages(n_col)
    rows, cols = momentum.shape
    rank = right_factor.shape[1]
    piece = rows // n_col
    act_rows, cot_rows = activations.shape[0], cotangent.shape[0]
    tokens = act_rows * n_row
    f32, bf16 = jnp.float32, jnp.bfloat16
    vmem = pl.BlockSpec(memory_space=pltpu.VMEM)
    hbm = pl.BlockSpec(memory_space=pl.ANY)
    dma = pltpu.SemaphoreType.DMA
    return pl.pallas_call(
        functools.partial(left_kernel, n_row, n_col),
        out_shape=(
            jax.ShapeDtypeStruct((n_col, piece, rank), f32),
            jax.ShapeDtypeStruct((rank, cols), f32),
            jax.ShapeDtypeStruct((rank, rank), f32),
            jax.ShapeDtypeStruct((act_rows, cols), bf16),
            jax.ShapeDtypeStruct((rows, cols), f32),
        ),
        in_specs=[vmem, vmem, hbm, hbm, vmem],
        out_specs=(vmem, vmem, vmem, vmem, hbm),
        scratch_shapes=[
            pltpu.VMEM((n_row, act_rows, cols), bf16),
            pltpu.VMEM((n_col, cot_rows, rows), bf16),
            pltpu.VMEM((tokens, rows), bf16),
            pltpu.VMEM((rows, tokens), bf16),
            pltpu.VMEM((n_col, piece, cols), f32),
            pltpu.VMEM((n_col, piece, cols), bf16),
            pltpu.VMEM((n_col, piece, cols), bf16),
            pltpu.VMEM((rows, cols), bf16),
            pltpu.VMEM((cols, rank), bf16),
            pltpu.VMEM((cols, rank), bf16),
            pltpu.VMEM((inner - 1, outer, piece, rank), f32),
            pltpu.VMEM((inner - 1, outer, piece, rank), f32),
            pltpu.VMEM((outer, piece, rank), f32),
            pltpu.VMEM((outer - 1, piece, rank), f32),
            pltpu.VMEM((n_row, act_rows, cols), f32),
            pltpu.VMEM((n_row - 1, act_rows, cols), f32),
            dma((n_col,)),
            dma((n_col,)),
            dma,
            dma((2, n_row - 1)),
            dma((2, n_col - 1)),
            dma((2, inner - 1, outer)),
            dma((2, outer - 1)),
            dma((2, outer - 1)),
            dma((2, inner - 1, outer)),
            dma((2, n_row - 1)),
        ],
        compiler_params=pltpu.CompilerParams(
            collective_id=1, has_side_effects=True, vmem_limit_bytes=60 * 1024 * 1024
        ),
        name="left_factor",
    )(activations, cotangent, weight, momentum, right_factor)


def right_kernel(
    n_row,
    n_col,
    ridge,
    din,
    gram_ref,
    projected_ref,
    left_ref,
    orthonormal_ref,
    right_ref,
    scale_ref,
    gram_in,
    gram_out,
    gram_all,
    proj_in,
    proj_out,
    proj_all,
    inverse,
    work,
    corner,
    squares_all,
    gram_in_sem,
    gram_out_sem,
    gram_all_sem,
    proj_in_sem,
    proj_out_sem,
    proj_all_sem,
    squares_sem,
):
    inner, outer = two_stages(n_row)
    row, col = lax.axis_index("row"), lax.axis_index("col")
    me_in, me_out = lax.rem(row, inner), lax.div(row, inner)
    rank = gram_ref.shape[0]
    part = rank // inner
    inner_peers = [(lax.rem(me_in + 1 + d, inner)) for d in range(inner - 1)]
    outer_peers = [(lax.rem(me_out + 1 + d, outer)) for d in range(outer - 1)]
    col_peers = [lax.rem(col + d, n_col) for d in range(1, n_col)]
    greet(
        [(me_out * inner + peer, col) for peer in inner_peers]
        + [(peer * inner + me_in, col) for peer in outer_peers]
        + [(row, peer) for peer in col_peers]
    )

    def at(index):
        return pl.ds(pl.multiple_of(index * part, SUBLANES), part)

    def reduce_in(source, buffer, sem):
        copies = [
            remote(source.at[at(peer), :], buffer.at[d], sem.at[0, d], sem.at[1, d], (me_out * inner + peer, col))
            for d, peer in enumerate(inner_peers)
        ]
        for copy in copies:
            copy.start()
        return copies

    def exchange_out(source, copies_in, buffer_in, buffer_out, sem):
        total = source[at(me_in), :]
        for d, copy in enumerate(copies_in):
            copy.wait()
            total = total + buffer_in[d]
        buffer_out[me_out] = total
        copies = [
            remote(
                buffer_out.at[me_out], buffer_out.at[me_out], sem.at[0, d], sem.at[1, d], (peer * inner + me_in, col)
            )
            for d, peer in enumerate(outer_peers)
        ]
        for copy in copies:
            copy.start()
        return copies

    def gather_in(copies_out, buffer_out, whole, sem):
        for copy in copies_out:
            copy.wait()
        total = buffer_out[0]
        for o in range(1, outer):
            total = total + buffer_out[o]
        whole[at(me_in), :] = total
        copies = [
            remote(
                whole.at[at(me_in), :], whole.at[at(me_in), :], sem.at[0, d], sem.at[1, d], (me_out * inner + peer, col)
            )
            for d, peer in enumerate(inner_peers)
        ]
        for copy in copies:
            copy.start()
        return copies

    gram_copies = reduce_in(gram_ref, gram_in, gram_in_sem)
    proj_copies = reduce_in(projected_ref, proj_in, proj_in_sem)
    gram_copies = exchange_out(gram_ref, gram_copies, gram_in, gram_out, gram_out_sem)
    proj_copies = exchange_out(projected_ref, proj_copies, proj_in, proj_out, proj_out_sem)
    gram_copies = gather_in(gram_copies, gram_out, gram_all, gram_all_sem)
    for copy in gram_copies:
        copy.wait()
    inverse_factor_body(corner.shape[0], ridge, gram_all, inverse, work, corner)
    proj_copies = gather_in(proj_copies, proj_out, proj_all, proj_all_sem)
    factor = split(inverse[...])
    for q in range(n_col):
        orthonormal_ref[q] = contract_split(split(left_ref[q]), factor, 1, 1)
    for copy in proj_copies:
        copy.wait()
    right = contract_split(factor, split(proj_all[...]), 1, 0)
    right_ref[...] = right
    squares = jnp.sum(right * right, axis=1, keepdims=True)
    squares = jnp.broadcast_to(squares, (rank, LANES)).T[:SUBLANES, :]
    squares_all[col] = squares
    copies = [
        remote(squares_all.at[col], squares_all.at[col], squares_sem.at[0, d], squares_sem.at[1, d], (row, peer))
        for d, peer in enumerate(col_peers)
    ]
    for copy in copies:
        copy.start()
    for copy in copies:
        copy.wait()
    total = squares_all[0]
    for q in range(1, n_col):
        total = total + squares_all[q]
    scale_ref[...] = lax.rsqrt(total / din + 1e-06)


def right_call(n_row, n_col, ridge, din, gram_part, projected_part, left):
    inner, outer = two_stages(n_row)
    rank, cols = projected_part.shape
    part = rank // inner
    block = min(64, rank)
    f32 = jnp.float32
    vmem = pl.BlockSpec(memory_space=pltpu.VMEM)
    dma = pltpu.SemaphoreType.DMA
    return pl.pallas_call(
        functools.partial(right_kernel, n_row, n_col, ridge, din),
        out_shape=(
            jax.ShapeDtypeStruct(left.shape, f32),
            jax.ShapeDtypeStruct((rank, cols), f32),
            jax.ShapeDtypeStruct((SUBLANES, rank), f32),
        ),
        in_specs=[vmem] * 3,
        out_specs=(vmem,) * 3,
        scratch_shapes=[
            pltpu.VMEM((inner - 1, part, rank), f32),
            pltpu.VMEM((outer, part, rank), f32),
            pltpu.VMEM((rank, rank), f32),
            pltpu.VMEM((inner - 1, part, cols), f32),
            pltpu.VMEM((outer, part, cols), f32),
            pltpu.VMEM((rank, cols), f32),
            pltpu.VMEM((rank, rank), f32),
            pltpu.VMEM((rank, 2 * rank), f32),
            pltpu.VMEM((block, 2 * block), f32),
            pltpu.VMEM((n_col, SUBLANES, rank), f32),
            dma((2, inner - 1)),
            dma((2, outer - 1)),
            dma((2, inner - 1)),
            dma((2, inner - 1)),
            dma((2, outer - 1)),
            dma((2, inner - 1)),
            dma((2, n_col - 1)),
        ],
        compiler_params=pltpu.CompilerParams(
            collective_id=2, has_side_effects=True, vmem_limit_bytes=60 * 1024 * 1024
        ),
        name="right_factor",
    )(gram_part, projected_part, left)


def output_kernel(
    step_scale,
    buffer_ref,
    orthonormal_ref,
    right_ref,
    scale_ref,
    momentum_ref,
    step_ref,
    next_ref,
    right_high,
    right_low,
):
    @pl.when(pl.program_id(0) == 0)
    def _():
        right_high[...], right_low[...] = split(right_ref[...])
        next_ref[...] = right_ref[...].T * scale_ref[:1, :]

    right = (right_high[...], right_low[...])
    orthonormal = orthonormal_ref[...]
    momentum_ref[...] = buffer_ref[...] - (1.0 - momentum_decay) * contract_split(split(orthonormal), right, 1, 0)
    scaled = orthonormal * scale_ref[:1, :]
    step_ref[...] = (step_scale * contract_split(split(scaled), right, 1, 0)).astype(jnp.bfloat16)


def output_call(step_scale, buffer, orthonormal, right, scale):
    rows, cols = buffer.shape
    rank = right.shape[0]
    tile = max(t for t in range(16, 289, 16) if rows % t == 0)
    f32 = jnp.float32
    return pl.pallas_call(
        functools.partial(output_kernel, step_scale),
        grid=(rows // tile,),
        out_shape=(
            jax.ShapeDtypeStruct((rows, cols), f32),
            jax.ShapeDtypeStruct((rows, cols), jnp.bfloat16),
            jax.ShapeDtypeStruct((cols, rank), f32),
        ),
        in_specs=[
            pl.BlockSpec((tile, cols), lambda i: (i, 0)),
            pl.BlockSpec((tile, rank), lambda i: (i, 0)),
            pl.BlockSpec((rank, cols), lambda i: (0, 0)),
            pl.BlockSpec(scale.shape, lambda i: (0, 0)),
        ],
        out_specs=(
            pl.BlockSpec((tile, cols), lambda i: (i, 0)),
            pl.BlockSpec((tile, cols), lambda i: (i, 0)),
            pl.BlockSpec((cols, rank), lambda i: (0, 0)),
        ),
        scratch_shapes=[pltpu.VMEM((rank, cols), jnp.bfloat16), pltpu.VMEM((rank, cols), jnp.bfloat16)],
        compiler_params=pltpu.CompilerParams(
            dimension_semantics=("arbitrary",), vmem_limit_bytes=40 * 1024 * 1024
        ),
        name="outputs",
    )(buffer, orthonormal, right, scale)


def kernel_shards(n_row, n_col, activations, cotangent, weight, momentum, right_factor):
    rows, cols = momentum.shape
    rank = right_factor.shape[1]
    dout, din = rows * n_row, cols * n_col
    left, projected, gram, input_grad, buffer = left_call(
        n_row, n_col, activations, cotangent, weight, momentum, right_factor
    )
    orthonormal, right, scale = right_call(n_row, n_col, ridge_weight * dout, din, gram, projected, left)
    step_scale = (dout / rank) ** 0.5
    momentum_next, weight_step, right_next = output_call(
        step_scale, buffer, orthonormal.reshape(rows, rank), right, scale
    )
    return input_grad, momentum_next, right_next, weight_step


def shards(n_row, n_col, activations, cotangent, weight, momentum, right_factor):
    rows, cols = momentum.shape
    rank = right_factor.shape[1]
    aligned = (
        rows % (n_col * 2 * SUBLANES) == 0
        and rows % LANES == 0
        and cols % LANES == 0
        and rank % LANES == 0
        and activations.shape[0] % (2 * SUBLANES) == 0
        and cotangent.shape[0] % SUBLANES == 0
        and two_stages(n_row)[0] > 1
        and two_stages(n_col)[0] > 1
        and rank % (two_stages(n_row)[0] * SUBLANES) == 0
    )
    chosen = kernel_shards if aligned else plain_shards
    return chosen(n_row, n_col, activations, cotangent, weight, momentum, right_factor)


def solution(mesh):
    placed = (P("row", "col"), P("col", "row"), P("row", "col"), P("row", "col"), P("col", None))
    return jax.shard_map(
        functools.partial(shards, mesh.shape["row"], mesh.shape["col"]),
        mesh=mesh,
        in_specs=placed,
        out_specs=(P("row", "col"), P("row", "col"), P("col", None), P("row", "col")),
        check_vma=False,
    )
```

```python
import functools

import jax
import jax.numpy as jnp
from jax import lax
from jax.experimental import pallas as pl
from jax.experimental.pallas import tpu as pltpu
from jax.sharding import PartitionSpec as P

momentum_decay = 0.6
ridge_weight = 0.001

HIGHEST = lax.Precision.HIGHEST
HIGH = lax.Precision.HIGH
SUBLANES = 8
LANES = 128
MESH = pl.DeviceIdType.MESH


def contract(left_side, right_side, left_dim, right_dim, precision=None):
    return lax.dot_general(
        left_side,
        right_side,
        (((left_dim,), (right_dim,)), ((), ())),
        precision=precision,
        preferred_element_type=jnp.float32,
    )


def identity(size):
    shape = (size, size)
    same = lax.broadcasted_iota(jnp.int32, shape, 0) == lax.broadcasted_iota(jnp.int32, shape, 1)
    return jnp.where(same, 1.0, 0.0).astype(jnp.float32)


def two_stages(size):
    inner = max(k for k in range(1, size + 1) if size % k == 0 and k * k <= size)
    return inner, size // inner


def split(value):
    high = value.astype(jnp.bfloat16)
    return high, (value - high.astype(jnp.float32)).astype(jnp.bfloat16)


def contract_split(left_pair, right_pair, left_dim, right_dim):
    total = contract(left_pair[0], right_pair[0], left_dim, right_dim)
    total = total + contract(left_pair[1], right_pair[0], left_dim, right_dim)
    return total + contract(left_pair[0], right_pair[1], left_dim, right_dim)


def inverse_factor_body(block, ridge, gram_ref, inverse_ref, work, corner):
    size = gram_ref.shape[0]
    work[:, :size] = gram_ref[...] + ridge * identity(size)
    work[:, size:] = identity(size)
    row_in_group = lax.broadcasted_iota(jnp.int32, (SUBLANES, 2 * block), 0)
    for low in range(0, size, block):
        high = low + block
        corner[:, :block] = work[low:high, low:high]
        corner[:, block:] = identity(block)
        groups = [corner[g : g + SUBLANES, :] for g in range(0, block, SUBLANES)]
        for k in range(block):
            own, inside = divmod(k, SUBLANES)
            pivot_row = groups[own][inside : inside + 1, :]
            scaled = pivot_row / pivot_row[:, k : k + 1]
            for g in range(own, len(groups)):
                factor = groups[g][:, k : k + 1]
                change = factor * scaled
                if g == own:
                    change = jnp.where(row_in_group > inside, change, 0.0)
                groups[g] = groups[g] - change
        for g, rows in enumerate(groups):
            corner[g * SUBLANES : (g + 1) * SUBLANES, :] = rows
        pivots = jnp.sum(corner[:, :block] * identity(block), axis=1, keepdims=True)
        corner_inverse = corner[:, block:] * (1.0 / jnp.sqrt(pivots))
        panel = contract(corner_inverse, work[low:high, :], 1, 0, HIGHEST)
        inverse_ref[low:high, :] = panel[:, size:]
        if high < size:
            update = contract(panel[:, :size], panel, 0, 0, HIGHEST)
            work[high:, :] = work[high:, :] - update[high:, :]


def eliminate_four(groups, k, row_in_group, lanes):
    own, inside = divmod(k, SUBLANES)
    rows = [groups[own][inside + j : inside + j + 1, :] for j in range(4)]
    def splat(value, j, sublanes):
        return jnp.broadcast_to(value[:, k + j : k + j + 1], (sublanes, lanes))
    a = [[splat(rows[i], j, 1) for j in range(i + 1)] for i in range(4)]
    i0 = 1.0 / a[0][0]
    i1 = a[0][0] * (1.0 / (a[0][0] * a[1][1] - a[1][0] * a[1][0]))
    l10, l20, l30 = a[1][0] * i0, a[2][0] * i0, a[3][0] * i0
    b21, b31 = a[2][1] - l20 * a[1][0], a[3][1] - l30 * a[1][0]
    l21, l31 = b21 * i1, b31 * i1
    d2 = a[2][2] - l20 * a[2][0] - l21 * b21
    b32 = a[3][2] - l30 * a[2][0] - l31 * b21
    s33 = a[3][3] - l30 * a[3][0] - l31 * b31
    i2 = 1.0 / d2
    i3 = d2 * (1.0 / (d2 * s33 - b32 * b32))
    l32 = b32 * i2
    u0 = rows[0]
    u1 = rows[1] - l10 * u0
    u2 = rows[2] - l20 * u0 - l21 * u1
    u3 = rows[3] - l30 * u0 - l31 * u1 - l32 * u2
    w = [u0 * i0, u1 * i1, u2 * i2, u3 * i3]
    for g in range(own, len(groups)):
        if g == own and inside + 4 == SUBLANES:
            change = None
        else:
            c = [splat(groups[g], j, SUBLANES) for j in range(4)]
            f1 = c[1] - c[0] * l10
            f2 = c[2] - c[0] * l20 - f1 * l21
            f3 = c[3] - c[0] * l30 - f1 * l31 - f2 * l32
            change = (c[0] * w[0] + f1 * w[1]) + (f2 * w[2] + f3 * w[3])
        if g == own:
            value = groups[g]
            if change is not None:
                value = jnp.where(row_in_group > inside + 3, value - change, value)
            for j, u in ((1, u1), (2, u2), (3, u3)):
                value = jnp.where(row_in_group == inside + j, u, value)
            groups[g] = value
        else:
            groups[g] = groups[g] - change


def inverse_by_fours(block, ridge, gram_ref, inverse_ref, work, corner):
    size = gram_ref.shape[0]
    work[:, :size] = gram_ref[...] + ridge * identity(size)
    work[:, size:] = identity(size)
    row_in_group = lax.broadcasted_iota(jnp.int32, (SUBLANES, 2 * block), 0)
    for low in range(0, size, block):
        high = low + block
        corner[:, :block] = work[low:high, low:high]
        corner[:, block:] = identity(block)
        groups = [corner[g : g + SUBLANES, :] for g in range(0, block, SUBLANES)]
        for k in range(0, block, 4):
            eliminate_four(groups, k, row_in_group, 2 * block)
        for g, rows in enumerate(groups):
            corner[g * SUBLANES : (g + 1) * SUBLANES, :] = rows
        pivots = jnp.sum(corner[:, :block] * identity(block), axis=1, keepdims=True)
        corner_inverse = corner[:, block:] * (1.0 / jnp.sqrt(pivots))
        panel = contract(corner_inverse, work[low:high, :], 1, 0, HIGHEST)
        inverse_ref[low:high, :] = panel[:, size:]
        if high < size:
            update = contract(panel[:, :size], panel, 0, 0, HIGHEST)
            work[high:, :] = work[high:, :] - update[high:, :]


def inverse_factor(gram_matrix, ridge):
    size = gram_matrix.shape[0]
    block = min(64, size)
    return pl.pallas_call(
        functools.partial(inverse_factor_body, block, ridge),
        out_shape=jax.ShapeDtypeStruct((size, size), jnp.float32),
        in_specs=[pl.BlockSpec(memory_space=pltpu.VMEM)],
        out_specs=pl.BlockSpec(memory_space=pltpu.VMEM),
        scratch_shapes=[
            pltpu.VMEM((size, 2 * size), jnp.float32),
            pltpu.VMEM((block, 2 * block), jnp.float32),
        ],
        cost_estimate=pl.CostEstimate(flops=20_000_000_000, bytes_accessed=8 * size * size, transcendentals=0),
        name="inverse_factor",
    )(gram_matrix)


def plain_shards(rows_of, cols_of, activations, cotangent, weight, momentum, right_factor):
    dout = momentum.shape[0] * rows_of
    din = momentum.shape[1] * cols_of
    rank = right_factor.shape[1]
    cot_tokens = lax.all_gather(cotangent, "col", axis=0, tiled=True)
    act_tokens = lax.all_gather(activations, "row", axis=0, tiled=True)
    held_part = contract(momentum, right_factor, 1, 0, HIGH)
    act_part = contract(act_tokens.astype(jnp.float32), right_factor, 1, 0, HIGH)
    grad_part = contract(cot_tokens.astype(jnp.float32), act_part, 0, 0, HIGH)
    left_part = (held_part + grad_part) / jnp.sqrt(jnp.float32(din))
    left_piece = lax.psum_scatter(left_part, "col", scatter_dimension=0, tiled=True)
    input_part = jnp.dot(cot_tokens, weight, preferred_element_type=jnp.float32)
    buffer = momentum + contract(cot_tokens, act_tokens, 0, 0, None)
    left_block = lax.all_gather(left_piece, "col", axis=0, tiled=True)
    gram_matrix = lax.psum(contract(left_block, left_block, 0, 0, HIGHEST), "row")
    projected_part = contract(buffer, left_block, 0, 0, HIGH)
    gram_matrix, projected_part = lax.optimization_barrier((gram_matrix, projected_part))
    projected = lax.psum(projected_part, "row")
    projected, input_part = lax.optimization_barrier((projected, input_part))
    input_sums = lax.psum_scatter(input_part, "row", scatter_dimension=0, tiled=True)
    inverse = inverse_factor(gram_matrix, ridge_weight * dout)
    orthonormal = contract(left_block, inverse, 1, 1, HIGHEST)
    right = contract(projected, inverse, 1, 1, HIGHEST)
    squares = lax.psum(jnp.sum(right * right, axis=0), "col")
    momentum_next = buffer - (1.0 - momentum_decay) * contract(orthonormal, right, 1, 1, HIGH)
    right_next = right * lax.rsqrt(squares / din + 1e-06)
    step_scale = jnp.sqrt(jnp.float32(dout) / rank)
    weight_step = (step_scale * contract(orthonormal, right_next, 1, 1, HIGH)).astype(jnp.bfloat16)
    return (input_sums.astype(jnp.bfloat16), momentum_next, right_next, weight_step)


def remote(source, target, send_sem, recv_sem, device):
    return pltpu.make_async_remote_copy(
        src_ref=source,
        dst_ref=target,
        send_sem=send_sem,
        recv_sem=recv_sem,
        device_id=device,
        device_id_type=MESH,
    )


def greet(devices):
    barrier = pltpu.get_barrier_semaphore()
    for device in devices:
        pl.semaphore_signal(barrier, inc=1, device_id=device, device_id_type=MESH)
    pl.semaphore_wait(barrier, len(devices))


def factor_kernel(
    n_row,
    n_col,
    ridge,
    act_ref,
    cot_ref,
    weight_hbm,
    momentum_hbm,
    factor_ref,
    input_ref,
    buffer_hbm,
    orthonormal_hbm,
    right_hbm,
    scale_ref,
    act_all,
    cot_all,
    cot_flat,
    cot_turned,
    chunks,
    chunk_high,
    chunk_low,
    weight,
    factor_high,
    factor_low,
    token_high,
    token_low,
    send_inner,
    recv_inner,
    totals,
    recv_outer,
    left_ref,
    gram_ref,
    projected_ref,
    input_send,
    input_recv,
    gram_in,
    gram_out,
    gram_all,
    proj_in,
    proj_out,
    proj_all,
    inverse,
    work,
    corner,
    squares_all,
    orthonormal,
    right_ref,
    load_sem,
    store_sem,
    weight_sem,
    act_sem,
    cot_sem,
    inner_sem,
    chain_sem,
    chain_in_sem,
    gather_send_sem,
    gather_outer_sem,
    gather_inner_sem,
    input_sem,
    gram_in_sem,
    gram_out_sem,
    gram_all_sem,
    proj_in_sem,
    proj_out_sem,
    proj_all_sem,
    squares_sem,
    result_sem,
):
    inner, outer = two_stages(n_col)
    row, col = lax.axis_index("row"), lax.axis_index("col")
    me_in, me_out = lax.rem(col, inner), lax.div(col, inner)
    piece, cols = chunks.shape[1], chunks.shape[2]
    din = cols * n_col
    act_rows = act_ref.shape[0]
    tokens = act_rows * n_row

    flip = lax.div(2 * me_out, outer)
    near = me_out + flip * (outer - 1 - 2 * me_out)

    def turned_back(position):
        return position + flip * (outer - 1 - 2 * position)

    def target(k):
        last = k // (outer - 1)
        return turned_back(outer - 1 - k - (k + near + 1) // outer + last * (near + 1))

    def chunk_at(j):
        return target(j % outer) * inner + (me_in + 1 + j // outer) % inner

    def load(q):
        return pltpu.make_async_copy(
            momentum_hbm.at[pl.ds(pl.multiple_of(q * piece, SUBLANES), piece), :], chunks.at[q], load_sem.at[q]
        )

    def store(q):
        return pltpu.make_async_copy(
            chunks.at[q], buffer_hbm.at[pl.ds(pl.multiple_of(q * piece, SUBLANES), piece), :], store_sem.at[q]
        )

    for j in range(n_col):
        load(chunk_at(j)).start()
    weight_copy = pltpu.make_async_copy(weight_hbm, weight, weight_sem)
    weight_copy.start()

    row_peers = [lax.rem(row + d, n_row) for d in range(1, n_row)]
    col_peers = [lax.rem(col + d, n_col) for d in range(1, n_col)]
    greet([(peer, col) for peer in row_peers] + [(row, peer) for peer in col_peers])

    cot_copies = [
        remote(cot_ref, cot_all.at[col], cot_sem.at[0, d], cot_sem.at[1, d], (row, peer))
        for d, peer in enumerate(col_peers)
    ]
    act_copies = [
        remote(act_ref, act_all.at[row], act_sem.at[0, d], act_sem.at[1, d], (peer, col))
        for d, peer in enumerate(row_peers)
    ]
    for copy in cot_copies + act_copies:
        copy.start()
    act_all[row] = act_ref[...]
    cot_all[col] = cot_ref[...]
    factor_high[...], factor_low[...] = split(factor_ref[...])

    def held_part(j):
        q = chunk_at(j)
        load(q).wait()
        return contract_split(split(chunks[q]), (factor_high[...], factor_low[...]), 1, 0)

    def turned_rows(q):
        return cot_turned[pl.ds(pl.multiple_of(q * piece, 2 * SUBLANES), piece), :]

    def token_part(j):
        rows = turned_rows(chunk_at(j))
        return contract(rows, token_high[...], 1, 0) + contract(rows, token_low[...], 1, 0)

    for d in range(inner - 1):

        def begin(k, carry, d=d):
            send_inner[d, k] = held_part(d * outer + k)
            return carry

        lax.fori_loop(0, outer, begin, 0)

    for copy in act_copies:
        copy.wait()
    acts = act_all[...].reshape(tokens, cols)
    token_sums = contract(acts, factor_high[...], 1, 0) + contract(acts, factor_low[...], 1, 0)
    token_high[...], token_low[...] = split(token_sums)
    for copy in cot_copies:
        copy.wait()

    def turn(b, carry):
        lanes = pl.ds(pl.multiple_of(b * LANES, LANES), LANES)
        slab = cot_all[:, :, lanes].astype(jnp.float32).reshape(tokens, LANES)
        cot_flat[:, lanes] = slab.astype(jnp.bfloat16)
        cot_turned[lanes, :] = slab.T.astype(jnp.bfloat16)
        return carry

    lax.fori_loop(0, cot_ref.shape[1] // LANES, turn, 0)

    def form(q):
        value = chunks[q] + contract(turned_rows(q), act_all[...].reshape(tokens, cols), 1, 0)
        chunks[q] = value
        chunk_high[q], chunk_low[q] = split(value)
        store(q).start()

    def inner_copy(d, k):
        peer = me_out * inner + lax.rem(me_in + 1 + d, inner)
        return remote(
            send_inner.at[d, k], recv_inner.at[d, k], inner_sem.at[0, d, k], inner_sem.at[1, d, k], (row, peer)
        )

    def toward(q):
        return 2 * ((q - me_out + outer - 1) // outer) - 1

    def chain_copy(k):
        q = target(k)
        up = (q - me_out + outer - 1) // outer
        ending = (outer - (me_out - q)) // (outer - 1) * (1 - up)
        slot = q + ending * (outer - q)
        peer = (me_out + toward(q)) * inner + me_in
        return remote(totals.at[k], recv_outer.at[slot], chain_sem.at[k], chain_in_sem.at[slot], (row, peer))

    def chain_arrival(slot):
        return remote(totals.at[0], recv_outer.at[slot], chain_sem.at[0], chain_in_sem.at[slot], (row, col))

    for d in range(inner - 1):

        def push(k, carry, d=d):
            send_inner[d, k] = send_inner[d, k] + token_part(d * outer + k)
            inner_copy(d, k).start()
            return carry

        lax.fori_loop(0, outer, push, 0)

    weight_copy.wait()
    input_part = contract(cot_flat[...], weight[...], 1, 0)
    input_send[...] = input_part.reshape(n_row, act_rows, cols)
    input_copies = [
        remote(input_send.at[peer], input_recv.at[d], input_sem.at[0, d], input_sem.at[1, d], (peer, col))
        for d, peer in enumerate(row_peers)
    ]
    for copy in input_copies:
        copy.start()

    def own_part(k):
        j = (inner - 1) * outer + k
        value = held_part(j) + token_part(j)
        for d in range(inner):
            form(chunk_at(d * outer + k))
        return value

    def chain(k, carry):
        total = own_part(k)
        for d in range(inner - 1):
            inner_copy(d, k).wait_recv()
            total = total + recv_inner[d, k]
        totals[k] = total
        q = target(k)

        @pl.when(jnp.logical_and(me_out - toward(q) >= 0, me_out - toward(q) < outer))
        def _():
            chain_arrival(q).wait_recv()
            totals[k] = totals[k] + recv_outer[q]

        chain_copy(k).start()
        return carry

    lax.fori_loop(0, outer - 1, chain, 0)
    mine = own_part(outer - 1)
    for d in range(inner - 1):
        inner_copy(d, outer - 1).wait_recv()
        mine = mine + recv_inner[d, outer - 1]
    totals[outer - 1] = mine

    @pl.when(me_out > 0)
    def _():
        chain_arrival(me_out).wait_recv()
        totals[outer - 1] = totals[outer - 1] + recv_outer[me_out]

    @pl.when(me_out < outer - 1)
    def _():
        chain_arrival(outer).wait_recv()
        totals[outer - 1] = totals[outer - 1] + recv_outer[outer]

    left_ref[col] = totals[outer - 1] / jnp.sqrt(jnp.float32(din))

    def gather_outer(q, up):
        piece_ref = left_ref.at[q * inner + me_in]
        peer = (me_out + 2 * up - 1) * inner + me_in
        return remote(piece_ref, piece_ref, gather_send_sem.at[up, q], gather_outer_sem.at[q], (row, peer))

    def gather_inner(d, q):
        piece_ref = left_ref.at[q * inner + me_in]
        peer = me_out * inner + (me_in + 1 + d) % inner
        return remote(
            piece_ref, piece_ref, gather_inner_sem.at[0, d, q], gather_inner_sem.at[1, d, q], (row, peer)
        )

    def onward(q, start):
        up = 1 - (q - me_out + outer - 1) // outer

        @pl.when(jnp.logical_and(me_out + 2 * up - 1 >= 0, me_out + 2 * up - 1 < outer))
        def _():
            copy = gather_outer(q, up)
            copy.start() if start else copy.wait_send()

    def own_outward(start):
        for up in range(2):

            @pl.when(jnp.logical_and(me_out + 2 * up - 1 >= 0, me_out + 2 * up - 1 < outer))
            def _():
                copy = gather_outer(me_out, up)
                copy.start() if start else copy.wait_send()

    own_outward(True)
    for d in range(inner - 1):
        gather_inner(d, me_out).start()

    def arrival(n):
        paired = (2 * near - n - 1 + 2 * outer) // (2 * outer)
        step = (n // 2 + 1) * (2 * (n % 2) - 1)
        return turned_back(paired * (near + step) + (1 - paired) * (n + 1))

    def absorb(q):
        value = left_ref[q]
        pair = split(value)
        gram_ref[...] = gram_ref[...] + contract(value, value, 0, 0, HIGHEST)
        projected_ref[...] = projected_ref[...] + contract_split(pair, (chunk_high[q], chunk_low[q]), 0, 0)

    def absorb_inner(d, q):
        gather_inner(d, q).wait_recv()
        absorb(q * inner + (me_in - 1 - d + inner) % inner)

    gram_ref[...] = jnp.zeros_like(gram_ref)
    projected_ref[...] = jnp.zeros_like(projected_ref)
    absorb(col)

    def gather(n, before):
        q = arrival(n)
        gather_outer(q, 0).wait_recv()
        onward(q, True)
        for d in range(inner - 1):
            gather_inner(d, q).start()
        absorb(q * inner + me_in)
        for d in range(inner - 1):
            absorb_inner(d, before)
        return q

    final = lax.fori_loop(0, outer - 1, gather, me_out)
    for d in range(inner - 1):
        absorb_inner(d, final)

    def finish():
        total = input_send[row]
        for d, copy in enumerate(input_copies):
            copy.wait()
            total = total + input_recv[d]
        input_ref[...] = total.astype(jnp.bfloat16)
        for q in range(n_col):
            store(q).wait()

        def drain(k, carry):
            for d in range(inner - 1):
                inner_copy(d, k).wait_send()
                gather_inner(d, k).wait_send()
            return carry

        lax.fori_loop(0, outer, drain, 0)

        def drain_chain(k, carry):
            chain_copy(k).wait_send()
            onward(arrival(k), False)
            return carry

        lax.fori_loop(0, outer - 1, drain_chain, 0)
        own_outward(False)


    rank = gram_ref.shape[0]
    row_inner, row_outer = two_stages(n_row)
    row_me_in, row_me_out = lax.rem(row, row_inner), lax.div(row, row_inner)
    part = rank // row_inner
    inner_peers = [(lax.rem(row_me_in + 1 + d, row_inner)) for d in range(row_inner - 1)]
    outer_peers = [(lax.rem(row_me_out + 1 + d, row_outer)) for d in range(row_outer - 1)]
    def at(index):
        return pl.ds(pl.multiple_of(index * part, SUBLANES), part)

    def reduce_in(source, buffer, sem):
        copies = [
            remote(source.at[at(peer), :], buffer.at[d], sem.at[0, d], sem.at[1, d], (row_me_out * row_inner + peer, col))
            for d, peer in enumerate(inner_peers)
        ]
        for copy in copies:
            copy.start()
        return copies

    def exchange_out(source, copies_in, buffer_in, buffer_out, sem):
        total = source[at(row_me_in), :]
        for d, copy in enumerate(copies_in):
            copy.wait()
            total = total + buffer_in[d]
        buffer_out[row_me_out] = total
        copies = [
            remote(
                buffer_out.at[row_me_out], buffer_out.at[row_me_out], sem.at[0, d], sem.at[1, d], (peer * row_inner + row_me_in, col)
            )
            for d, peer in enumerate(outer_peers)
        ]
        for copy in copies:
            copy.start()
        return copies

    def gather_in(copies_out, buffer_out, whole, sem):
        for copy in copies_out:
            copy.wait()
        total = buffer_out[0]
        for o in range(1, row_outer):
            total = total + buffer_out[o]
        whole[at(row_me_in), :] = total
        copies = [
            remote(
                whole.at[at(row_me_in), :], whole.at[at(row_me_in), :], sem.at[0, d], sem.at[1, d], (row_me_out * row_inner + peer, col)
            )
            for d, peer in enumerate(inner_peers)
        ]
        for copy in copies:
            copy.start()
        return copies

    gram_copies = reduce_in(gram_ref, gram_in, gram_in_sem)
    proj_copies = reduce_in(projected_ref, proj_in, proj_in_sem)
    gram_copies = exchange_out(gram_ref, gram_copies, gram_in, gram_out, gram_out_sem)
    proj_copies = exchange_out(projected_ref, proj_copies, proj_in, proj_out, proj_out_sem)
    finish()
    gram_copies = gather_in(gram_copies, gram_out, gram_all, gram_all_sem)
    for copy in gram_copies:
        copy.wait()
    inverse_by_fours(corner.shape[0], ridge, gram_all, inverse, work, corner)
    proj_copies = gather_in(proj_copies, proj_out, proj_all, proj_all_sem)
    factor = split(inverse[...])
    for copy in proj_copies:
        copy.wait()
    right = contract_split(factor, split(proj_all[...]), 1, 0)
    right_ref[...] = right
    squares = jnp.sum(right * right, axis=1, keepdims=True)
    squares = jnp.broadcast_to(squares, (rank, LANES)).T[:SUBLANES, :]
    squares_all[col] = squares
    copies = [
        remote(squares_all.at[col], squares_all.at[col], squares_sem.at[0, d], squares_sem.at[1, d], (row, peer))
        for d, peer in enumerate(col_peers)
    ]
    for copy in copies:
        copy.start()
    right_copy = pltpu.make_async_copy(right_ref, right_hbm, result_sem.at[n_col])
    right_copy.start()

    def result(q):
        return pltpu.make_async_copy(orthonormal.at[q], orthonormal_hbm.at[q], result_sem.at[q])

    def orthonormalise(q, carry):
        orthonormal[q] = contract_split(split(left_ref[q]), factor, 1, 1)
        result(q).start()
        return carry

    lax.fori_loop(0, n_col, orthonormalise, 0)
    for copy in copies:
        copy.wait()
    total = squares_all[0]
    for q in range(1, n_col):
        total = total + squares_all[q]
    scale_ref[...] = lax.rsqrt(total / din + 1e-06)
    right_copy.wait()
    for q in range(n_col):
        result(q).wait()


def factor_call(n_row, n_col, ridge, activations, cotangent, weight, momentum, right_factor):
    inner, outer = two_stages(n_col)
    row_inner, row_outer = two_stages(n_row)
    rows, cols = momentum.shape
    rank = right_factor.shape[1]
    piece = rows // n_col
    part = rank // row_inner
    block = min(64, rank)
    act_rows, cot_rows = activations.shape[0], cotangent.shape[0]
    tokens = act_rows * n_row
    f32, bf16 = jnp.float32, jnp.bfloat16
    vmem = pl.BlockSpec(memory_space=pltpu.VMEM)
    hbm = pl.BlockSpec(memory_space=pl.ANY)
    dma = pltpu.SemaphoreType.DMA
    return pl.pallas_call(
        functools.partial(factor_kernel, n_row, n_col, ridge),
        out_shape=(
            jax.ShapeDtypeStruct((act_rows, cols), bf16),
            jax.ShapeDtypeStruct((rows, cols), f32),
            jax.ShapeDtypeStruct((n_col, piece, rank), f32),
            jax.ShapeDtypeStruct((rank, cols), f32),
            jax.ShapeDtypeStruct((SUBLANES, rank), f32),
        ),
        in_specs=[vmem, vmem, hbm, hbm, vmem],
        out_specs=(vmem, hbm, hbm, hbm, vmem),
        scratch_shapes=[
            pltpu.VMEM((n_row, act_rows, cols), bf16),
            pltpu.VMEM((n_col, cot_rows, rows), bf16),
            pltpu.VMEM((tokens, rows), bf16),
            pltpu.VMEM((rows, tokens), bf16),
            pltpu.VMEM((n_col, piece, cols), f32),
            pltpu.VMEM((n_col, piece, cols), bf16),
            pltpu.VMEM((n_col, piece, cols), bf16),
            pltpu.VMEM((rows, cols), bf16),
            pltpu.VMEM((cols, rank), bf16),
            pltpu.VMEM((cols, rank), bf16),
            pltpu.VMEM((tokens, rank), bf16),
            pltpu.VMEM((tokens, rank), bf16),
            pltpu.VMEM((inner - 1, outer, piece, rank), f32),
            pltpu.VMEM((inner - 1, outer, piece, rank), f32),
            pltpu.VMEM((outer, piece, rank), f32),
            pltpu.VMEM((outer + 1, piece, rank), f32),
            pltpu.VMEM((n_col, piece, rank), f32),
            pltpu.VMEM((rank, rank), f32),
            pltpu.VMEM((rank, cols), f32),
            pltpu.VMEM((n_row, act_rows, cols), f32),
            pltpu.VMEM((n_row - 1, act_rows, cols), f32),
            pltpu.VMEM((row_inner - 1, part, rank), f32),
            pltpu.VMEM((row_outer, part, rank), f32),
            pltpu.VMEM((rank, rank), f32),
            pltpu.VMEM((row_inner - 1, part, cols), f32),
            pltpu.VMEM((row_outer, part, cols), f32),
            pltpu.VMEM((rank, cols), f32),
            pltpu.VMEM((rank, rank), f32),
            pltpu.VMEM((rank, 2 * rank), f32),
            pltpu.VMEM((block, 2 * block), f32),
            pltpu.VMEM((n_col, SUBLANES, rank), f32),
            pltpu.VMEM((n_col, piece, rank), f32),
            pltpu.VMEM((rank, cols), f32),
            dma((n_col,)),
            dma((n_col,)),
            dma,
            dma((2, n_row - 1)),
            dma((2, n_col - 1)),
            dma((2, inner - 1, outer)),
            dma((outer,)),
            dma((outer + 1,)),
            dma((2, outer)),
            dma((outer,)),
            dma((2, inner - 1, outer)),
            dma((2, n_row - 1)),
            dma((2, row_inner - 1)),
            dma((2, row_outer - 1)),
            dma((2, row_inner - 1)),
            dma((2, row_inner - 1)),
            dma((2, row_outer - 1)),
            dma((2, row_inner - 1)),
            dma((2, n_col - 1)),
            dma((n_col + 1,)),
        ],
        compiler_params=pltpu.CompilerParams(
            collective_id=1, has_side_effects=True, vmem_limit_bytes=60 * 1024 * 1024
        ),
        name="factors",
    )(activations, cotangent, weight, momentum, right_factor)


def output_kernel(
    step_scale,
    buffer_ref,
    orthonormal_ref,
    right_ref,
    scale_ref,
    momentum_ref,
    step_ref,
    next_ref,
    right_high,
    right_low,
):
    @pl.when(pl.program_id(0) == 0)
    def _():
        right_high[...], right_low[...] = split(right_ref[...])
        next_ref[...] = right_ref[...].T * scale_ref[:1, :]

    right = (right_high[...], right_low[...])
    orthonormal = orthonormal_ref[...]
    momentum_ref[...] = buffer_ref[...] - (1.0 - momentum_decay) * contract_split(split(orthonormal), right, 1, 0)
    scaled = orthonormal * scale_ref[:1, :]
    step_ref[...] = (step_scale * contract_split(split(scaled), right, 1, 0)).astype(jnp.bfloat16)


def output_call(step_scale, buffer, orthonormal, right, scale):
    rows, cols = buffer.shape
    rank = right.shape[0]
    tile = max(t for t in range(16, 289, 16) if rows % t == 0)
    f32 = jnp.float32
    return pl.pallas_call(
        functools.partial(output_kernel, step_scale),
        grid=(rows // tile,),
        out_shape=(
            jax.ShapeDtypeStruct((rows, cols), f32),
            jax.ShapeDtypeStruct((rows, cols), jnp.bfloat16),
            jax.ShapeDtypeStruct((cols, rank), f32),
        ),
        in_specs=[
            pl.BlockSpec((tile, cols), lambda i: (i, 0)),
            pl.BlockSpec((tile, rank), lambda i: (i, 0)),
            pl.BlockSpec((rank, cols), lambda i: (0, 0)),
            pl.BlockSpec(scale.shape, lambda i: (0, 0)),
        ],
        out_specs=(
            pl.BlockSpec((tile, cols), lambda i: (i, 0)),
            pl.BlockSpec((tile, cols), lambda i: (i, 0)),
            pl.BlockSpec((cols, rank), lambda i: (0, 0)),
        ),
        scratch_shapes=[pltpu.VMEM((rank, cols), jnp.bfloat16), pltpu.VMEM((rank, cols), jnp.bfloat16)],
        compiler_params=pltpu.CompilerParams(
            dimension_semantics=("arbitrary",), vmem_limit_bytes=60 * 1024 * 1024
        ),
        name="outputs",
    )(buffer, orthonormal, right, scale)


def kernel_shards(n_row, n_col, activations, cotangent, weight, momentum, right_factor):
    rows, cols = momentum.shape
    rank = right_factor.shape[1]
    dout = rows * n_row
    input_grad, buffer, orthonormal, right, scale = factor_call(
        n_row, n_col, ridge_weight * dout, activations, cotangent, weight, momentum, right_factor
    )
    step_scale = (dout / rank) ** 0.5
    momentum_next, weight_step, right_next = output_call(
        step_scale, buffer, orthonormal.reshape(rows, rank), right, scale
    )
    return input_grad, momentum_next, right_next, weight_step


def shards(n_row, n_col, activations, cotangent, weight, momentum, right_factor):
    rows, cols = momentum.shape
    rank = right_factor.shape[1]
    aligned = (
        rows % (n_col * 2 * SUBLANES) == 0
        and rows % LANES == 0
        and cols % LANES == 0
        and rank % LANES == 0
        and activations.shape[0] % (2 * SUBLANES) == 0
        and cotangent.shape[0] % SUBLANES == 0
        and two_stages(n_row)[0] > 1
        and two_stages(n_col)[0] > 1
        and rank % (two_stages(n_row)[0] * SUBLANES) == 0
    )
    chosen = kernel_shards if aligned else plain_shards
    return chosen(n_row, n_col, activations, cotangent, weight, momentum, right_factor)


def solution(mesh):
    placed = (P("row", "col"), P("col", "row"), P("row", "col"), P("row", "col"), P("col", None))
    return jax.shard_map(
        functools.partial(shards, mesh.shape["row"], mesh.shape["col"]),
        mesh=mesh,
        in_specs=placed,
        out_specs=(P("row", "col"), P("row", "col"), P("col", None), P("row", "col")),
        check_vma=False,
    )
```

```python
import functools

import jax
import jax.numpy as jnp
from jax import lax
from jax.experimental import pallas as pl
from jax.experimental.pallas import tpu as pltpu
from jax.sharding import PartitionSpec as P

momentum_decay = 0.6
ridge_weight = 0.001

HIGHEST = lax.Precision.HIGHEST
HIGH = lax.Precision.HIGH
SUBLANES = 8
LANES = 128
MESH = pl.DeviceIdType.MESH


def contract(left_side, right_side, left_dim, right_dim, precision=None):
    return lax.dot_general(
        left_side,
        right_side,
        (((left_dim,), (right_dim,)), ((), ())),
        precision=precision,
        preferred_element_type=jnp.float32,
    )


def identity(size):
    shape = (size, size)
    same = lax.broadcasted_iota(jnp.int32, shape, 0) == lax.broadcasted_iota(jnp.int32, shape, 1)
    return jnp.where(same, 1.0, 0.0).astype(jnp.float32)


def two_stages(size):
    inner = max(k for k in range(1, size + 1) if size % k == 0 and k * k <= size)
    return inner, size // inner


def split(value):
    high = value.astype(jnp.bfloat16)
    return high, (value - high.astype(jnp.float32)).astype(jnp.bfloat16)


def contract_split(left_pair, right_pair, left_dim, right_dim):
    total = contract(left_pair[0], right_pair[0], left_dim, right_dim)
    total = total + contract(left_pair[1], right_pair[0], left_dim, right_dim)
    return total + contract(left_pair[0], right_pair[1], left_dim, right_dim)


def inverse_factor_body(block, ridge, gram_ref, inverse_ref, work, corner):
    size = gram_ref.shape[0]
    work[:, :size] = gram_ref[...] + ridge * identity(size)
    work[:, size:] = identity(size)
    row_in_group = lax.broadcasted_iota(jnp.int32, (SUBLANES, 2 * block), 0)
    for low in range(0, size, block):
        high = low + block
        corner[:, :block] = work[low:high, low:high]
        corner[:, block:] = identity(block)
        groups = [corner[g : g + SUBLANES, :] for g in range(0, block, SUBLANES)]
        for k in range(block):
            own, inside = divmod(k, SUBLANES)
            pivot_row = groups[own][inside : inside + 1, :]
            scaled = pivot_row / pivot_row[:, k : k + 1]
            for g in range(own, len(groups)):
                factor = groups[g][:, k : k + 1]
                change = factor * scaled
                if g == own:
                    change = jnp.where(row_in_group > inside, change, 0.0)
                groups[g] = groups[g] - change
        for g, rows in enumerate(groups):
            corner[g * SUBLANES : (g + 1) * SUBLANES, :] = rows
        pivots = jnp.sum(corner[:, :block] * identity(block), axis=1, keepdims=True)
        corner_inverse = corner[:, block:] * (1.0 / jnp.sqrt(pivots))
        panel = contract(corner_inverse, work[low:high, :], 1, 0, HIGHEST)
        inverse_ref[low:high, :] = panel[:, size:]
        if high < size:
            update = contract(panel[:, :size], panel, 0, 0, HIGHEST)
            work[high:, :] = work[high:, :] - update[high:, :]


def eliminate_four(groups, k, row_in_group, lanes):
    own, inside = divmod(k, SUBLANES)
    rows = [groups[own][inside + j : inside + j + 1, :] for j in range(4)]
    def splat(value, j, sublanes):
        return jnp.broadcast_to(value[:, k + j : k + j + 1], (sublanes, lanes))
    a = [[splat(rows[i], j, 1) for j in range(i + 1)] for i in range(4)]
    i0 = 1.0 / a[0][0]
    i1 = a[0][0] * (1.0 / (a[0][0] * a[1][1] - a[1][0] * a[1][0]))
    l10, l20, l30 = a[1][0] * i0, a[2][0] * i0, a[3][0] * i0
    b21, b31 = a[2][1] - l20 * a[1][0], a[3][1] - l30 * a[1][0]
    l21, l31 = b21 * i1, b31 * i1
    d2 = a[2][2] - l20 * a[2][0] - l21 * b21
    b32 = a[3][2] - l30 * a[2][0] - l31 * b21
    s33 = a[3][3] - l30 * a[3][0] - l31 * b31
    i2 = 1.0 / d2
    i3 = d2 * (1.0 / (d2 * s33 - b32 * b32))
    l32 = b32 * i2
    u0 = rows[0]
    u1 = rows[1] - l10 * u0
    u2 = rows[2] - l20 * u0 - l21 * u1
    u3 = rows[3] - l30 * u0 - l31 * u1 - l32 * u2
    w = [u0 * i0, u1 * i1, u2 * i2, u3 * i3]
    for g in range(own, len(groups)):
        if g == own and inside + 4 == SUBLANES:
            change = None
        else:
            c = [splat(groups[g], j, SUBLANES) for j in range(4)]
            f1 = c[1] - c[0] * l10
            f2 = c[2] - c[0] * l20 - f1 * l21
            f3 = c[3] - c[0] * l30 - f1 * l31 - f2 * l32
            change = (c[0] * w[0] + f1 * w[1]) + (f2 * w[2] + f3 * w[3])
        if g == own:
            value = groups[g]
            if change is not None:
                value = jnp.where(row_in_group > inside + 3, value - change, value)
            for j, u in ((1, u1), (2, u2), (3, u3)):
                value = jnp.where(row_in_group == inside + j, u, value)
            groups[g] = value
        else:
            groups[g] = groups[g] - change


def invert_block(low, block, work, corner, inverse_ref):
    size = work.shape[0]
    high = low + block
    row_in_group = lax.broadcasted_iota(jnp.int32, (SUBLANES, 2 * block), 0)
    corner[:, :block] = work[low:high, low:high]
    corner[:, block:] = identity(block)
    groups = [corner[g : g + SUBLANES, :] for g in range(0, block, SUBLANES)]
    for k in range(0, block, 4):
        eliminate_four(groups, k, row_in_group, 2 * block)
    for g, rows in enumerate(groups):
        corner[g * SUBLANES : (g + 1) * SUBLANES, :] = rows
    pivots = jnp.sum(corner[:, :block] * identity(block), axis=1, keepdims=True)
    corner_inverse = corner[:, block:] * (1.0 / jnp.sqrt(pivots))
    panel = contract(corner_inverse, work[low:high, :], 1, 0, HIGHEST)
    inverse_ref[low:high, :] = panel[:, size:]
    if high < size:
        update = contract(panel[:, :size], panel, 0, 0, HIGHEST)
        work[high:, :] = work[high:, :] - update[high:, :]


def inverse_factor(gram_matrix, ridge):
    size = gram_matrix.shape[0]
    block = min(64, size)
    return pl.pallas_call(
        functools.partial(inverse_factor_body, block, ridge),
        out_shape=jax.ShapeDtypeStruct((size, size), jnp.float32),
        in_specs=[pl.BlockSpec(memory_space=pltpu.VMEM)],
        out_specs=pl.BlockSpec(memory_space=pltpu.VMEM),
        scratch_shapes=[
            pltpu.VMEM((size, 2 * size), jnp.float32),
            pltpu.VMEM((block, 2 * block), jnp.float32),
        ],
        cost_estimate=pl.CostEstimate(flops=20_000_000_000, bytes_accessed=8 * size * size, transcendentals=0),
        name="inverse_factor",
    )(gram_matrix)


def plain_shards(rows_of, cols_of, activations, cotangent, weight, momentum, right_factor):
    dout = momentum.shape[0] * rows_of
    din = momentum.shape[1] * cols_of
    rank = right_factor.shape[1]
    cot_tokens = lax.all_gather(cotangent, "col", axis=0, tiled=True)
    act_tokens = lax.all_gather(activations, "row", axis=0, tiled=True)
    held_part = contract(momentum, right_factor, 1, 0, HIGH)
    act_part = contract(act_tokens.astype(jnp.float32), right_factor, 1, 0, HIGH)
    grad_part = contract(cot_tokens.astype(jnp.float32), act_part, 0, 0, HIGH)
    left_part = (held_part + grad_part) / jnp.sqrt(jnp.float32(din))
    left_piece = lax.psum_scatter(left_part, "col", scatter_dimension=0, tiled=True)
    input_part = jnp.dot(cot_tokens, weight, preferred_element_type=jnp.float32)
    buffer = momentum + contract(cot_tokens, act_tokens, 0, 0, None)
    left_block = lax.all_gather(left_piece, "col", axis=0, tiled=True)
    gram_matrix = lax.psum(contract(left_block, left_block, 0, 0, HIGHEST), "row")
    projected_part = contract(buffer, left_block, 0, 0, HIGH)
    gram_matrix, projected_part = lax.optimization_barrier((gram_matrix, projected_part))
    projected = lax.psum(projected_part, "row")
    projected, input_part = lax.optimization_barrier((projected, input_part))
    input_sums = lax.psum_scatter(input_part, "row", scatter_dimension=0, tiled=True)
    inverse = inverse_factor(gram_matrix, ridge_weight * dout)
    orthonormal = contract(left_block, inverse, 1, 1, HIGHEST)
    right = contract(projected, inverse, 1, 1, HIGHEST)
    squares = lax.psum(jnp.sum(right * right, axis=0), "col")
    momentum_next = buffer - (1.0 - momentum_decay) * contract(orthonormal, right, 1, 1, HIGH)
    right_next = right * lax.rsqrt(squares / din + 1e-06)
    step_scale = jnp.sqrt(jnp.float32(dout) / rank)
    weight_step = (step_scale * contract(orthonormal, right_next, 1, 1, HIGH)).astype(jnp.bfloat16)
    return (input_sums.astype(jnp.bfloat16), momentum_next, right_next, weight_step)


def remote(source, target, send_sem, recv_sem, device):
    return pltpu.make_async_remote_copy(
        src_ref=source,
        dst_ref=target,
        send_sem=send_sem,
        recv_sem=recv_sem,
        device_id=device,
        device_id_type=MESH,
    )


def greet(devices):
    barrier = pltpu.get_barrier_semaphore()
    for device in devices:
        pl.semaphore_signal(barrier, inc=1, device_id=device, device_id_type=MESH)
    pl.semaphore_wait(barrier, len(devices))


def factor_kernel(
    n_row,
    n_col,
    ridge,
    act_ref,
    cot_ref,
    weight_hbm,
    momentum_hbm,
    factor_ref,
    input_ref,
    buffer_hbm,
    orthonormal_hbm,
    right_high_hbm,
    right_low_hbm,
    right_turned_hbm,
    scale_ref,
    act_all,
    cot_all,
    cot_flat,
    cot_turned,
    chunks,
    chunk_high,
    chunk_low,
    weight,
    factor_high,
    factor_low,
    token_send,
    token_recv,
    token_high,
    token_low,
    send_inner,
    recv_inner,
    totals,
    recv_outer,
    left_ref,
    gram_ref,
    projected_ref,
    input_send,
    input_recv,
    gram_in,
    gram_out,
    gram_all,
    proj_in,
    proj_out,
    proj_all,
    inverse,
    diagonal,
    work,
    corner,
    squares_all,
    orthonormal,
    right_high,
    right_low,
    right_turned,
    load_sem,
    store_sem,
    weight_sem,
    act_sem,
    cot_sem,
    token_sem,
    inner_sem,
    chain_sem,
    chain_in_sem,
    gather_send_sem,
    gather_outer_sem,
    gather_inner_sem,
    input_sem,
    gram_in_sem,
    gram_out_sem,
    gram_all_sem,
    proj_in_sem,
    proj_out_sem,
    proj_all_sem,
    squares_sem,
    result_sem,
):
    inner, outer = two_stages(n_col)
    row_inner, row_outer = two_stages(n_row)
    row, col = lax.axis_index("row"), lax.axis_index("col")
    me_in, me_out = lax.rem(col, inner), lax.div(col, inner)
    row_in, row_out = lax.rem(row, row_inner), lax.div(row, row_inner)
    piece, cols = chunks.shape[1], chunks.shape[2]
    halves, width = left_ref.shape[0], left_ref.shape[3]
    rank = halves * width
    din = cols * n_col
    act_rows = act_ref.shape[0]
    tokens = act_rows * n_row
    flip = lax.div(2 * me_out, outer)
    near = me_out + flip * (outer - 1 - 2 * me_out)

    def lanes_of(h):
        return slice(h * width, (h + 1) * width)

    def turned_back(position):
        return position + flip * (outer - 1 - 2 * position)

    def target(k):
        last = k // (outer - 1)
        return turned_back(outer - 1 - k - (k + near + 1) // outer + last * (near + 1))

    def chunk_at(j):
        return target(j % outer) * inner + (me_in + 1 + j // outer) % inner

    def load(q):
        return pltpu.make_async_copy(
            momentum_hbm.at[pl.ds(pl.multiple_of(q * piece, SUBLANES), piece), :], chunks.at[q], load_sem.at[q]
        )

    def store(q):
        return pltpu.make_async_copy(
            chunks.at[q], buffer_hbm.at[pl.ds(pl.multiple_of(q * piece, SUBLANES), piece), :], store_sem.at[q]
        )

    for j in range(n_col):
        load(chunk_at(j)).start()
    weight_copy = pltpu.make_async_copy(weight_hbm, weight, weight_sem)
    weight_copy.start()
    factor_high[...], factor_low[...] = split(factor_ref[...])

    row_peers = [lax.rem(row + d, n_row) for d in range(1, n_row)]
    col_peers = [lax.rem(col + d, n_col) for d in range(1, n_col)]
    greet([(peer, col) for peer in row_peers] + [(row, peer) for peer in col_peers])

    cot_copies = [
        remote(cot_ref, cot_all.at[col], cot_sem.at[0, d], cot_sem.at[1, d], (row, peer))
        for d, peer in enumerate(col_peers)
    ]
    act_copies = [
        remote(act_ref, act_all.at[row], act_sem.at[0, d], act_sem.at[1, d], (peer, col))
        for d, peer in enumerate(row_peers)
    ]
    for copy in cot_copies + act_copies:
        copy.start()
    act_all[row] = act_ref[...]
    cot_all[col] = cot_ref[...]

    def held_part(j):
        q = chunk_at(j)
        load(q).wait()
        return contract_split(split(chunks[q]), (factor_high[...], factor_low[...]), 1, 0)

    def turned_rows(q):
        return cot_turned[pl.ds(pl.multiple_of(q * piece, 2 * SUBLANES), piece), :]

    def token_part(j):
        rows = turned_rows(chunk_at(j))
        return contract(rows, token_high[...], 1, 0) + contract(rows, token_low[...], 1, 0)

    def inner_copy(h, d, k):
        peer = me_out * inner + (me_in + 1 + d) % inner
        return remote(
            send_inner.at[h, d, k],
            recv_inner.at[h, d, k],
            inner_sem.at[0, h, d, k],
            inner_sem.at[1, h, d, k],
            (row, peer),
        )

    def push(d, k):
        value = held_part(d * outer + k)
        for h in range(halves):
            send_inner[h, d, k] = value[:, lanes_of(h)]
        inner_copy(0, d, k).start()

    push(0, 0)
    for copy in act_copies:
        copy.wait()
    acts = act_all[...].reshape(tokens, cols)
    token_send[...] = contract(acts, factor_high[...], 1, 0) + contract(acts, factor_low[...], 1, 0)
    token_copies = [
        remote(
            token_send,
            token_recv.at[d],
            token_sem.at[0, d],
            token_sem.at[1, d],
            (row, me_out * inner + (me_in + 1 + d) % inner),
        )
        for d in range(inner - 1)
    ]
    for copy in token_copies:
        copy.start()
    for d in range(inner - 1):

        def push_next(k, carry, d=d):
            push(d, k)
            return carry

        lax.fori_loop(1 if d == 0 else 0, outer, push_next, 0)
    for h in range(1, halves):
        for d in range(inner - 1):

            def push_half(k, carry, h=h, d=d):
                inner_copy(h, d, k).start()
                return carry

            lax.fori_loop(0, outer, push_half, 0)
    for copy in cot_copies:
        copy.wait()

    def turn(b, carry):
        lanes = pl.ds(pl.multiple_of(b * LANES, LANES), LANES)
        slab = cot_all[:, :, lanes].astype(jnp.float32).reshape(tokens, LANES)
        cot_flat[:, lanes] = slab.astype(jnp.bfloat16)
        cot_turned[lanes, :] = slab.T.astype(jnp.bfloat16)
        return carry

    lax.fori_loop(0, cot_ref.shape[1] // LANES, turn, 0)

    token_sums = token_send[...]
    for d, copy in enumerate(token_copies):
        copy.wait()
        token_sums = token_sums + token_recv[d]
    token_high[...], token_low[...] = split(token_sums)

    def form(q):
        value = chunks[q] + contract(turned_rows(q), act_all[...].reshape(tokens, cols), 1, 0)
        chunks[q] = value
        chunk_high[q], chunk_low[q] = split(value)
        store(q).start()

    def own_part(k):
        j = (inner - 1) * outer + k
        value = held_part(j) + token_part(j)
        for h in range(halves):
            totals[h, k] = value[:, lanes_of(h)]

    def toward(q):
        return 2 * ((q - me_out + outer - 1) // outer) - 1

    def chain_copy(h, k):
        q = target(k)
        up = (q - me_out + outer - 1) // outer
        ending = (outer - (me_out - q)) // (outer - 1) * (1 - up)
        slot = q + ending * (outer - q)
        peer = (me_out + toward(q)) * inner + me_in
        return remote(
            totals.at[h, k], recv_outer.at[h, slot], chain_sem.at[h, k], chain_in_sem.at[h, slot], (row, peer)
        )

    def chain_arrival(h, slot):
        return remote(
            totals.at[h, 0], recv_outer.at[h, slot], chain_sem.at[h, 0], chain_in_sem.at[h, slot], (row, col)
        )

    def add_inner(h, k):
        for d in range(inner - 1):
            inner_copy(h, d, k).wait_recv()
            totals[h, k] = totals[h, k] + recv_inner[h, d, k]

    def chain(h, k):
        add_inner(h, k)
        q = target(k)

        @pl.when(jnp.logical_and(me_out - toward(q) >= 0, me_out - toward(q) < outer))
        def _():
            chain_arrival(h, q).wait_recv()
            totals[h, k] = totals[h, k] + recv_outer[h, q]

        chain_copy(h, k).start()

    def gather_outer(h, q, up):
        piece_ref = left_ref.at[h, q * inner + me_in]
        peer = (me_out + 2 * up - 1) * inner + me_in
        return remote(piece_ref, piece_ref, gather_send_sem.at[h, up, q], gather_outer_sem.at[h, q], (row, peer))

    def gather_inner(h, d, q):
        piece_ref = left_ref.at[h, q * inner + me_in]
        peer = me_out * inner + (me_in + 1 + d) % inner
        return remote(
            piece_ref, piece_ref, gather_inner_sem.at[0, h, d, q], gather_inner_sem.at[1, h, d, q], (row, peer)
        )

    def onward(h, q, start):
        up = 1 - (q - me_out + outer - 1) // outer

        @pl.when(jnp.logical_and(me_out + 2 * up - 1 >= 0, me_out + 2 * up - 1 < outer))
        def _():
            copy = gather_outer(h, q, up)
            copy.start() if start else copy.wait_send()

    def own_outward(h, start):
        for up in range(2):

            @pl.when(jnp.logical_and(me_out + 2 * up - 1 >= 0, me_out + 2 * up - 1 < outer))
            def _():
                copy = gather_outer(h, me_out, up)
                copy.start() if start else copy.wait_send()

    def settle(h):
        add_inner(h, outer - 1)

        @pl.when(me_out > 0)
        def _():
            chain_arrival(h, me_out).wait_recv()
            totals[h, outer - 1] = totals[h, outer - 1] + recv_outer[h, me_out]

        @pl.when(me_out < outer - 1)
        def _():
            chain_arrival(h, outer).wait_recv()
            totals[h, outer - 1] = totals[h, outer - 1] + recv_outer[h, outer]

        left_ref[h, col] = totals[h, outer - 1] / jnp.sqrt(jnp.float32(din))
        own_outward(h, True)
        for d in range(inner - 1):
            gather_inner(h, d, me_out).start()

    def arrival(n):
        paired = (2 * near - n - 1 + 2 * outer) // (2 * outer)
        step = (n // 2 + 1) * (2 * (n % 2) - 1)
        return turned_back(paired * (near + step) + (1 - paired) * (n + 1))

    def forward(h, n):
        q = arrival(n)
        gather_outer(h, q, 0).wait_recv()
        onward(h, q, True)
        for d in range(inner - 1):
            gather_inner(h, d, q).start()

    def absorb(h, q):
        value = left_ref[h, q]
        for g in range(h + 1):
            gram_ref[h, :, lanes_of(g)] = gram_ref[h, :, lanes_of(g)] + contract(value, left_ref[g, q], 0, 0, HIGHEST)
        projected_ref[h] = projected_ref[h] + contract_split(split(value), (chunk_high[q], chunk_low[q]), 0, 0)

    def absorb_outer(h, n):
        absorb(h, arrival(n) * inner + me_in)

    def absorb_inner(h, q):
        for d in range(inner - 1):
            gather_inner(h, d, q).wait_recv()
            absorb(h, q * inner + (me_in - 1 - d + inner) % inner)

    part = width // row_inner
    inner_peers = [lax.rem(row_in + 1 + d, row_inner) for d in range(row_inner - 1)]
    outer_peers = [lax.rem(row_out + 1 + d, row_outer) for d in range(row_outer - 1)]

    def rows_at(index):
        return pl.ds(pl.multiple_of(index * part, SUBLANES), part)

    class RowSum:
        def __init__(self, source, buffer_in, buffer_out, whole, sems, h, span):
            self.source, self.whole, self.h = source, whole, h
            self.buffer_in, self.buffer_out, self.lanes = buffer_in, buffer_out, pl.ds(0, span)
            self.sems = sems

        def view(self, ref, index, rows=None):
            if rows is None:
                return ref.at[self.h, index, :, self.lanes]
            return ref.at[self.h, rows, self.lanes]

        def begin(self):
            sem = self.sems[0]
            self.first = [
                remote(
                    self.view(self.source, None, rows_at(peer)),
                    self.view(self.buffer_in, d),
                    sem.at[0, self.h, d],
                    sem.at[1, self.h, d],
                    (row_out * row_inner + peer, col),
                )
                for d, peer in enumerate(inner_peers)
            ]
            for copy in self.first:
                copy.start()

        def cross(self):
            sem = self.sems[1]
            total = self.source[self.h, rows_at(row_in), self.lanes]
            for d, copy in enumerate(self.first):
                copy.wait()
                total = total + self.buffer_in[self.h, d, :, self.lanes]
            self.buffer_out[self.h, row_out, :, self.lanes] = total
            mine = self.view(self.buffer_out, row_out)
            self.second = [
                remote(mine, mine, sem.at[0, self.h, d], sem.at[1, self.h, d], (peer * row_inner + row_in, col))
                for d, peer in enumerate(outer_peers)
            ]
            for copy in self.second:
                copy.start()

        def spread(self):
            sem = self.sems[2]
            for copy in self.second:
                copy.wait()
            total = self.buffer_out[self.h, 0, :, self.lanes]
            for o in range(1, row_outer):
                total = total + self.buffer_out[self.h, o, :, self.lanes]
            self.whole[self.h, rows_at(row_in), self.lanes] = total
            mine = self.view(self.whole, None, rows_at(row_in))
            self.third = [
                remote(mine, mine, sem.at[0, self.h, d], sem.at[1, self.h, d], (row_out * row_inner + peer, col))
                for d, peer in enumerate(inner_peers)
            ]
            for copy in self.third:
                copy.start()

        def end(self):
            for copy in self.third:
                copy.wait()

    gram_sums = [
        RowSum(gram_ref, gram_in, gram_out, gram_all, (gram_in_sem, gram_out_sem, gram_all_sem), h, (h + 1) * width)
        for h in range(halves)
    ]
    proj_sums = [
        RowSum(projected_ref, proj_in, proj_out, proj_all, (proj_in_sem, proj_out_sem, proj_all_sem), h, cols)
        for h in range(halves)
    ]
    block = corner.shape[0]

    def prepare_half(h):
        known = h * width
        shift = ridge * identity(width)
        gram = gram_all[h, :, known : known + width]
        if h == 0:
            inverse[...] = jnp.zeros_like(inverse)
            rest = None
        else:
            before = inverse[:known, :known]
            solved = contract(before, gram_all[h, :, :known], 1, 1, HIGHEST)
            gram = gram - contract(solved, solved, 0, 0, HIGHEST)
            rest = contract(solved, before, 0, 0, HIGHEST)
        work[:, :width] = gram + shift
        work[:, width:] = identity(width)
        return rest

    def finish_half(h, rest):
        known = h * width
        inverse[known : known + width, known : known + width] = diagonal[...]
        if h > 0:
            inverse[known : known + width, :known] = -contract(diagonal[...], rest, 1, 0, HIGHEST)

    def right_half(h):
        known = (h + 1) * width
        projected = proj_all[: h + 1].reshape(known, cols)
        factor = split(inverse[h * width : known, :known])
        right = contract_split(factor, split(projected), 1, 0)
        right_high[lanes_of(h), :], right_low[lanes_of(h), :] = split(right)
        squares = jnp.sum(right * right, axis=1, keepdims=True)
        squares_all[col, :, lanes_of(h)] = jnp.broadcast_to(squares, (width, LANES)).T[:SUBLANES, :]
        return right

    gram_ref[...] = jnp.zeros_like(gram_ref)
    projected_ref[...] = jnp.zeros_like(projected_ref)

    def open_chain(k, carry):
        own_part(k)
        chain(0, k)
        return carry

    lax.fori_loop(0, outer - 1, open_chain, 0)
    own_part(outer - 1)

    def form_some(q, carry):
        form(q)
        return carry

    lax.fori_loop(0, n_col // 2, form_some, 0)
    settle(0)
    weight_copy.wait()
    input_part = contract(cot_flat[...], weight[...], 1, 0)
    input_send[...] = input_part.reshape(n_row, act_rows, cols)
    input_copies = [
        remote(input_send.at[peer], input_recv.at[d], input_sem.at[0, d], input_sem.at[1, d], (peer, col))
        for d, peer in enumerate(row_peers)
    ]
    for copy in input_copies:
        copy.start()
    chain(1, 0)
    lax.fori_loop(n_col // 2, n_col, form_some, 0)

    def next_chain(k, carry):
        chain(1, k)
        forward(0, k - 1)
        return carry

    lax.fori_loop(1, outer - 1, next_chain, 0)
    absorb(0, col)
    settle(1)
    forward(0, outer - 2)

    def absorb_first(n, carry):
        absorb_outer(0, n)
        return carry

    lax.fori_loop(0, outer - 1, absorb_first, 0)
    absorb_inner(0, me_out)
    absorb(1, col)

    def absorb_second(n, carry):
        forward(1, n)
        absorb_inner(0, arrival(n))
        absorb_outer(1, n)
        return carry

    lax.fori_loop(0, outer - 2, absorb_second, 0)
    absorb_inner(0, arrival(outer - 2))
    gram_sums[0].begin()
    proj_sums[0].begin()
    absorb_inner(1, me_out)
    gram_sums[0].cross()
    proj_sums[0].cross()
    forward(1, outer - 2)
    absorb_outer(1, outer - 2)
    gram_sums[0].spread()

    def absorb_third(n, carry):
        absorb_inner(1, arrival(n))
        return carry

    lax.fori_loop(0, outer - 1, absorb_third, 0)
    gram_sums[1].begin()
    proj_sums[1].begin()
    gram_sums[0].end()
    gram_sums[1].cross()
    proj_sums[0].spread()
    proj_sums[1].cross()
    rest = prepare_half(0)
    for low in range(0, width, block):
        invert_block(low, block, work, corner, diagonal)
        if low == 0:
            gram_sums[1].spread()
    finish_half(0, rest)
    proj_sums[0].end()
    right_turned_parts = [right_half(0)]
    gram_sums[1].end()
    rest = prepare_half(1)
    for low in range(0, width, block):
        invert_block(low, block, work, corner, diagonal)
        if low == 0:
            proj_sums[1].spread()
    finish_half(1, rest)
    proj_sums[1].end()
    right_turned_parts.append(right_half(1))

    copies = [
        remote(squares_all.at[col], squares_all.at[col], squares_sem.at[0, d], squares_sem.at[1, d], (row, peer))
        for d, peer in enumerate(col_peers)
    ]
    for copy in copies:
        copy.start()

    for h in range(halves):
        right_turned[:, lanes_of(h)] = right_turned_parts[h].T

    def result(q):
        return pltpu.make_async_copy(orthonormal.at[q], orthonormal_hbm.at[q], result_sem.at[q])

    right_copies = [
        pltpu.make_async_copy(right_high, right_high_hbm, result_sem.at[n_col]),
        pltpu.make_async_copy(right_low, right_low_hbm, result_sem.at[n_col + 1]),
        pltpu.make_async_copy(right_turned, right_turned_hbm, result_sem.at[n_col + 2]),
    ]
    for copy in right_copies:
        copy.start()

    def orthonormalise(q, carry):
        total = contract_split(split(left_ref[0, q]), split(inverse[:, :width]), 1, 1)
        for h in range(1, halves):
            total = total + contract_split(split(left_ref[h, q]), split(inverse[:, lanes_of(h)]), 1, 1)
        orthonormal[q] = total
        result(q).start()
        return carry

    lax.fori_loop(0, n_col, orthonormalise, 0)
    total = input_send[row]
    for d, copy in enumerate(input_copies):
        copy.wait()
        total = total + input_recv[d]
    input_ref[...] = total.astype(jnp.bfloat16)
    for q in range(n_col):
        store(q).wait()

    for h in range(halves):

        def drain(k, carry, h=h):
            for d in range(inner - 1):
                inner_copy(h, d, k).wait_send()
                gather_inner(h, d, k).wait_send()
            return carry

        lax.fori_loop(0, outer, drain, 0)

        def drain_chain(k, carry, h=h):
            chain_copy(h, k).wait_send()
            onward(h, arrival(k), False)
            return carry

        lax.fori_loop(0, outer - 1, drain_chain, 0)
        own_outward(h, False)

    for copy in copies:
        copy.wait()
    total = squares_all[0]
    for q in range(1, n_col):
        total = total + squares_all[q]
    scale_ref[...] = lax.rsqrt(total / din + 1e-06)
    for copy in right_copies:
        copy.wait()
    for q in range(n_col):
        result(q).wait()


def factor_call(n_row, n_col, ridge, activations, cotangent, weight, momentum, right_factor):
    inner, outer = two_stages(n_col)
    row_inner, row_outer = two_stages(n_row)
    rows, cols = momentum.shape
    rank = right_factor.shape[1]
    halves, width = 2, rank // 2
    piece = rows // n_col
    part = width // row_inner
    block = min(64, width)
    act_rows, cot_rows = activations.shape[0], cotangent.shape[0]
    tokens = act_rows * n_row
    f32, bf16 = jnp.float32, jnp.bfloat16
    vmem = pl.BlockSpec(memory_space=pltpu.VMEM)
    hbm = pl.BlockSpec(memory_space=pl.ANY)
    dma = pltpu.SemaphoreType.DMA
    return pl.pallas_call(
        functools.partial(factor_kernel, n_row, n_col, ridge),
        out_shape=(
            jax.ShapeDtypeStruct((act_rows, cols), bf16),
            jax.ShapeDtypeStruct((rows, cols), f32),
            jax.ShapeDtypeStruct((n_col, piece, rank), f32),
            jax.ShapeDtypeStruct((rank, cols), bf16),
            jax.ShapeDtypeStruct((rank, cols), bf16),
            jax.ShapeDtypeStruct((cols, rank), f32),
            jax.ShapeDtypeStruct((SUBLANES, rank), f32),
        ),
        in_specs=[vmem, vmem, hbm, hbm, vmem],
        out_specs=(vmem, hbm, hbm, hbm, hbm, hbm, vmem),
        scratch_shapes=[
            pltpu.VMEM((n_row, act_rows, cols), bf16),
            pltpu.VMEM((n_col, cot_rows, rows), bf16),
            pltpu.VMEM((tokens, rows), bf16),
            pltpu.VMEM((rows, tokens), bf16),
            pltpu.VMEM((n_col, piece, cols), f32),
            pltpu.VMEM((n_col, piece, cols), bf16),
            pltpu.VMEM((n_col, piece, cols), bf16),
            pltpu.VMEM((rows, cols), bf16),
            pltpu.VMEM((cols, rank), bf16),
            pltpu.VMEM((cols, rank), bf16),
            pltpu.VMEM((tokens, rank), f32),
            pltpu.VMEM((inner - 1, tokens, rank), f32),
            pltpu.VMEM((tokens, rank), bf16),
            pltpu.VMEM((tokens, rank), bf16),
            pltpu.VMEM((halves, inner - 1, outer, piece, width), f32),
            pltpu.VMEM((halves, inner - 1, outer, piece, width), f32),
            pltpu.VMEM((halves, outer, piece, width), f32),
            pltpu.VMEM((halves, outer + 1, piece, width), f32),
            pltpu.VMEM((halves, n_col, piece, width), f32),
            pltpu.VMEM((halves, width, rank), f32),
            pltpu.VMEM((halves, width, cols), f32),
            pltpu.VMEM((n_row, act_rows, cols), f32),
            pltpu.VMEM((n_row - 1, act_rows, cols), f32),
            pltpu.VMEM((halves, row_inner - 1, part, rank), f32),
            pltpu.VMEM((halves, row_outer, part, rank), f32),
            pltpu.VMEM((halves, width, rank), f32),
            pltpu.VMEM((halves, row_inner - 1, part, cols), f32),
            pltpu.VMEM((halves, row_outer, part, cols), f32),
            pltpu.VMEM((halves, width, cols), f32),
            pltpu.VMEM((rank, rank), f32),
            pltpu.VMEM((width, width), f32),
            pltpu.VMEM((width, 2 * width), f32),
            pltpu.VMEM((block, 2 * block), f32),
            pltpu.VMEM((n_col, SUBLANES, rank), f32),
            pltpu.VMEM((n_col, piece, rank), f32),
            pltpu.VMEM((rank, cols), bf16),
            pltpu.VMEM((rank, cols), bf16),
            pltpu.VMEM((cols, rank), f32),
            dma((n_col,)),
            dma((n_col,)),
            dma,
            dma((2, n_row - 1)),
            dma((2, n_col - 1)),
            dma((2, inner - 1)),
            dma((2, halves, inner - 1, outer)),
            dma((halves, outer)),
            dma((halves, outer + 1)),
            dma((halves, 2, outer)),
            dma((halves, outer)),
            dma((2, halves, inner - 1, outer)),
            dma((2, n_row - 1)),
            dma((2, halves, row_inner - 1)),
            dma((2, halves, row_outer - 1)),
            dma((2, halves, row_inner - 1)),
            dma((2, halves, row_inner - 1)),
            dma((2, halves, row_outer - 1)),
            dma((2, halves, row_inner - 1)),
            dma((2, n_col - 1)),
            dma((n_col + 3,)),
        ],
        compiler_params=pltpu.CompilerParams(
            collective_id=1, has_side_effects=True, vmem_limit_bytes=60 * 1024 * 1024
        ),
        name="factors",
    )(activations, cotangent, weight, momentum, right_factor)


def output_kernel(
    step_scale,
    buffer_ref,
    orthonormal_ref,
    right_high_ref,
    right_low_ref,
    right_turned_ref,
    scale_ref,
    momentum_ref,
    step_ref,
    next_ref,
):
    right = (right_high_ref[...], right_low_ref[...])
    orthonormal = orthonormal_ref[...]
    momentum_ref[...] = buffer_ref[...] - (1.0 - momentum_decay) * contract_split(split(orthonormal), right, 1, 0)
    scaled = orthonormal * scale_ref[:1, :]
    step_ref[...] = (step_scale * contract_split(split(scaled), right, 1, 0)).astype(jnp.bfloat16)
    next_ref[...] = right_turned_ref[...] * scale_ref[:1, :]


def output_tile(rows, cols):
    fits = [t for t in range(16, 289, 16) if rows % t == 0 and cols % (rows // t * SUBLANES) == 0]
    return max(fits, default=0)


def output_call(step_scale, buffer, orthonormal, right_high, right_low, right_turned, scale):
    rows, cols = buffer.shape
    rank = right_high.shape[0]
    tile = output_tile(rows, cols)
    steps = rows // tile
    f32 = jnp.float32
    whole = pl.BlockSpec((rank, cols), lambda i: (0, 0))
    return pl.pallas_call(
        functools.partial(output_kernel, step_scale),
        grid=(steps,),
        out_shape=(
            jax.ShapeDtypeStruct((rows, cols), f32),
            jax.ShapeDtypeStruct((rows, cols), jnp.bfloat16),
            jax.ShapeDtypeStruct((cols, rank), f32),
        ),
        in_specs=[
            pl.BlockSpec((tile, cols), lambda i: (i, 0)),
            pl.BlockSpec((tile, rank), lambda i: (i, 0)),
            whole,
            whole,
            pl.BlockSpec((cols // steps, rank), lambda i: (i, 0)),
            pl.BlockSpec(scale.shape, lambda i: (0, 0)),
        ],
        out_specs=(
            pl.BlockSpec((tile, cols), lambda i: (i, 0)),
            pl.BlockSpec((tile, cols), lambda i: (i, 0)),
            pl.BlockSpec((cols // steps, rank), lambda i: (i, 0)),
        ),
        compiler_params=pltpu.CompilerParams(
            dimension_semantics=("arbitrary",), vmem_limit_bytes=60 * 1024 * 1024
        ),
        name="outputs",
    )(buffer, orthonormal, right_high, right_low, right_turned, scale)


def kernel_shards(n_row, n_col, activations, cotangent, weight, momentum, right_factor):
    rows, cols = momentum.shape
    rank = right_factor.shape[1]
    dout = rows * n_row
    input_grad, buffer, orthonormal, right_high, right_low, right_turned, scale = factor_call(
        n_row, n_col, ridge_weight * dout, activations, cotangent, weight, momentum, right_factor
    )
    step_scale = (dout / rank) ** 0.5
    momentum_next, weight_step, right_next = output_call(
        step_scale, buffer, orthonormal.reshape(rows, rank), right_high, right_low, right_turned, scale
    )
    return input_grad, momentum_next, right_next, weight_step


def shards(n_row, n_col, activations, cotangent, weight, momentum, right_factor):
    rows, cols = momentum.shape
    rank = right_factor.shape[1]
    aligned = (
        rows % (n_col * 2 * SUBLANES) == 0
        and rows % LANES == 0
        and cols % LANES == 0
        and rank % (2 * LANES) == 0
        and output_tile(rows, cols) > 0
        and activations.shape[0] % (2 * SUBLANES) == 0
        and cotangent.shape[0] % SUBLANES == 0
        and two_stages(n_row)[0] > 1
        and two_stages(n_col)[0] > 1
        and n_col % 2 == 0
        and rank % (2 * two_stages(n_row)[0] * SUBLANES) == 0
    )
    chosen = kernel_shards if aligned else plain_shards
    return chosen(n_row, n_col, activations, cotangent, weight, momentum, right_factor)


def solution(mesh):
    placed = (P("row", "col"), P("col", "row"), P("row", "col"), P("row", "col"), P("col", None))
    return jax.shard_map(
        functools.partial(shards, mesh.shape["row"], mesh.shape["col"]),
        mesh=mesh,
        in_specs=placed,
        out_specs=(P("row", "col"), P("row", "col"), P("col", None), P("row", "col")),
        check_vma=False,
    )
```

```python
import functools

import jax
import jax.numpy as jnp
from jax import lax
from jax.experimental import pallas as pl
from jax.experimental.pallas import tpu as pltpu
from jax.sharding import PartitionSpec as P

momentum_decay = 0.6
ridge_weight = 0.001

HIGHEST = lax.Precision.HIGHEST
HIGH = lax.Precision.HIGH
SUBLANES = 8
LANES = 128
MESH = pl.DeviceIdType.MESH


def contract(left_side, right_side, left_dim, right_dim, precision=None):
    return lax.dot_general(
        left_side,
        right_side,
        (((left_dim,), (right_dim,)), ((), ())),
        precision=precision,
        preferred_element_type=jnp.float32,
    )


def identity(size):
    shape = (size, size)
    same = lax.broadcasted_iota(jnp.int32, shape, 0) == lax.broadcasted_iota(jnp.int32, shape, 1)
    return jnp.where(same, 1.0, 0.0).astype(jnp.float32)


def two_stages(size):
    inner = max(k for k in range(1, size + 1) if size % k == 0 and k * k <= size)
    return inner, size // inner


def split(value):
    high = value.astype(jnp.bfloat16)
    return high, (value - high.astype(jnp.float32)).astype(jnp.bfloat16)


def contract_split(left_pair, right_pair, left_dim, right_dim):
    total = contract(left_pair[0], right_pair[0], left_dim, right_dim)
    total = total + contract(left_pair[1], right_pair[0], left_dim, right_dim)
    return total + contract(left_pair[0], right_pair[1], left_dim, right_dim)


def inverse_factor_body(block, ridge, gram_ref, inverse_ref, work, corner):
    size = gram_ref.shape[0]
    work[:, :size] = gram_ref[...] + ridge * identity(size)
    work[:, size:] = identity(size)
    row_in_group = lax.broadcasted_iota(jnp.int32, (SUBLANES, 2 * block), 0)
    for low in range(0, size, block):
        high = low + block
        corner[:, :block] = work[low:high, low:high]
        corner[:, block:] = identity(block)
        groups = [corner[g : g + SUBLANES, :] for g in range(0, block, SUBLANES)]
        for k in range(block):
            own, inside = divmod(k, SUBLANES)
            pivot_row = groups[own][inside : inside + 1, :]
            scaled = pivot_row / pivot_row[:, k : k + 1]
            for g in range(own, len(groups)):
                factor = groups[g][:, k : k + 1]
                change = factor * scaled
                if g == own:
                    change = jnp.where(row_in_group > inside, change, 0.0)
                groups[g] = groups[g] - change
        for g, rows in enumerate(groups):
            corner[g * SUBLANES : (g + 1) * SUBLANES, :] = rows
        pivots = jnp.sum(corner[:, :block] * identity(block), axis=1, keepdims=True)
        corner_inverse = corner[:, block:] * (1.0 / jnp.sqrt(pivots))
        panel = contract(corner_inverse, work[low:high, :], 1, 0, HIGHEST)
        inverse_ref[low:high, :] = panel[:, size:]
        if high < size:
            update = contract(panel[:, :size], panel, 0, 0, HIGHEST)
            work[high:, :] = work[high:, :] - update[high:, :]


def eliminate_four(groups, k, row_in_group, lanes):
    own, inside = divmod(k, SUBLANES)
    rows = [groups[own][inside + j : inside + j + 1, :] for j in range(4)]
    def splat(value, j, sublanes):
        return jnp.broadcast_to(value[:, k + j : k + j + 1], (sublanes, lanes))
    a = [[splat(rows[i], j, 1) for j in range(i + 1)] for i in range(4)]
    i0 = 1.0 / a[0][0]
    i1 = a[0][0] * (1.0 / (a[0][0] * a[1][1] - a[1][0] * a[1][0]))
    l10, l20, l30 = a[1][0] * i0, a[2][0] * i0, a[3][0] * i0
    b21, b31 = a[2][1] - l20 * a[1][0], a[3][1] - l30 * a[1][0]
    l21, l31 = b21 * i1, b31 * i1
    d2 = a[2][2] - l20 * a[2][0] - l21 * b21
    b32 = a[3][2] - l30 * a[2][0] - l31 * b21
    s33 = a[3][3] - l30 * a[3][0] - l31 * b31
    i2 = 1.0 / d2
    i3 = d2 * (1.0 / (d2 * s33 - b32 * b32))
    l32 = b32 * i2
    u0 = rows[0]
    u1 = rows[1] - l10 * u0
    u2 = rows[2] - l20 * u0 - l21 * u1
    u3 = rows[3] - l30 * u0 - l31 * u1 - l32 * u2
    w = [u0 * i0, u1 * i1, u2 * i2, u3 * i3]
    for g in range(own, len(groups)):
        if g == own and inside + 4 == SUBLANES:
            change = None
        else:
            c = [splat(groups[g], j, SUBLANES) for j in range(4)]
            f1 = c[1] - c[0] * l10
            f2 = c[2] - c[0] * l20 - f1 * l21
            f3 = c[3] - c[0] * l30 - f1 * l31 - f2 * l32
            change = (c[0] * w[0] + f1 * w[1]) + (f2 * w[2] + f3 * w[3])
        if g == own:
            value = groups[g]
            if change is not None:
                value = jnp.where(row_in_group > inside + 3, value - change, value)
            for j, u in ((1, u1), (2, u2), (3, u3)):
                value = jnp.where(row_in_group == inside + j, u, value)
            groups[g] = value
        else:
            groups[g] = groups[g] - change


def invert_block(low, block, work, corner, inverse_ref):
    size = work.shape[0]
    high = low + block
    row_in_group = lax.broadcasted_iota(jnp.int32, (SUBLANES, 2 * block), 0)
    corner[:, :block] = work[low:high, low:high]
    corner[:, block:] = identity(block)
    groups = [corner[g : g + SUBLANES, :] for g in range(0, block, SUBLANES)]
    for k in range(0, block, 4):
        eliminate_four(groups, k, row_in_group, 2 * block)
    for g, rows in enumerate(groups):
        corner[g * SUBLANES : (g + 1) * SUBLANES, :] = rows
    pivots = jnp.sum(corner[:, :block] * identity(block), axis=1, keepdims=True)
    corner_inverse = corner[:, block:] * (1.0 / jnp.sqrt(pivots))
    panel = contract(corner_inverse, work[low:high, :], 1, 0, HIGHEST)
    inverse_ref[low:high, :] = panel[:, size:]
    if high < size:
        update = contract(panel[:, :size], panel, 0, 0, HIGHEST)
        work[high:, :] = work[high:, :] - update[high:, :]


def inverse_factor(gram_matrix, ridge):
    size = gram_matrix.shape[0]
    block = min(64, size)
    return pl.pallas_call(
        functools.partial(inverse_factor_body, block, ridge),
        out_shape=jax.ShapeDtypeStruct((size, size), jnp.float32),
        in_specs=[pl.BlockSpec(memory_space=pltpu.VMEM)],
        out_specs=pl.BlockSpec(memory_space=pltpu.VMEM),
        scratch_shapes=[
            pltpu.VMEM((size, 2 * size), jnp.float32),
            pltpu.VMEM((block, 2 * block), jnp.float32),
        ],
        cost_estimate=pl.CostEstimate(flops=20_000_000_000, bytes_accessed=8 * size * size, transcendentals=0),
        name="inverse_factor",
    )(gram_matrix)


def plain_shards(rows_of, cols_of, activations, cotangent, weight, momentum, right_factor):
    dout = momentum.shape[0] * rows_of
    din = momentum.shape[1] * cols_of
    rank = right_factor.shape[1]
    cot_tokens = lax.all_gather(cotangent, "col", axis=0, tiled=True)
    act_tokens = lax.all_gather(activations, "row", axis=0, tiled=True)
    held_part = contract(momentum, right_factor, 1, 0, HIGH)
    act_part = contract(act_tokens.astype(jnp.float32), right_factor, 1, 0, HIGH)
    grad_part = contract(cot_tokens.astype(jnp.float32), act_part, 0, 0, HIGH)
    left_part = (held_part + grad_part) / jnp.sqrt(jnp.float32(din))
    left_piece = lax.psum_scatter(left_part, "col", scatter_dimension=0, tiled=True)
    input_part = jnp.dot(cot_tokens, weight, preferred_element_type=jnp.float32)
    buffer = momentum + contract(cot_tokens, act_tokens, 0, 0, None)
    left_block = lax.all_gather(left_piece, "col", axis=0, tiled=True)
    gram_matrix = lax.psum(contract(left_block, left_block, 0, 0, HIGHEST), "row")
    projected_part = contract(buffer, left_block, 0, 0, HIGH)
    gram_matrix, projected_part = lax.optimization_barrier((gram_matrix, projected_part))
    projected = lax.psum(projected_part, "row")
    projected, input_part = lax.optimization_barrier((projected, input_part))
    input_sums = lax.psum_scatter(input_part, "row", scatter_dimension=0, tiled=True)
    inverse = inverse_factor(gram_matrix, ridge_weight * dout)
    orthonormal = contract(left_block, inverse, 1, 1, HIGHEST)
    right = contract(projected, inverse, 1, 1, HIGHEST)
    squares = lax.psum(jnp.sum(right * right, axis=0), "col")
    momentum_next = buffer - (1.0 - momentum_decay) * contract(orthonormal, right, 1, 1, HIGH)
    right_next = right * lax.rsqrt(squares / din + 1e-06)
    step_scale = jnp.sqrt(jnp.float32(dout) / rank)
    weight_step = (step_scale * contract(orthonormal, right_next, 1, 1, HIGH)).astype(jnp.bfloat16)
    return (input_sums.astype(jnp.bfloat16), momentum_next, right_next, weight_step)


def remote(source, target, send_sem, recv_sem, device):
    return pltpu.make_async_remote_copy(
        src_ref=source,
        dst_ref=target,
        send_sem=send_sem,
        recv_sem=recv_sem,
        device_id=device,
        device_id_type=MESH,
    )


def greet(devices):
    barrier = pltpu.get_barrier_semaphore()
    for device in devices:
        pl.semaphore_signal(barrier, inc=1, device_id=device, device_id_type=MESH)
    pl.semaphore_wait(barrier, len(devices))


def factor_kernel(
    n_row,
    n_col,
    ridge,
    act_ref,
    cot_ref,
    weight_hbm,
    momentum_hbm,
    factor_ref,
    input_ref,
    buffer_hbm,
    orthonormal_hbm,
    right_high_hbm,
    right_low_hbm,
    right_turned_hbm,
    scale_ref,
    act_all,
    cot_all,
    cot_flat,
    cot_turned,
    chunks,
    chunk_high,
    chunk_low,
    weight,
    factor_high,
    factor_low,
    token_send,
    token_recv,
    token_high,
    token_low,
    send_inner,
    recv_inner,
    totals,
    recv_outer,
    left_ref,
    gram_ref,
    projected_ref,
    input_send,
    input_recv,
    gram_in,
    gram_out,
    gram_all,
    proj_in,
    proj_out,
    proj_all,
    inverse,
    diagonal,
    work,
    corner,
    squares_all,
    orthonormal,
    right_high,
    right_low,
    right_turned,
    load_sem,
    store_sem,
    weight_sem,
    act_sem,
    cot_sem,
    token_sem,
    inner_sem,
    chain_sem,
    chain_in_sem,
    gather_send_sem,
    gather_outer_sem,
    gather_inner_sem,
    input_sem,
    gram_in_sem,
    gram_out_sem,
    gram_all_sem,
    proj_in_sem,
    proj_out_sem,
    proj_all_sem,
    squares_sem,
    result_sem,
):
    inner, outer = two_stages(n_col)
    row_inner, row_outer = two_stages(n_row)
    row, col = lax.axis_index("row"), lax.axis_index("col")
    me_in, me_out = lax.rem(col, inner), lax.div(col, inner)
    row_in, row_out = lax.rem(row, row_inner), lax.div(row, row_inner)
    piece, cols = chunks.shape[1], chunks.shape[2]
    halves, width = left_ref.shape[0], left_ref.shape[3]
    rank = halves * width
    din = cols * n_col
    act_rows = act_ref.shape[0]
    tokens = act_rows * n_row
    flip = lax.div(2 * me_out, outer)
    near = me_out + flip * (outer - 1 - 2 * me_out)

    def lanes_of(h):
        return slice(h * width, (h + 1) * width)

    def turned_back(position):
        return position + flip * (outer - 1 - 2 * position)

    def target(k):
        last = k // (outer - 1)
        return turned_back(outer - 1 - k - (k + near + 1) // outer + last * (near + 1))

    def chunk_at(j):
        return target(j % outer) * inner + (me_in + 1 + j // outer) % inner

    def load(q):
        return pltpu.make_async_copy(
            momentum_hbm.at[pl.ds(pl.multiple_of(q * piece, SUBLANES), piece), :], chunks.at[q], load_sem.at[q]
        )

    def store(q):
        return pltpu.make_async_copy(
            chunks.at[q], buffer_hbm.at[pl.ds(pl.multiple_of(q * piece, SUBLANES), piece), :], store_sem.at[q]
        )

    for j in range(n_col):
        load(chunk_at(j)).start()
    weight_copy = pltpu.make_async_copy(weight_hbm, weight, weight_sem)
    weight_copy.start()
    factor_high[...], factor_low[...] = split(factor_ref[...])

    row_peers = [lax.rem(row + d, n_row) for d in range(1, n_row)]
    col_peers = [lax.rem(col + d, n_col) for d in range(1, n_col)]
    greet([(peer, col) for peer in row_peers] + [(row, peer) for peer in col_peers])

    cot_copies = [
        remote(cot_ref, cot_all.at[col], cot_sem.at[0, d], cot_sem.at[1, d], (row, peer))
        for d, peer in enumerate(col_peers)
    ]
    act_copies = [
        remote(act_ref, act_all.at[row], act_sem.at[0, d], act_sem.at[1, d], (peer, col))
        for d, peer in enumerate(row_peers)
    ]
    for copy in cot_copies + act_copies:
        copy.start()
    act_all[row] = act_ref[...]
    cot_all[col] = cot_ref[...]

    def held_part(j):
        q = chunk_at(j)
        load(q).wait()
        return contract_split(split(chunks[q]), (factor_high[...], factor_low[...]), 1, 0)

    def turned_rows(q):
        return cot_turned[pl.ds(pl.multiple_of(q * piece, 2 * SUBLANES), piece), :]

    def token_part(j):
        rows = turned_rows(chunk_at(j))
        return contract(rows, token_high[...], 1, 0) + contract(rows, token_low[...], 1, 0)

    def inner_copy(h, d, k):
        peer = me_out * inner + (me_in + 1 + d) % inner
        return remote(
            send_inner.at[h, d, k],
            recv_inner.at[h, d, k],
            inner_sem.at[0, h, d, k],
            inner_sem.at[1, h, d, k],
            (row, peer),
        )

    def push(d, k):
        value = held_part(d * outer + k)
        for h in range(halves):
            send_inner[h, d, k] = value[:, lanes_of(h)]
        inner_copy(0, d, k).start()

    push(0, 0)
    for copy in act_copies:
        copy.wait()
    acts = act_all[...].reshape(tokens, cols)
    token_send[...] = contract(acts, factor_high[...], 1, 0) + contract(acts, factor_low[...], 1, 0)
    token_copies = [
        remote(
            token_send,
            token_recv.at[d],
            token_sem.at[0, d],
            token_sem.at[1, d],
            (row, me_out * inner + (me_in + 1 + d) % inner),
        )
        for d in range(inner - 1)
    ]
    for copy in token_copies:
        copy.start()
    for d in range(inner - 1):

        def push_next(k, carry, d=d):
            push(d, k)
            return carry

        lax.fori_loop(1 if d == 0 else 0, outer, push_next, 0)
    for h in range(1, halves):
        for d in range(inner - 1):

            def push_half(k, carry, h=h, d=d):
                inner_copy(h, d, k).start()
                return carry

            lax.fori_loop(0, outer, push_half, 0)
    for copy in cot_copies:
        copy.wait()

    def turn(b, carry):
        lanes = pl.ds(pl.multiple_of(b * LANES, LANES), LANES)
        slab = cot_all[:, :, lanes].astype(jnp.float32).reshape(tokens, LANES)
        cot_flat[:, lanes] = slab.astype(jnp.bfloat16)
        cot_turned[lanes, :] = slab.T.astype(jnp.bfloat16)
        return carry

    lax.fori_loop(0, cot_ref.shape[1] // LANES, turn, 0)

    token_sums = token_send[...]
    for d, copy in enumerate(token_copies):
        copy.wait()
        token_sums = token_sums + token_recv[d]
    token_high[...], token_low[...] = split(token_sums)

    def form(q):
        value = chunks[q] + contract(turned_rows(q), act_all[...].reshape(tokens, cols), 1, 0)
        chunks[q] = value
        chunk_high[q], chunk_low[q] = split(value)
        store(q).start()

    def own_part(k):
        j = (inner - 1) * outer + k
        value = held_part(j) + token_part(j)
        for h in range(halves):
            totals[h, k] = value[:, lanes_of(h)]

    def toward(q):
        return 2 * ((q - me_out + outer - 1) // outer) - 1

    def chain_copy(h, k):
        q = target(k)
        up = (q - me_out + outer - 1) // outer
        ending = (outer - (me_out - q)) // (outer - 1) * (1 - up)
        slot = q + ending * (outer - q)
        peer = (me_out + toward(q)) * inner + me_in
        return remote(
            totals.at[h, k], recv_outer.at[h, slot], chain_sem.at[h, k], chain_in_sem.at[h, slot], (row, peer)
        )

    def chain_arrival(h, slot):
        return remote(
            totals.at[h, 0], recv_outer.at[h, slot], chain_sem.at[h, 0], chain_in_sem.at[h, slot], (row, col)
        )

    def add_inner(h, k):
        for d in range(inner - 1):
            inner_copy(h, d, k).wait_recv()
            totals[h, k] = totals[h, k] + recv_inner[h, d, k]

    def chain(h, k):
        add_inner(h, k)
        q = target(k)

        @pl.when(jnp.logical_and(me_out - toward(q) >= 0, me_out - toward(q) < outer))
        def _():
            chain_arrival(h, q).wait_recv()
            totals[h, k] = totals[h, k] + recv_outer[h, q]

        chain_copy(h, k).start()

    def gather_outer(h, q, up):
        piece_ref = left_ref.at[h, q * inner + me_in]
        peer = (me_out + 2 * up - 1) * inner + me_in
        return remote(piece_ref, piece_ref, gather_send_sem.at[h, up, q], gather_outer_sem.at[h, q], (row, peer))

    def gather_inner(h, d, q):
        piece_ref = left_ref.at[h, q * inner + me_in]
        peer = me_out * inner + (me_in + 1 + d) % inner
        return remote(
            piece_ref, piece_ref, gather_inner_sem.at[0, h, d, q], gather_inner_sem.at[1, h, d, q], (row, peer)
        )

    def onward(h, q, start):
        up = 1 - (q - me_out + outer - 1) // outer

        @pl.when(jnp.logical_and(me_out + 2 * up - 1 >= 0, me_out + 2 * up - 1 < outer))
        def _():
            copy = gather_outer(h, q, up)
            copy.start() if start else copy.wait_send()

    def own_outward(h, start):
        for up in range(2):

            @pl.when(jnp.logical_and(me_out + 2 * up - 1 >= 0, me_out + 2 * up - 1 < outer))
            def _():
                copy = gather_outer(h, me_out, up)
                copy.start() if start else copy.wait_send()

    def settle(h):
        add_inner(h, outer - 1)

        @pl.when(me_out > 0)
        def _():
            chain_arrival(h, me_out).wait_recv()
            totals[h, outer - 1] = totals[h, outer - 1] + recv_outer[h, me_out]

        @pl.when(me_out < outer - 1)
        def _():
            chain_arrival(h, outer).wait_recv()
            totals[h, outer - 1] = totals[h, outer - 1] + recv_outer[h, outer]

        left_ref[h, col] = totals[h, outer - 1] / jnp.sqrt(jnp.float32(din))
        own_outward(h, True)
        for d in range(inner - 1):
            gather_inner(h, d, me_out).start()

    def arrival(n):
        paired = (2 * near - n - 1 + 2 * outer) // (2 * outer)
        step = (n // 2 + 1) * (1 - 2 * (n % 2))
        return turned_back(paired * (near + step) + (1 - paired) * (n + 1))

    def forward(h, n):
        q = arrival(n)
        gather_outer(h, q, 0).wait_recv()
        onward(h, q, True)
        for d in range(inner - 1):
            gather_inner(h, d, q).start()

    def absorb(h, q):
        value = left_ref[h, q]
        for g in range(h + 1):
            gram_ref[h, :, lanes_of(g)] = gram_ref[h, :, lanes_of(g)] + contract(value, left_ref[g, q], 0, 0, HIGHEST)
        projected_ref[h] = projected_ref[h] + contract_split(split(value), (chunk_high[q], chunk_low[q]), 0, 0)

    def absorb_outer(h, n):
        absorb(h, arrival(n) * inner + me_in)

    def absorb_inner(h, q):
        for d in range(inner - 1):
            gather_inner(h, d, q).wait_recv()
            absorb(h, q * inner + (me_in - 1 - d + inner) % inner)

    part = width // row_inner
    inner_peers = [lax.rem(row_in + 1 + d, row_inner) for d in range(row_inner - 1)]
    outer_peers = [lax.rem(row_out + 1 + d, row_outer) for d in range(row_outer - 1)]

    def rows_at(index):
        return pl.ds(pl.multiple_of(index * part, SUBLANES), part)

    class RowSum:
        def __init__(self, source, buffer_in, buffer_out, whole, sems, h, span):
            self.source, self.whole, self.h = source, whole, h
            self.buffer_in, self.buffer_out, self.lanes = buffer_in, buffer_out, pl.ds(0, span)
            self.sems = sems

        def view(self, ref, index, rows=None):
            if rows is None:
                return ref.at[self.h, index, :, self.lanes]
            return ref.at[self.h, rows, self.lanes]

        def begin(self):
            sem = self.sems[0]
            self.first = [
                remote(
                    self.view(self.source, None, rows_at(peer)),
                    self.view(self.buffer_in, d),
                    sem.at[0, self.h, d],
                    sem.at[1, self.h, d],
                    (row_out * row_inner + peer, col),
                )
                for d, peer in enumerate(inner_peers)
            ]
            for copy in self.first:
                copy.start()

        def cross(self):
            sem = self.sems[1]
            total = self.source[self.h, rows_at(row_in), self.lanes]
            for d, copy in enumerate(self.first):
                copy.wait()
                total = total + self.buffer_in[self.h, d, :, self.lanes]
            self.buffer_out[self.h, row_out, :, self.lanes] = total
            mine = self.view(self.buffer_out, row_out)
            self.second = [
                remote(mine, mine, sem.at[0, self.h, d], sem.at[1, self.h, d], (peer * row_inner + row_in, col))
                for d, peer in enumerate(outer_peers)
            ]
            for copy in self.second:
                copy.start()

        def spread(self):
            sem = self.sems[2]
            for copy in self.second:
                copy.wait()
            total = self.buffer_out[self.h, 0, :, self.lanes]
            for o in range(1, row_outer):
                total = total + self.buffer_out[self.h, o, :, self.lanes]
            self.whole[self.h, rows_at(row_in), self.lanes] = total
            mine = self.view(self.whole, None, rows_at(row_in))
            self.third = [
                remote(mine, mine, sem.at[0, self.h, d], sem.at[1, self.h, d], (row_out * row_inner + peer, col))
                for d, peer in enumerate(inner_peers)
            ]
            for copy in self.third:
                copy.start()

        def end(self):
            for copy in self.third:
                copy.wait()

    gram_sums = [
        RowSum(gram_ref, gram_in, gram_out, gram_all, (gram_in_sem, gram_out_sem, gram_all_sem), h, (h + 1) * width)
        for h in range(halves)
    ]
    proj_sums = [
        RowSum(projected_ref, proj_in, proj_out, proj_all, (proj_in_sem, proj_out_sem, proj_all_sem), h, cols)
        for h in range(halves)
    ]
    block = corner.shape[0]

    def prepare_half(h):
        known = h * width
        shift = ridge * identity(width)
        gram = gram_all[h, :, known : known + width]
        if h == 0:
            inverse[...] = jnp.zeros_like(inverse)
            rest = None
        else:
            before = inverse[:known, :known]
            solved = contract(before, gram_all[h, :, :known], 1, 1, HIGHEST)
            gram = gram - contract(solved, solved, 0, 0, HIGHEST)
            rest = contract(solved, before, 0, 0, HIGHEST)
        work[:, :width] = gram + shift
        work[:, width:] = identity(width)
        return rest

    def finish_half(h, rest):
        known = h * width
        inverse[known : known + width, known : known + width] = diagonal[...]
        if h > 0:
            inverse[known : known + width, :known] = -contract(diagonal[...], rest, 1, 0, HIGHEST)

    def right_half(h):
        known = (h + 1) * width
        projected = proj_all[: h + 1].reshape(known, cols)
        factor = split(inverse[h * width : known, :known])
        right = contract_split(factor, split(projected), 1, 0)
        right_high[lanes_of(h), :], right_low[lanes_of(h), :] = split(right)
        squares = jnp.sum(right * right, axis=1, keepdims=True)
        squares_all[col, :, lanes_of(h)] = jnp.broadcast_to(squares, (width, LANES)).T[:SUBLANES, :]
        return right

    gram_ref[...] = jnp.zeros_like(gram_ref)
    projected_ref[...] = jnp.zeros_like(projected_ref)

    def open_chain(k, carry):
        own_part(k)
        chain(0, k)
        return carry

    lax.fori_loop(0, outer - 1, open_chain, 0)
    own_part(outer - 1)

    def form_some(q, carry):
        form(q)
        return carry

    lax.fori_loop(0, n_col // 2, form_some, 0)

    @pl.when(near == 0)
    def _():
        chain(1, 0)

    settle(0)
    weight_copy.wait()
    input_part = contract(cot_flat[...], weight[...], 1, 0)
    input_send[...] = input_part.reshape(n_row, act_rows, cols)
    input_copies = [
        remote(input_send.at[peer], input_recv.at[d], input_sem.at[0, d], input_sem.at[1, d], (peer, col))
        for d, peer in enumerate(row_peers)
    ]
    for copy in input_copies:
        copy.start()
    lax.fori_loop(n_col // 2, n_col, form_some, 0)

    def next_chain(k, carry):
        chain(1, k)
        return carry

    def next_forward(n, carry):
        forward(0, n)
        return carry

    def next_both(k, carry):
        chain(1, k)
        forward(0, k - 1)
        return carry

    @pl.when(near == 0)
    def _():
        lax.fori_loop(1, outer - 1, next_chain, 0)
        lax.fori_loop(0, outer - 2, next_forward, 0)

    @pl.when(near > 0)
    def _():
        chain(1, 0)
        lax.fori_loop(1, outer - 1, next_both, 0)

    absorb(0, col)
    settle(1)
    forward(0, outer - 2)

    def absorb_first(n, carry):
        absorb_outer(0, n)
        return carry

    lax.fori_loop(0, outer - 1, absorb_first, 0)
    absorb_inner(0, me_out)
    absorb(1, col)

    def absorb_second(n, carry):
        forward(1, n)
        absorb_inner(0, arrival(n))
        absorb_outer(1, n)
        return carry

    lax.fori_loop(0, outer - 2, absorb_second, 0)
    absorb_inner(0, arrival(outer - 2))
    gram_sums[0].begin()
    proj_sums[0].begin()
    absorb_inner(1, me_out)
    gram_sums[0].cross()
    proj_sums[0].cross()
    forward(1, outer - 2)
    absorb_outer(1, outer - 2)
    gram_sums[0].spread()

    def absorb_third(n, carry):
        absorb_inner(1, arrival(n))
        return carry

    lax.fori_loop(0, outer - 1, absorb_third, 0)
    gram_sums[1].begin()
    proj_sums[1].begin()
    gram_sums[0].end()
    gram_sums[1].cross()
    proj_sums[1].cross()
    rest = prepare_half(0)
    for low in range(0, width, block):
        invert_block(low, block, work, corner, diagonal)
        if low == 0:
            gram_sums[1].spread()
    proj_sums[0].spread()
    finish_half(0, rest)
    proj_sums[0].end()
    right_turned_parts = [right_half(0)]
    gram_sums[1].end()
    rest = prepare_half(1)
    for low in range(0, width, block):
        invert_block(low, block, work, corner, diagonal)
        if low == 0:
            proj_sums[1].spread()
    finish_half(1, rest)
    proj_sums[1].end()
    right_turned_parts.append(right_half(1))

    copies = [
        remote(squares_all.at[col], squares_all.at[col], squares_sem.at[0, d], squares_sem.at[1, d], (row, peer))
        for d, peer in enumerate(col_peers)
    ]
    for copy in copies:
        copy.start()

    for h in range(halves):
        right_turned[:, lanes_of(h)] = right_turned_parts[h].T

    def result(q):
        return pltpu.make_async_copy(orthonormal.at[q], orthonormal_hbm.at[q], result_sem.at[q])

    right_copies = [
        pltpu.make_async_copy(right_high, right_high_hbm, result_sem.at[n_col]),
        pltpu.make_async_copy(right_low, right_low_hbm, result_sem.at[n_col + 1]),
        pltpu.make_async_copy(right_turned, right_turned_hbm, result_sem.at[n_col + 2]),
    ]
    for copy in right_copies:
        copy.start()

    def orthonormalise(q, carry):
        total = contract_split(split(left_ref[0, q]), split(inverse[:, :width]), 1, 1)
        for h in range(1, halves):
            total = total + contract_split(split(left_ref[h, q]), split(inverse[:, lanes_of(h)]), 1, 1)
        orthonormal[q] = total
        result(q).start()
        return carry

    lax.fori_loop(0, n_col, orthonormalise, 0)
    total = input_send[row]
    for d, copy in enumerate(input_copies):
        copy.wait()
        total = total + input_recv[d]
    input_ref[...] = total.astype(jnp.bfloat16)
    for q in range(n_col):
        store(q).wait()

    for h in range(halves):

        def drain(k, carry, h=h):
            for d in range(inner - 1):
                inner_copy(h, d, k).wait_send()
                gather_inner(h, d, k).wait_send()
            return carry

        lax.fori_loop(0, outer, drain, 0)

        def drain_chain(k, carry, h=h):
            chain_copy(h, k).wait_send()
            onward(h, arrival(k), False)
            return carry

        lax.fori_loop(0, outer - 1, drain_chain, 0)
        own_outward(h, False)

    for copy in copies:
        copy.wait()
    total = squares_all[0]
    for q in range(1, n_col):
        total = total + squares_all[q]
    scale_ref[...] = lax.rsqrt(total / din + 1e-06)
    for copy in right_copies:
        copy.wait()
    for q in range(n_col):
        result(q).wait()


def factor_call(n_row, n_col, ridge, activations, cotangent, weight, momentum, right_factor):
    inner, outer = two_stages(n_col)
    row_inner, row_outer = two_stages(n_row)
    rows, cols = momentum.shape
    rank = right_factor.shape[1]
    halves, width = 2, rank // 2
    piece = rows // n_col
    part = width // row_inner
    block = min(64, width)
    act_rows, cot_rows = activations.shape[0], cotangent.shape[0]
    tokens = act_rows * n_row
    f32, bf16 = jnp.float32, jnp.bfloat16
    vmem = pl.BlockSpec(memory_space=pltpu.VMEM)
    hbm = pl.BlockSpec(memory_space=pl.ANY)
    dma = pltpu.SemaphoreType.DMA
    return pl.pallas_call(
        functools.partial(factor_kernel, n_row, n_col, ridge),
        out_shape=(
            jax.ShapeDtypeStruct((act_rows, cols), bf16),
            jax.ShapeDtypeStruct((rows, cols), f32),
            jax.ShapeDtypeStruct((n_col, piece, rank), f32),
            jax.ShapeDtypeStruct((rank, cols), bf16),
            jax.ShapeDtypeStruct((rank, cols), bf16),
            jax.ShapeDtypeStruct((cols, rank), f32),
            jax.ShapeDtypeStruct((SUBLANES, rank), f32),
        ),
        in_specs=[vmem, vmem, hbm, hbm, vmem],
        out_specs=(vmem, hbm, hbm, hbm, hbm, hbm, vmem),
        scratch_shapes=[
            pltpu.VMEM((n_row, act_rows, cols), bf16),
            pltpu.VMEM((n_col, cot_rows, rows), bf16),
            pltpu.VMEM((tokens, rows), bf16),
            pltpu.VMEM((rows, tokens), bf16),
            pltpu.VMEM((n_col, piece, cols), f32),
            pltpu.VMEM((n_col, piece, cols), bf16),
            pltpu.VMEM((n_col, piece, cols), bf16),
            pltpu.VMEM((rows, cols), bf16),
            pltpu.VMEM((cols, rank), bf16),
            pltpu.VMEM((cols, rank), bf16),
            pltpu.VMEM((tokens, rank), f32),
            pltpu.VMEM((inner - 1, tokens, rank), f32),
            pltpu.VMEM((tokens, rank), bf16),
            pltpu.VMEM((tokens, rank), bf16),
            pltpu.VMEM((halves, inner - 1, outer, piece, width), f32),
            pltpu.VMEM((halves, inner - 1, outer, piece, width), f32),
            pltpu.VMEM((halves, outer, piece, width), f32),
            pltpu.VMEM((halves, outer + 1, piece, width), f32),
            pltpu.VMEM((halves, n_col, piece, width), f32),
            pltpu.VMEM((halves, width, rank), f32),
            pltpu.VMEM((halves, width, cols), f32),
            pltpu.VMEM((n_row, act_rows, cols), f32),
            pltpu.VMEM((n_row - 1, act_rows, cols), f32),
            pltpu.VMEM((halves, row_inner - 1, part, rank), f32),
            pltpu.VMEM((halves, row_outer, part, rank), f32),
            pltpu.VMEM((halves, width, rank), f32),
            pltpu.VMEM((halves, row_inner - 1, part, cols), f32),
            pltpu.VMEM((halves, row_outer, part, cols), f32),
            pltpu.VMEM((halves, width, cols), f32),
            pltpu.VMEM((rank, rank), f32),
            pltpu.VMEM((width, width), f32),
            pltpu.VMEM((width, 2 * width), f32),
            pltpu.VMEM((block, 2 * block), f32),
            pltpu.VMEM((n_col, SUBLANES, rank), f32),
            pltpu.VMEM((n_col, piece, rank), f32),
            pltpu.VMEM((rank, cols), bf16),
            pltpu.VMEM((rank, cols), bf16),
            pltpu.VMEM((cols, rank), f32),
            dma((n_col,)),
            dma((n_col,)),
            dma,
            dma((2, n_row - 1)),
            dma((2, n_col - 1)),
            dma((2, inner - 1)),
            dma((2, halves, inner - 1, outer)),
            dma((halves, outer)),
            dma((halves, outer + 1)),
            dma((halves, 2, outer)),
            dma((halves, outer)),
            dma((2, halves, inner - 1, outer)),
            dma((2, n_row - 1)),
            dma((2, halves, row_inner - 1)),
            dma((2, halves, row_outer - 1)),
            dma((2, halves, row_inner - 1)),
            dma((2, halves, row_inner - 1)),
            dma((2, halves, row_outer - 1)),
            dma((2, halves, row_inner - 1)),
            dma((2, n_col - 1)),
            dma((n_col + 3,)),
        ],
        compiler_params=pltpu.CompilerParams(
            collective_id=1, has_side_effects=True, vmem_limit_bytes=60 * 1024 * 1024
        ),
        name="factors",
    )(activations, cotangent, weight, momentum, right_factor)


def output_kernel(
    step_scale,
    buffer_ref,
    orthonormal_ref,
    right_high_ref,
    right_low_ref,
    right_turned_ref,
    scale_ref,
    sums_ref,
    momentum_ref,
    step_ref,
    next_ref,
    input_ref,
):
    input_ref[...] = sums_ref[...]
    right = jnp.concatenate([right_high_ref[...], right_high_ref[...], right_low_ref[...]], axis=0)

    def product(value):
        high, low = split(value)
        return contract(jnp.concatenate([high, low, high], axis=1), right, 1, 0)

    orthonormal = orthonormal_ref[...]
    momentum_ref[...] = buffer_ref[...] - (1.0 - momentum_decay) * product(orthonormal)
    step_ref[...] = (step_scale * product(orthonormal * scale_ref[:1, :])).astype(jnp.bfloat16)
    next_ref[...] = right_turned_ref[...] * scale_ref[:1, :]


def output_tile(rows, cols):
    fits = [t for t in range(16, min(rows // 4, 576) + 1, 16) if rows % t == 0 and cols % (rows // t * SUBLANES) == 0]
    return max(fits, default=0)


def output_call(step_scale, buffer, orthonormal, right_high, right_low, right_turned, scale, sums):
    rows, cols = buffer.shape
    rank = right_high.shape[0]
    tile = output_tile(rows, cols)
    steps = rows // tile
    f32 = jnp.float32
    whole = pl.BlockSpec((rank, cols), lambda i: (0, 0))
    return pl.pallas_call(
        functools.partial(output_kernel, step_scale),
        grid=(steps,),
        out_shape=(
            jax.ShapeDtypeStruct((rows, cols), f32),
            jax.ShapeDtypeStruct((rows, cols), jnp.bfloat16),
            jax.ShapeDtypeStruct((cols, rank), f32),
            jax.ShapeDtypeStruct(sums.shape, sums.dtype),
        ),
        in_specs=[
            pl.BlockSpec((tile, cols), lambda i: (i, 0)),
            pl.BlockSpec((tile, rank), lambda i: (i, 0)),
            whole,
            whole,
            pl.BlockSpec((cols // steps, rank), lambda i: (i, 0)),
            pl.BlockSpec(scale.shape, lambda i: (0, 0)),
            pl.BlockSpec(sums.shape, lambda i: (0, 0)),
        ],
        out_specs=(
            pl.BlockSpec((tile, cols), lambda i: (i, 0)),
            pl.BlockSpec((tile, cols), lambda i: (i, 0)),
            pl.BlockSpec((cols // steps, rank), lambda i: (i, 0)),
            pl.BlockSpec(sums.shape, lambda i: (0, 0)),
        ),
        compiler_params=pltpu.CompilerParams(
            dimension_semantics=("arbitrary",), vmem_limit_bytes=60 * 1024 * 1024
        ),
        name="outputs",
    )(buffer, orthonormal, right_high, right_low, right_turned, scale, sums)


def kernel_shards(n_row, n_col, activations, cotangent, weight, momentum, right_factor):
    rows, cols = momentum.shape
    rank = right_factor.shape[1]
    dout = rows * n_row
    input_sums, buffer, orthonormal, right_high, right_low, right_turned, scale = factor_call(
        n_row, n_col, ridge_weight * dout, activations, cotangent, weight, momentum, right_factor
    )
    step_scale = (dout / rank) ** 0.5
    momentum_next, weight_step, right_next, input_grad = output_call(
        step_scale, buffer, orthonormal.reshape(rows, rank), right_high, right_low, right_turned, scale, input_sums
    )
    return input_grad, momentum_next, right_next, weight_step


def shards(n_row, n_col, activations, cotangent, weight, momentum, right_factor):
    rows, cols = momentum.shape
    rank = right_factor.shape[1]
    aligned = (
        rows % (n_col * 2 * SUBLANES) == 0
        and rows % LANES == 0
        and cols % LANES == 0
        and rank % (2 * LANES) == 0
        and output_tile(rows, cols) > 0
        and activations.shape[0] % (2 * SUBLANES) == 0
        and cotangent.shape[0] % SUBLANES == 0
        and two_stages(n_row)[0] > 1
        and two_stages(n_col)[0] > 1
        and n_col % 2 == 0
        and rank % (2 * two_stages(n_row)[0] * SUBLANES) == 0
    )
    chosen = kernel_shards if aligned else plain_shards
    return chosen(n_row, n_col, activations, cotangent, weight, momentum, right_factor)


def solution(mesh):
    placed = (P("row", "col"), P("col", "row"), P("row", "col"), P("row", "col"), P("col", None))
    return jax.shard_map(
        functools.partial(shards, mesh.shape["row"], mesh.shape["col"]),
        mesh=mesh,
        in_specs=placed,
        out_specs=(P("row", "col"), P("row", "col"), P("col", None), P("row", "col")),
        check_vma=False,
    )
```

```python
import functools

import jax
import jax.numpy as jnp
from jax import lax
from jax.experimental import pallas as pl
from jax.experimental.pallas import tpu as pltpu
from jax.sharding import PartitionSpec as P

momentum_decay = 0.6
ridge_weight = 0.001

HIGHEST = lax.Precision.HIGHEST
HIGH = lax.Precision.HIGH
SUBLANES = 8
LANES = 128
MESH = pl.DeviceIdType.MESH


def contract(left_side, right_side, left_dim, right_dim, precision=None):
    return lax.dot_general(
        left_side,
        right_side,
        (((left_dim,), (right_dim,)), ((), ())),
        precision=precision,
        preferred_element_type=jnp.float32,
    )


def identity(size):
    shape = (size, size)
    same = lax.broadcasted_iota(jnp.int32, shape, 0) == lax.broadcasted_iota(jnp.int32, shape, 1)
    return jnp.where(same, 1.0, 0.0).astype(jnp.float32)


def two_stages(size):
    inner = max(k for k in range(1, size + 1) if size % k == 0 and k * k <= size)
    return inner, size // inner


def split(value):
    high = value.astype(jnp.bfloat16)
    return high, (value - high.astype(jnp.float32)).astype(jnp.bfloat16)


def contract_split(left_pair, right_pair, left_dim, right_dim):
    total = contract(left_pair[0], right_pair[0], left_dim, right_dim)
    total = total + contract(left_pair[1], right_pair[0], left_dim, right_dim)
    return total + contract(left_pair[0], right_pair[1], left_dim, right_dim)


def inverse_factor_body(block, ridge, gram_ref, inverse_ref, work, corner):
    size = gram_ref.shape[0]
    work[:, :size] = gram_ref[...] + ridge * identity(size)
    work[:, size:] = identity(size)
    row_in_group = lax.broadcasted_iota(jnp.int32, (SUBLANES, 2 * block), 0)
    for low in range(0, size, block):
        high = low + block
        corner[:, :block] = work[low:high, low:high]
        corner[:, block:] = identity(block)
        groups = [corner[g : g + SUBLANES, :] for g in range(0, block, SUBLANES)]
        for k in range(block):
            own, inside = divmod(k, SUBLANES)
            pivot_row = groups[own][inside : inside + 1, :]
            scaled = pivot_row / pivot_row[:, k : k + 1]
            for g in range(own, len(groups)):
                factor = groups[g][:, k : k + 1]
                change = factor * scaled
                if g == own:
                    change = jnp.where(row_in_group > inside, change, 0.0)
                groups[g] = groups[g] - change
        for g, rows in enumerate(groups):
            corner[g * SUBLANES : (g + 1) * SUBLANES, :] = rows
        pivots = jnp.sum(corner[:, :block] * identity(block), axis=1, keepdims=True)
        corner_inverse = corner[:, block:] * (1.0 / jnp.sqrt(pivots))
        panel = contract(corner_inverse, work[low:high, :], 1, 0, HIGHEST)
        inverse_ref[low:high, :] = panel[:, size:]
        if high < size:
            update = contract(panel[:, :size], panel, 0, 0, HIGHEST)
            work[high:, :] = work[high:, :] - update[high:, :]


def eliminate_four(groups, k, row_in_group, lanes):
    own, inside = divmod(k, SUBLANES)
    rows = [groups[own][inside + j : inside + j + 1, :] for j in range(4)]
    def splat(value, j, sublanes):
        return jnp.broadcast_to(value[:, k + j : k + j + 1], (sublanes, lanes))
    a = [[splat(rows[i], j, 1) for j in range(i + 1)] for i in range(4)]
    i0 = 1.0 / a[0][0]
    i1 = a[0][0] * (1.0 / (a[0][0] * a[1][1] - a[1][0] * a[1][0]))
    l10, l20, l30 = a[1][0] * i0, a[2][0] * i0, a[3][0] * i0
    b21, b31 = a[2][1] - l20 * a[1][0], a[3][1] - l30 * a[1][0]
    l21, l31 = b21 * i1, b31 * i1
    d2 = a[2][2] - l20 * a[2][0] - l21 * b21
    b32 = a[3][2] - l30 * a[2][0] - l31 * b21
    s33 = a[3][3] - l30 * a[3][0] - l31 * b31
    i2 = 1.0 / d2
    i3 = d2 * (1.0 / (d2 * s33 - b32 * b32))
    l32 = b32 * i2
    u0 = rows[0]
    u1 = rows[1] - l10 * u0
    u2 = rows[2] - l20 * u0 - l21 * u1
    u3 = rows[3] - l30 * u0 - l31 * u1 - l32 * u2
    w = [u0 * i0, u1 * i1, u2 * i2, u3 * i3]
    for g in range(own, len(groups)):
        if g == own and inside + 4 == SUBLANES:
            change = None
        else:
            c = [splat(groups[g], j, SUBLANES) for j in range(4)]
            f1 = c[1] - c[0] * l10
            f2 = c[2] - c[0] * l20 - f1 * l21
            f3 = c[3] - c[0] * l30 - f1 * l31 - f2 * l32
            change = (c[0] * w[0] + f1 * w[1]) + (f2 * w[2] + f3 * w[3])
        if g == own:
            value = groups[g]
            if change is not None:
                value = jnp.where(row_in_group > inside + 3, value - change, value)
            for j, u in ((1, u1), (2, u2), (3, u3)):
                value = jnp.where(row_in_group == inside + j, u, value)
            groups[g] = value
        else:
            groups[g] = groups[g] - change


def invert_block(low, block, work, corner, inverse_ref):
    size = work.shape[0]
    high = low + block
    row_in_group = lax.broadcasted_iota(jnp.int32, (SUBLANES, 2 * block), 0)
    corner[:, :block] = work[low:high, low:high]
    corner[:, block:] = identity(block)
    groups = [corner[g : g + SUBLANES, :] for g in range(0, block, SUBLANES)]
    for k in range(0, block, 4):
        eliminate_four(groups, k, row_in_group, 2 * block)
    for g, rows in enumerate(groups):
        corner[g * SUBLANES : (g + 1) * SUBLANES, :] = rows
    pivots = jnp.sum(corner[:, :block] * identity(block), axis=1, keepdims=True)
    corner_inverse = corner[:, block:] * (1.0 / jnp.sqrt(pivots))
    panel = contract(corner_inverse, work[low:high, :], 1, 0, HIGHEST)
    inverse_ref[low:high, :] = panel[:, size:]
    if high < size:
        update = contract(panel[:, :size], panel, 0, 0, HIGHEST)
        work[high:, :] = work[high:, :] - update[high:, :]


def inverse_factor(gram_matrix, ridge):
    size = gram_matrix.shape[0]
    block = min(64, size)
    return pl.pallas_call(
        functools.partial(inverse_factor_body, block, ridge),
        out_shape=jax.ShapeDtypeStruct((size, size), jnp.float32),
        in_specs=[pl.BlockSpec(memory_space=pltpu.VMEM)],
        out_specs=pl.BlockSpec(memory_space=pltpu.VMEM),
        scratch_shapes=[
            pltpu.VMEM((size, 2 * size), jnp.float32),
            pltpu.VMEM((block, 2 * block), jnp.float32),
        ],
        cost_estimate=pl.CostEstimate(flops=20_000_000_000, bytes_accessed=8 * size * size, transcendentals=0),
        name="inverse_factor",
    )(gram_matrix)


def plain_shards(rows_of, cols_of, activations, cotangent, weight, momentum, right_factor):
    dout = momentum.shape[0] * rows_of
    din = momentum.shape[1] * cols_of
    rank = right_factor.shape[1]
    cot_tokens = lax.all_gather(cotangent, "col", axis=0, tiled=True)
    act_tokens = lax.all_gather(activations, "row", axis=0, tiled=True)
    held_part = contract(momentum, right_factor, 1, 0, HIGH)
    act_part = contract(act_tokens.astype(jnp.float32), right_factor, 1, 0, HIGH)
    grad_part = contract(cot_tokens.astype(jnp.float32), act_part, 0, 0, HIGH)
    left_part = (held_part + grad_part) / jnp.sqrt(jnp.float32(din))
    left_piece = lax.psum_scatter(left_part, "col", scatter_dimension=0, tiled=True)
    input_part = jnp.dot(cot_tokens, weight, preferred_element_type=jnp.float32)
    buffer = momentum + contract(cot_tokens, act_tokens, 0, 0, None)
    left_block = lax.all_gather(left_piece, "col", axis=0, tiled=True)
    gram_matrix = lax.psum(contract(left_block, left_block, 0, 0, HIGHEST), "row")
    projected_part = contract(buffer, left_block, 0, 0, HIGH)
    gram_matrix, projected_part = lax.optimization_barrier((gram_matrix, projected_part))
    projected = lax.psum(projected_part, "row")
    projected, input_part = lax.optimization_barrier((projected, input_part))
    input_sums = lax.psum_scatter(input_part, "row", scatter_dimension=0, tiled=True)
    inverse = inverse_factor(gram_matrix, ridge_weight * dout)
    orthonormal = contract(left_block, inverse, 1, 1, HIGHEST)
    right = contract(projected, inverse, 1, 1, HIGHEST)
    squares = lax.psum(jnp.sum(right * right, axis=0), "col")
    momentum_next = buffer - (1.0 - momentum_decay) * contract(orthonormal, right, 1, 1, HIGH)
    right_next = right * lax.rsqrt(squares / din + 1e-06)
    step_scale = jnp.sqrt(jnp.float32(dout) / rank)
    weight_step = (step_scale * contract(orthonormal, right_next, 1, 1, HIGH)).astype(jnp.bfloat16)
    return (input_sums.astype(jnp.bfloat16), momentum_next, right_next, weight_step)


def remote(source, target, send_sem, recv_sem, device):
    return pltpu.make_async_remote_copy(
        src_ref=source,
        dst_ref=target,
        send_sem=send_sem,
        recv_sem=recv_sem,
        device_id=device,
        device_id_type=MESH,
    )


def greet(devices):
    barrier = pltpu.get_barrier_semaphore()
    for device in devices:
        pl.semaphore_signal(barrier, inc=1, device_id=device, device_id_type=MESH)
    pl.semaphore_wait(barrier, len(devices))


def factor_kernel(
    n_row,
    n_col,
    ridge,
    act_ref,
    cot_ref,
    weight_hbm,
    momentum_hbm,
    factor_ref,
    input_ref,
    buffer_hbm,
    orthonormal_hbm,
    right_high_hbm,
    right_low_hbm,
    right_turned_hbm,
    scale_ref,
    act_all,
    cot_all,
    cot_flat,
    cot_turned,
    chunks,
    chunk_high,
    chunk_low,
    weight,
    factor_high,
    factor_low,
    token_send,
    token_recv,
    token_high,
    token_low,
    send_inner,
    recv_inner,
    totals,
    recv_outer,
    left_ref,
    gram_ref,
    projected_ref,
    input_send,
    input_recv,
    gram_in,
    gram_out,
    gram_all,
    proj_in,
    proj_out,
    proj_all,
    inverse,
    diagonal,
    work,
    corner,
    squares_all,
    orthonormal,
    right_high,
    right_low,
    right_turned,
    load_sem,
    store_sem,
    weight_sem,
    act_sem,
    cot_sem,
    token_sem,
    inner_sem,
    chain_sem,
    chain_in_sem,
    gather_send_sem,
    gather_outer_sem,
    gather_inner_sem,
    input_sem,
    gram_in_sem,
    gram_out_sem,
    gram_all_sem,
    proj_in_sem,
    proj_out_sem,
    proj_all_sem,
    squares_sem,
    result_sem,
):
    inner, outer = two_stages(n_col)
    row_inner, row_outer = two_stages(n_row)
    row, col = lax.axis_index("row"), lax.axis_index("col")
    me_in, me_out = lax.rem(col, inner), lax.div(col, inner)
    row_in, row_out = lax.rem(row, row_inner), lax.div(row, row_inner)
    piece, cols = chunks.shape[1], chunks.shape[2]
    halves, width = left_ref.shape[0], left_ref.shape[3]
    rank = halves * width
    din = cols * n_col
    act_rows = act_ref.shape[0]
    tokens = act_rows * n_row
    flip = lax.div(2 * me_out, outer)
    near = me_out + flip * (outer - 1 - 2 * me_out)

    def lanes_of(h):
        return slice(h * width, (h + 1) * width)

    def turned_back(position):
        return position + flip * (outer - 1 - 2 * position)

    def target(k):
        last = k // (outer - 1)
        return turned_back(outer - 1 - k - (k + near + 1) // outer + last * (near + 1))

    def chunk_at(j):
        return target(j % outer) * inner + (me_in + 1 + j // outer) % inner

    def load(q):
        return pltpu.make_async_copy(
            momentum_hbm.at[pl.ds(pl.multiple_of(q * piece, SUBLANES), piece), :], chunks.at[q], load_sem.at[q]
        )

    def store(q):
        return pltpu.make_async_copy(
            chunks.at[q], buffer_hbm.at[pl.ds(pl.multiple_of(q * piece, SUBLANES), piece), :], store_sem.at[q]
        )

    for j in range(n_col):
        load(chunk_at(j)).start()
    weight_copy = pltpu.make_async_copy(weight_hbm, weight, weight_sem)
    weight_copy.start()
    factor_high[...], factor_low[...] = split(factor_ref[...])

    row_peers = [lax.rem(row + d, n_row) for d in range(1, n_row)]
    col_peers = [lax.rem(col + d, n_col) for d in range(1, n_col)]
    greet([(peer, col) for peer in row_peers] + [(row, peer) for peer in col_peers])

    cot_copies = [
        remote(cot_ref, cot_all.at[col], cot_sem.at[0, d], cot_sem.at[1, d], (row, peer))
        for d, peer in enumerate(col_peers)
    ]
    act_copies = [
        remote(act_ref, act_all.at[row], act_sem.at[0, d], act_sem.at[1, d], (peer, col))
        for d, peer in enumerate(row_peers)
    ]
    for copy in cot_copies + act_copies:
        copy.start()
    act_all[row] = act_ref[...]
    cot_all[col] = cot_ref[...]

    def held_part(j):
        q = chunk_at(j)
        load(q).wait()
        return contract_split(split(chunks[q]), (factor_high[...], factor_low[...]), 1, 0)

    def turned_rows(q):
        return cot_turned[pl.ds(pl.multiple_of(q * piece, 2 * SUBLANES), piece), :]

    def token_part(j):
        rows = turned_rows(chunk_at(j))
        return contract(rows, token_high[...], 1, 0) + contract(rows, token_low[...], 1, 0)

    def inner_copy(h, d, k):
        peer = me_out * inner + (me_in + 1 + d) % inner
        return remote(
            send_inner.at[h, d, k],
            recv_inner.at[h, d, k],
            inner_sem.at[0, h, d, k],
            inner_sem.at[1, h, d, k],
            (row, peer),
        )

    def push(d, k):
        value = held_part(d * outer + k)
        for h in range(halves):
            send_inner[h, d, k] = value[:, lanes_of(h)]
        inner_copy(0, d, k).start()

    push(0, 0)
    for copy in act_copies:
        copy.wait()
    acts = act_all[...].reshape(tokens, cols)
    token_send[...] = contract(acts, factor_high[...], 1, 0) + contract(acts, factor_low[...], 1, 0)
    token_copies = [
        remote(
            token_send,
            token_recv.at[d],
            token_sem.at[0, d],
            token_sem.at[1, d],
            (row, me_out * inner + (me_in + 1 + d) % inner),
        )
        for d in range(inner - 1)
    ]
    for copy in token_copies:
        copy.start()
    for d in range(inner - 1):

        def push_next(k, carry, d=d):
            push(d, k)
            return carry

        lax.fori_loop(1 if d == 0 else 0, outer, push_next, 0)
    for h in range(1, halves):
        for d in range(inner - 1):

            def push_half(k, carry, h=h, d=d):
                inner_copy(h, d, k).start()
                return carry

            lax.fori_loop(0, outer, push_half, 0)
    for copy in cot_copies:
        copy.wait()

    def turn(b, carry):
        lanes = pl.ds(pl.multiple_of(b * LANES, LANES), LANES)
        slab = cot_all[:, :, lanes].astype(jnp.float32).reshape(tokens, LANES)
        cot_flat[:, lanes] = slab.astype(jnp.bfloat16)
        cot_turned[lanes, :] = slab.T.astype(jnp.bfloat16)
        return carry

    lax.fori_loop(0, cot_ref.shape[1] // LANES, turn, 0)

    token_sums = token_send[...]
    for d, copy in enumerate(token_copies):
        copy.wait()
        token_sums = token_sums + token_recv[d]
    token_high[...], token_low[...] = split(token_sums)

    def form(q):
        value = chunks[q] + contract(turned_rows(q), act_all[...].reshape(tokens, cols), 1, 0)
        chunks[q] = value
        chunk_high[q], chunk_low[q] = split(value)
        store(q).start()

    def own_part(k):
        j = (inner - 1) * outer + k
        value = held_part(j) + token_part(j)
        for h in range(halves):
            totals[h, k] = value[:, lanes_of(h)]

    def toward(q):
        return 2 * ((q - me_out + outer - 1) // outer) - 1

    def chain_copy(h, k):
        q = target(k)
        up = (q - me_out + outer - 1) // outer
        ending = (outer - (me_out - q)) // (outer - 1) * (1 - up)
        slot = q + ending * (outer - q)
        peer = (me_out + toward(q)) * inner + me_in
        return remote(
            totals.at[h, k], recv_outer.at[h, slot], chain_sem.at[h, k], chain_in_sem.at[h, slot], (row, peer)
        )

    def chain_arrival(h, slot):
        return remote(
            totals.at[h, 0], recv_outer.at[h, slot], chain_sem.at[h, 0], chain_in_sem.at[h, slot], (row, col)
        )

    def add_inner(h, k):
        for d in range(inner - 1):
            inner_copy(h, d, k).wait_recv()
            totals[h, k] = totals[h, k] + recv_inner[h, d, k]

    def chain(h, k):
        add_inner(h, k)
        q = target(k)

        @pl.when(jnp.logical_and(me_out - toward(q) >= 0, me_out - toward(q) < outer))
        def _():
            chain_arrival(h, q).wait_recv()
            totals[h, k] = totals[h, k] + recv_outer[h, q]

        chain_copy(h, k).start()

    def gather_outer(h, q, up):
        piece_ref = left_ref.at[h, q * inner + me_in]
        peer = (me_out + 2 * up - 1) * inner + me_in
        return remote(piece_ref, piece_ref, gather_send_sem.at[h, up, q], gather_outer_sem.at[h, q], (row, peer))

    def gather_inner(h, d, q):
        piece_ref = left_ref.at[h, q * inner + me_in]
        peer = me_out * inner + (me_in + 1 + d) % inner
        return remote(
            piece_ref, piece_ref, gather_inner_sem.at[0, h, d, q], gather_inner_sem.at[1, h, d, q], (row, peer)
        )

    def onward(h, q, start):
        up = 1 - (q - me_out + outer - 1) // outer

        @pl.when(jnp.logical_and(me_out + 2 * up - 1 >= 0, me_out + 2 * up - 1 < outer))
        def _():
            copy = gather_outer(h, q, up)
            copy.start() if start else copy.wait_send()

    def own_outward(h, start):
        for up in range(2):

            @pl.when(jnp.logical_and(me_out + 2 * up - 1 >= 0, me_out + 2 * up - 1 < outer))
            def _():
                copy = gather_outer(h, me_out, up)
                copy.start() if start else copy.wait_send()

    def settle(h):
        add_inner(h, outer - 1)

        @pl.when(me_out > 0)
        def _():
            chain_arrival(h, me_out).wait_recv()
            totals[h, outer - 1] = totals[h, outer - 1] + recv_outer[h, me_out]

        @pl.when(me_out < outer - 1)
        def _():
            chain_arrival(h, outer).wait_recv()
            totals[h, outer - 1] = totals[h, outer - 1] + recv_outer[h, outer]

        left_ref[h, col] = totals[h, outer - 1] / jnp.sqrt(jnp.float32(din))
        own_outward(h, True)
        for d in range(inner - 1):
            gather_inner(h, d, me_out).start()

    def arrival(n):
        paired = (2 * near - n - 1 + 2 * outer) // (2 * outer)
        step = (n // 2 + 1) * (1 - 2 * (n % 2))
        return turned_back(paired * (near + step) + (1 - paired) * (n + 1))

    def forward(h, n):
        q = arrival(n)
        gather_outer(h, q, 0).wait_recv()
        onward(h, q, True)
        for d in range(inner - 1):
            gather_inner(h, d, q).start()

    def absorb(h, q):
        value = left_ref[h, q]
        for g in range(h + 1):
            gram_ref[h, :, lanes_of(g)] = gram_ref[h, :, lanes_of(g)] + contract(value, left_ref[g, q], 0, 0, HIGHEST)
        projected_ref[h] = projected_ref[h] + contract_split(split(value), (chunk_high[q], chunk_low[q]), 0, 0)

    def absorb_outer(h, n):
        absorb(h, arrival(n) * inner + me_in)

    def absorb_inner(h, q):
        for d in range(inner - 1):
            gather_inner(h, d, q).wait_recv()
            absorb(h, q * inner + (me_in - 1 - d + inner) % inner)

    part = width // row_inner
    inner_peers = [lax.rem(row_in + 1 + d, row_inner) for d in range(row_inner - 1)]
    outer_peers = [lax.rem(row_out + 1 + d, row_outer) for d in range(row_outer - 1)]

    def rows_at(index):
        return pl.ds(pl.multiple_of(index * part, SUBLANES), part)

    class RowSum:
        def __init__(self, source, buffer_in, buffer_out, whole, sems, h, span):
            self.source, self.whole, self.h = source, whole, h
            self.buffer_in, self.buffer_out, self.lanes = buffer_in, buffer_out, pl.ds(0, span)
            self.sems = sems

        def view(self, ref, index, rows=None):
            if rows is None:
                return ref.at[self.h, index, :, self.lanes]
            return ref.at[self.h, rows, self.lanes]

        def begin(self):
            sem = self.sems[0]
            self.first = [
                remote(
                    self.view(self.source, None, rows_at(peer)),
                    self.view(self.buffer_in, d),
                    sem.at[0, self.h, d],
                    sem.at[1, self.h, d],
                    (row_out * row_inner + peer, col),
                )
                for d, peer in enumerate(inner_peers)
            ]
            for copy in self.first:
                copy.start()

        def cross(self):
            sem = self.sems[1]
            total = self.source[self.h, rows_at(row_in), self.lanes]
            for d, copy in enumerate(self.first):
                copy.wait()
                total = total + self.buffer_in[self.h, d, :, self.lanes]
            self.buffer_out[self.h, row_out, :, self.lanes] = total
            mine = self.view(self.buffer_out, row_out)
            self.second = [
                remote(mine, mine, sem.at[0, self.h, d], sem.at[1, self.h, d], (peer * row_inner + row_in, col))
                for d, peer in enumerate(outer_peers)
            ]
            for copy in self.second:
                copy.start()

        def spread(self):
            sem = self.sems[2]
            for copy in self.second:
                copy.wait()
            total = self.buffer_out[self.h, 0, :, self.lanes]
            for o in range(1, row_outer):
                total = total + self.buffer_out[self.h, o, :, self.lanes]
            self.whole[self.h, rows_at(row_in), self.lanes] = total
            mine = self.view(self.whole, None, rows_at(row_in))
            self.third = [
                remote(mine, mine, sem.at[0, self.h, d], sem.at[1, self.h, d], (row_out * row_inner + peer, col))
                for d, peer in enumerate(inner_peers)
            ]
            for copy in self.third:
                copy.start()

        def end(self):
            for copy in self.third:
                copy.wait()

    gram_sums = [
        RowSum(gram_ref, gram_in, gram_out, gram_all, (gram_in_sem, gram_out_sem, gram_all_sem), h, (h + 1) * width)
        for h in range(halves)
    ]
    proj_sums = [
        RowSum(projected_ref, proj_in, proj_out, proj_all, (proj_in_sem, proj_out_sem, proj_all_sem), h, cols)
        for h in range(halves)
    ]
    block = corner.shape[0]

    def prepare_half(h):
        known = h * width
        shift = ridge * identity(width)
        gram = gram_all[h, :, known : known + width]
        if h == 0:
            inverse[...] = jnp.zeros_like(inverse)
            rest = None
        else:
            before = inverse[:known, :known]
            solved = contract(before, gram_all[h, :, :known], 1, 1, HIGHEST)
            gram = gram - contract(solved, solved, 0, 0, HIGHEST)
            rest = contract(solved, before, 0, 0, HIGHEST)
        work[:, :width] = gram + shift
        work[:, width:] = identity(width)
        return rest

    def finish_half(h, rest):
        known = h * width
        inverse[known : known + width, known : known + width] = diagonal[...]
        if h > 0:
            inverse[known : known + width, :known] = -contract(diagonal[...], rest, 1, 0, HIGHEST)

    def right_half(h):
        known = (h + 1) * width
        projected = proj_all[: h + 1].reshape(known, cols)
        factor = split(inverse[h * width : known, :known])
        right = contract_split(factor, split(projected), 1, 0)
        right_high[lanes_of(h), :], right_low[lanes_of(h), :] = split(right)
        squares = jnp.sum(right * right, axis=1, keepdims=True)
        squares_all[col, :, lanes_of(h)] = jnp.broadcast_to(squares, (width, LANES)).T[:SUBLANES, :]
        return right

    gram_ref[...] = jnp.zeros_like(gram_ref)
    projected_ref[...] = jnp.zeros_like(projected_ref)

    def open_chain(k, carry):
        own_part(k)
        chain(0, k)
        return carry

    lax.fori_loop(0, outer - 1, open_chain, 0)
    own_part(outer - 1)

    def form_some(q, carry):
        form(q)
        return carry

    lax.fori_loop(0, n_col // 2, form_some, 0)

    @pl.when(near == 0)
    def _():
        chain(1, 0)

    settle(0)
    weight_copy.wait()
    input_part = contract(cot_flat[...], weight[...], 1, 0)
    input_send[...] = input_part.reshape(n_row, act_rows, cols)
    input_copies = [
        remote(input_send.at[peer], input_recv.at[d], input_sem.at[0, d], input_sem.at[1, d], (peer, col))
        for d, peer in enumerate(row_peers)
    ]
    for copy in input_copies:
        copy.start()
    lax.fori_loop(n_col // 2, n_col, form_some, 0)

    def next_chain(k, carry):
        chain(1, k)
        return carry

    def next_forward(n, carry):
        forward(0, n)
        return carry

    def next_both(k, carry):
        chain(1, k)
        forward(0, k - 1)
        return carry

    @pl.when(near == 0)
    def _():
        lax.fori_loop(1, outer - 1, next_chain, 0)
        lax.fori_loop(0, outer - 2, next_forward, 0)

    @pl.when(near > 0)
    def _():
        chain(1, 0)
        lax.fori_loop(1, outer - 1, next_both, 0)

    absorb(0, col)
    settle(1)

    @pl.when(near > 0)
    def _():
        forward(0, outer - 2)


    def absorb_first(n, carry):
        absorb_outer(0, n)
        return carry

    lax.fori_loop(0, outer - 2, absorb_first, 0)
    absorb_inner(0, me_out)
    absorb(1, col)

    @pl.when(near == 0)
    def _():
        forward(0, outer - 2)

    absorb_outer(0, outer - 2)

    def absorb_second(n, carry):
        forward(1, n)
        absorb_inner(0, arrival(n))
        absorb_outer(1, n)
        return carry

    lax.fori_loop(0, outer - 2, absorb_second, 0)
    absorb_inner(0, arrival(outer - 2))
    gram_sums[0].begin()
    proj_sums[0].begin()
    absorb_inner(1, me_out)
    gram_sums[0].cross()
    proj_sums[0].cross()
    forward(1, outer - 2)
    absorb_outer(1, outer - 2)
    absorb_inner(1, arrival(0))
    gram_sums[0].spread()

    def absorb_third(n, carry):
        absorb_inner(1, arrival(n))
        return carry

    lax.fori_loop(1, outer - 1, absorb_third, 0)
    gram_sums[1].begin()
    proj_sums[1].begin()
    gram_sums[0].end()
    gram_sums[1].cross()
    proj_sums[1].cross()
    rest = prepare_half(0)
    for low in range(0, width, block):
        invert_block(low, block, work, corner, diagonal)
        if low == 0:
            gram_sums[1].spread()
            proj_sums[0].spread()
    finish_half(0, rest)
    proj_sums[0].end()
    right_turned_parts = [right_half(0)]
    gram_sums[1].end()
    rest = prepare_half(1)
    for low in range(0, width, block):
        invert_block(low, block, work, corner, diagonal)
        if low == 0:
            proj_sums[1].spread()
    finish_half(1, rest)
    proj_sums[1].end()
    right_turned_parts.append(right_half(1))

    copies = [
        remote(squares_all.at[col], squares_all.at[col], squares_sem.at[0, d], squares_sem.at[1, d], (row, peer))
        for d, peer in enumerate(col_peers)
    ]
    for copy in copies:
        copy.start()

    for h in range(halves):
        right_turned[:, lanes_of(h)] = right_turned_parts[h].T

    def result(q):
        return pltpu.make_async_copy(orthonormal.at[q], orthonormal_hbm.at[q], result_sem.at[q])

    right_copies = [
        pltpu.make_async_copy(right_high, right_high_hbm, result_sem.at[n_col]),
        pltpu.make_async_copy(right_low, right_low_hbm, result_sem.at[n_col + 1]),
        pltpu.make_async_copy(right_turned, right_turned_hbm, result_sem.at[n_col + 2]),
    ]
    for copy in right_copies:
        copy.start()

    def orthonormalise(q, carry):
        total = contract_split(split(left_ref[0, q]), split(inverse[:, :width]), 1, 1)
        for h in range(1, halves):
            total = total + contract_split(split(left_ref[h, q]), split(inverse[:, lanes_of(h)]), 1, 1)
        orthonormal[q] = total
        result(q).start()
        return carry

    lax.fori_loop(0, n_col, orthonormalise, 0)
    total = input_send[row]
    for d, copy in enumerate(input_copies):
        copy.wait()
        total = total + input_recv[d]
    input_ref[...] = total.astype(jnp.bfloat16)
    for q in range(n_col):
        store(q).wait()

    for h in range(halves):

        def drain(k, carry, h=h):
            for d in range(inner - 1):
                inner_copy(h, d, k).wait_send()
                gather_inner(h, d, k).wait_send()
            return carry

        lax.fori_loop(0, outer, drain, 0)

        def drain_chain(k, carry, h=h):
            chain_copy(h, k).wait_send()
            onward(h, arrival(k), False)
            return carry

        lax.fori_loop(0, outer - 1, drain_chain, 0)
        own_outward(h, False)

    for copy in copies:
        copy.wait()
    total = squares_all[0]
    for q in range(1, n_col):
        total = total + squares_all[q]
    scale_ref[...] = lax.rsqrt(total / din + 1e-06)
    for copy in right_copies:
        copy.wait()
    for q in range(n_col):
        result(q).wait()


def factor_call(n_row, n_col, ridge, activations, cotangent, weight, momentum, right_factor):
    inner, outer = two_stages(n_col)
    row_inner, row_outer = two_stages(n_row)
    rows, cols = momentum.shape
    rank = right_factor.shape[1]
    halves, width = 2, rank // 2
    piece = rows // n_col
    part = width // row_inner
    block = min(64, width)
    act_rows, cot_rows = activations.shape[0], cotangent.shape[0]
    tokens = act_rows * n_row
    f32, bf16 = jnp.float32, jnp.bfloat16
    vmem = pl.BlockSpec(memory_space=pltpu.VMEM)
    hbm = pl.BlockSpec(memory_space=pl.ANY)
    dma = pltpu.SemaphoreType.DMA
    return pl.pallas_call(
        functools.partial(factor_kernel, n_row, n_col, ridge),
        out_shape=(
            jax.ShapeDtypeStruct((act_rows, cols), bf16),
            jax.ShapeDtypeStruct((rows, cols), f32),
            jax.ShapeDtypeStruct((n_col, piece, rank), f32),
            jax.ShapeDtypeStruct((rank, cols), bf16),
            jax.ShapeDtypeStruct((rank, cols), bf16),
            jax.ShapeDtypeStruct((cols, rank), f32),
            jax.ShapeDtypeStruct((SUBLANES, rank), f32),
        ),
        in_specs=[vmem, vmem, hbm, hbm, vmem],
        out_specs=(vmem, hbm, hbm, hbm, hbm, hbm, vmem),
        scratch_shapes=[
            pltpu.VMEM((n_row, act_rows, cols), bf16),
            pltpu.VMEM((n_col, cot_rows, rows), bf16),
            pltpu.VMEM((tokens, rows), bf16),
            pltpu.VMEM((rows, tokens), bf16),
            pltpu.VMEM((n_col, piece, cols), f32),
            pltpu.VMEM((n_col, piece, cols), bf16),
            pltpu.VMEM((n_col, piece, cols), bf16),
            pltpu.VMEM((rows, cols), bf16),
            pltpu.VMEM((cols, rank), bf16),
            pltpu.VMEM((cols, rank), bf16),
            pltpu.VMEM((tokens, rank), f32),
            pltpu.VMEM((inner - 1, tokens, rank), f32),
            pltpu.VMEM((tokens, rank), bf16),
            pltpu.VMEM((tokens, rank), bf16),
            pltpu.VMEM((halves, inner - 1, outer, piece, width), f32),
            pltpu.VMEM((halves, inner - 1, outer, piece, width), f32),
            pltpu.VMEM((halves, outer, piece, width), f32),
            pltpu.VMEM((halves, outer + 1, piece, width), f32),
            pltpu.VMEM((halves, n_col, piece, width), f32),
            pltpu.VMEM((halves, width, rank), f32),
            pltpu.VMEM((halves, width, cols), f32),
            pltpu.VMEM((n_row, act_rows, cols), f32),
            pltpu.VMEM((n_row - 1, act_rows, cols), f32),
            pltpu.VMEM((halves, row_inner - 1, part, rank), f32),
            pltpu.VMEM((halves, row_outer, part, rank), f32),
            pltpu.VMEM((halves, width, rank), f32),
            pltpu.VMEM((halves, row_inner - 1, part, cols), f32),
            pltpu.VMEM((halves, row_outer, part, cols), f32),
            pltpu.VMEM((halves, width, cols), f32),
            pltpu.VMEM((rank, rank), f32),
            pltpu.VMEM((width, width), f32),
            pltpu.VMEM((width, 2 * width), f32),
            pltpu.VMEM((block, 2 * block), f32),
            pltpu.VMEM((n_col, SUBLANES, rank), f32),
            pltpu.VMEM((n_col, piece, rank), f32),
            pltpu.VMEM((rank, cols), bf16),
            pltpu.VMEM((rank, cols), bf16),
            pltpu.VMEM((cols, rank), f32),
            dma((n_col,)),
            dma((n_col,)),
            dma,
            dma((2, n_row - 1)),
            dma((2, n_col - 1)),
            dma((2, inner - 1)),
            dma((2, halves, inner - 1, outer)),
            dma((halves, outer)),
            dma((halves, outer + 1)),
            dma((halves, 2, outer)),
            dma((halves, outer)),
            dma((2, halves, inner - 1, outer)),
            dma((2, n_row - 1)),
            dma((2, halves, row_inner - 1)),
            dma((2, halves, row_outer - 1)),
            dma((2, halves, row_inner - 1)),
            dma((2, halves, row_inner - 1)),
            dma((2, halves, row_outer - 1)),
            dma((2, halves, row_inner - 1)),
            dma((2, n_col - 1)),
            dma((n_col + 3,)),
        ],
        compiler_params=pltpu.CompilerParams(
            collective_id=1, has_side_effects=True, vmem_limit_bytes=60 * 1024 * 1024
        ),
        name="factors",
    )(activations, cotangent, weight, momentum, right_factor)


def output_kernel(
    step_scale,
    buffer_ref,
    orthonormal_ref,
    right_high_ref,
    right_low_ref,
    right_turned_ref,
    scale_ref,
    sums_ref,
    momentum_ref,
    step_ref,
    next_ref,
    input_ref,
):
    input_ref[...] = sums_ref[...]
    right = jnp.concatenate([right_high_ref[...], right_high_ref[...], right_low_ref[...]], axis=0)

    def product(value):
        high, low = split(value)
        return contract(jnp.concatenate([high, low, high], axis=1), right, 1, 0)

    orthonormal = orthonormal_ref[...]
    momentum_ref[...] = buffer_ref[...] - (1.0 - momentum_decay) * product(orthonormal)
    step_ref[...] = (step_scale * product(orthonormal * scale_ref[:1, :])).astype(jnp.bfloat16)
    next_ref[...] = right_turned_ref[...] * scale_ref[:1, :]


def output_tile(rows, cols):
    fits = [t for t in range(16, min(rows // 4, 576) + 1, 16) if rows % t == 0 and cols % (rows // t * SUBLANES) == 0]
    return max(fits, default=0)


def output_call(step_scale, buffer, orthonormal, right_high, right_low, right_turned, scale, sums):
    rows, cols = buffer.shape
    rank = right_high.shape[0]
    tile = output_tile(rows, cols)
    steps = rows // tile
    f32 = jnp.float32
    whole = pl.BlockSpec((rank, cols), lambda i: (0, 0))
    return pl.pallas_call(
        functools.partial(output_kernel, step_scale),
        grid=(steps,),
        out_shape=(
            jax.ShapeDtypeStruct((rows, cols), f32),
            jax.ShapeDtypeStruct((rows, cols), jnp.bfloat16),
            jax.ShapeDtypeStruct((cols, rank), f32),
            jax.ShapeDtypeStruct(sums.shape, sums.dtype),
        ),
        in_specs=[
            pl.BlockSpec((tile, cols), lambda i: (i, 0)),
            pl.BlockSpec((tile, rank), lambda i: (i, 0)),
            whole,
            whole,
            pl.BlockSpec((cols // steps, rank), lambda i: (i, 0)),
            pl.BlockSpec(scale.shape, lambda i: (0, 0)),
            pl.BlockSpec(sums.shape, lambda i: (0, 0)),
        ],
        out_specs=(
            pl.BlockSpec((tile, cols), lambda i: (i, 0)),
            pl.BlockSpec((tile, cols), lambda i: (i, 0)),
            pl.BlockSpec((cols // steps, rank), lambda i: (i, 0)),
            pl.BlockSpec(sums.shape, lambda i: (0, 0)),
        ),
        compiler_params=pltpu.CompilerParams(
            dimension_semantics=("arbitrary",), vmem_limit_bytes=60 * 1024 * 1024
        ),
        name="outputs",
    )(buffer, orthonormal, right_high, right_low, right_turned, scale, sums)


def kernel_shards(n_row, n_col, activations, cotangent, weight, momentum, right_factor):
    rows, cols = momentum.shape
    rank = right_factor.shape[1]
    dout = rows * n_row
    input_sums, buffer, orthonormal, right_high, right_low, right_turned, scale = factor_call(
        n_row, n_col, ridge_weight * dout, activations, cotangent, weight, momentum, right_factor
    )
    step_scale = (dout / rank) ** 0.5
    momentum_next, weight_step, right_next, input_grad = output_call(
        step_scale, buffer, orthonormal.reshape(rows, rank), right_high, right_low, right_turned, scale, input_sums
    )
    return input_grad, momentum_next, right_next, weight_step


def shards(n_row, n_col, activations, cotangent, weight, momentum, right_factor):
    rows, cols = momentum.shape
    rank = right_factor.shape[1]
    aligned = (
        rows % (n_col * 2 * SUBLANES) == 0
        and rows % LANES == 0
        and cols % LANES == 0
        and rank % (2 * LANES) == 0
        and output_tile(rows, cols) > 0
        and activations.shape[0] % (2 * SUBLANES) == 0
        and cotangent.shape[0] % SUBLANES == 0
        and two_stages(n_row)[0] > 1
        and two_stages(n_col)[0] > 1
        and n_col % 2 == 0
        and rank % (2 * two_stages(n_row)[0] * SUBLANES) == 0
    )
    chosen = kernel_shards if aligned else plain_shards
    return chosen(n_row, n_col, activations, cotangent, weight, momentum, right_factor)


def solution(mesh):
    placed = (P("row", "col"), P("col", "row"), P("row", "col"), P("row", "col"), P("col", None))
    return jax.shard_map(
        functools.partial(shards, mesh.shape["row"], mesh.shape["col"]),
        mesh=mesh,
        in_specs=placed,
        out_specs=(P("row", "col"), P("row", "col"), P("col", None), P("row", "col")),
        check_vma=False,
    )
```

```python
import functools

import jax
import jax.numpy as jnp
from jax import lax
from jax.experimental import pallas as pl
from jax.experimental.pallas import tpu as pltpu
from jax.sharding import PartitionSpec as P

momentum_decay = 0.6
ridge_weight = 0.001

HIGHEST = lax.Precision.HIGHEST
HIGH = lax.Precision.HIGH
SUBLANES = 8
LANES = 128
MESH = pl.DeviceIdType.MESH


def contract(left_side, right_side, left_dim, right_dim, precision=None):
    return lax.dot_general(
        left_side,
        right_side,
        (((left_dim,), (right_dim,)), ((), ())),
        precision=precision,
        preferred_element_type=jnp.float32,
    )


def identity(size):
    shape = (size, size)
    same = lax.broadcasted_iota(jnp.int32, shape, 0) == lax.broadcasted_iota(jnp.int32, shape, 1)
    return jnp.where(same, 1.0, 0.0).astype(jnp.float32)


def two_stages(size):
    inner = max(k for k in range(1, size + 1) if size % k == 0 and k * k <= size)
    return inner, size // inner


def split(value):
    high = value.astype(jnp.bfloat16)
    return high, (value - high.astype(jnp.float32)).astype(jnp.bfloat16)


def contract_split(left_pair, right_pair, left_dim, right_dim):
    total = contract(left_pair[0], right_pair[0], left_dim, right_dim)
    total = total + contract(left_pair[1], right_pair[0], left_dim, right_dim)
    return total + contract(left_pair[0], right_pair[1], left_dim, right_dim)


def inverse_factor_body(block, ridge, gram_ref, inverse_ref, work, corner):
    size = gram_ref.shape[0]
    work[:, :size] = gram_ref[...] + ridge * identity(size)
    work[:, size:] = identity(size)
    row_in_group = lax.broadcasted_iota(jnp.int32, (SUBLANES, 2 * block), 0)
    for low in range(0, size, block):
        high = low + block
        corner[:, :block] = work[low:high, low:high]
        corner[:, block:] = identity(block)
        groups = [corner[g : g + SUBLANES, :] for g in range(0, block, SUBLANES)]
        for k in range(block):
            own, inside = divmod(k, SUBLANES)
            pivot_row = groups[own][inside : inside + 1, :]
            scaled = pivot_row / pivot_row[:, k : k + 1]
            for g in range(own, len(groups)):
                factor = groups[g][:, k : k + 1]
                change = factor * scaled
                if g == own:
                    change = jnp.where(row_in_group > inside, change, 0.0)
                groups[g] = groups[g] - change
        for g, rows in enumerate(groups):
            corner[g * SUBLANES : (g + 1) * SUBLANES, :] = rows
        pivots = jnp.sum(corner[:, :block] * identity(block), axis=1, keepdims=True)
        corner_inverse = corner[:, block:] * (1.0 / jnp.sqrt(pivots))
        panel = contract(corner_inverse, work[low:high, :], 1, 0, HIGHEST)
        inverse_ref[low:high, :] = panel[:, size:]
        if high < size:
            update = contract(panel[:, :size], panel, 0, 0, HIGHEST)
            work[high:, :] = work[high:, :] - update[high:, :]


def eliminate_four(groups, k, row_in_group, lanes):
    own, inside = divmod(k, SUBLANES)
    rows = [groups[own][inside + j : inside + j + 1, :] for j in range(4)]
    def splat(value, j, sublanes):
        return jnp.broadcast_to(value[:, k + j : k + j + 1], (sublanes, lanes))
    a = [[splat(rows[i], j, 1) for j in range(i + 1)] for i in range(4)]
    i0 = 1.0 / a[0][0]
    i1 = a[0][0] * (1.0 / (a[0][0] * a[1][1] - a[1][0] * a[1][0]))
    l10, l20, l30 = a[1][0] * i0, a[2][0] * i0, a[3][0] * i0
    b21, b31 = a[2][1] - l20 * a[1][0], a[3][1] - l30 * a[1][0]
    l21, l31 = b21 * i1, b31 * i1
    d2 = a[2][2] - l20 * a[2][0] - l21 * b21
    b32 = a[3][2] - l30 * a[2][0] - l31 * b21
    s33 = a[3][3] - l30 * a[3][0] - l31 * b31
    i2 = 1.0 / d2
    i3 = d2 * (1.0 / (d2 * s33 - b32 * b32))
    l32 = b32 * i2
    u0 = rows[0]
    u1 = rows[1] - l10 * u0
    u2 = rows[2] - l20 * u0 - l21 * u1
    u3 = rows[3] - l30 * u0 - l31 * u1 - l32 * u2
    w = [u0 * i0, u1 * i1, u2 * i2, u3 * i3]
    for g in range(own, len(groups)):
        if g == own and inside + 4 == SUBLANES:
            change = None
        else:
            c = [splat(groups[g], j, SUBLANES) for j in range(4)]
            f1 = c[1] - c[0] * l10
            f2 = c[2] - c[0] * l20 - f1 * l21
            f3 = c[3] - c[0] * l30 - f1 * l31 - f2 * l32
            change = (c[0] * w[0] + f1 * w[1]) + (f2 * w[2] + f3 * w[3])
        if g == own:
            value = groups[g]
            if change is not None:
                value = jnp.where(row_in_group > inside + 3, value - change, value)
            for j, u in ((1, u1), (2, u2), (3, u3)):
                value = jnp.where(row_in_group == inside + j, u, value)
            groups[g] = value
        else:
            groups[g] = groups[g] - change


def invert_block(low, block, work, corner, inverse_ref):
    size = work.shape[0]
    high = low + block
    row_in_group = lax.broadcasted_iota(jnp.int32, (SUBLANES, 2 * block), 0)
    corner[:, :block] = work[low:high, low:high]
    corner[:, block:] = identity(block)
    groups = [corner[g : g + SUBLANES, :] for g in range(0, block, SUBLANES)]
    for k in range(0, block, 4):
        eliminate_four(groups, k, row_in_group, 2 * block)
    for g, rows in enumerate(groups):
        corner[g * SUBLANES : (g + 1) * SUBLANES, :] = rows
    pivots = jnp.sum(corner[:, :block] * identity(block), axis=1, keepdims=True)
    corner_inverse = corner[:, block:] * (1.0 / jnp.sqrt(pivots))
    panel = contract(corner_inverse, work[low:high, :], 1, 0, HIGHEST)
    inverse_ref[low:high, :] = panel[:, size:]
    if high < size:
        update = contract(panel[:, :size], panel, 0, 0, HIGHEST)
        work[high:, :] = work[high:, :] - update[high:, :]


def inverse_factor(gram_matrix, ridge):
    size = gram_matrix.shape[0]
    block = min(64, size)
    return pl.pallas_call(
        functools.partial(inverse_factor_body, block, ridge),
        out_shape=jax.ShapeDtypeStruct((size, size), jnp.float32),
        in_specs=[pl.BlockSpec(memory_space=pltpu.VMEM)],
        out_specs=pl.BlockSpec(memory_space=pltpu.VMEM),
        scratch_shapes=[
            pltpu.VMEM((size, 2 * size), jnp.float32),
            pltpu.VMEM((block, 2 * block), jnp.float32),
        ],
        cost_estimate=pl.CostEstimate(flops=20_000_000_000, bytes_accessed=8 * size * size, transcendentals=0),
        name="inverse_factor",
    )(gram_matrix)


def plain_shards(rows_of, cols_of, activations, cotangent, weight, momentum, right_factor):
    dout = momentum.shape[0] * rows_of
    din = momentum.shape[1] * cols_of
    rank = right_factor.shape[1]
    cot_tokens = lax.all_gather(cotangent, "col", axis=0, tiled=True)
    act_tokens = lax.all_gather(activations, "row", axis=0, tiled=True)
    held_part = contract(momentum, right_factor, 1, 0, HIGH)
    act_part = contract(act_tokens.astype(jnp.float32), right_factor, 1, 0, HIGH)
    grad_part = contract(cot_tokens.astype(jnp.float32), act_part, 0, 0, HIGH)
    left_part = (held_part + grad_part) / jnp.sqrt(jnp.float32(din))
    left_piece = lax.psum_scatter(left_part, "col", scatter_dimension=0, tiled=True)
    input_part = jnp.dot(cot_tokens, weight, preferred_element_type=jnp.float32)
    buffer = momentum + contract(cot_tokens, act_tokens, 0, 0, None)
    left_block = lax.all_gather(left_piece, "col", axis=0, tiled=True)
    gram_matrix = lax.psum(contract(left_block, left_block, 0, 0, HIGHEST), "row")
    projected_part = contract(buffer, left_block, 0, 0, HIGH)
    gram_matrix, projected_part = lax.optimization_barrier((gram_matrix, projected_part))
    projected = lax.psum(projected_part, "row")
    projected, input_part = lax.optimization_barrier((projected, input_part))
    input_sums = lax.psum_scatter(input_part, "row", scatter_dimension=0, tiled=True)
    inverse = inverse_factor(gram_matrix, ridge_weight * dout)
    orthonormal = contract(left_block, inverse, 1, 1, HIGHEST)
    right = contract(projected, inverse, 1, 1, HIGHEST)
    squares = lax.psum(jnp.sum(right * right, axis=0), "col")
    momentum_next = buffer - (1.0 - momentum_decay) * contract(orthonormal, right, 1, 1, HIGH)
    right_next = right * lax.rsqrt(squares / din + 1e-06)
    step_scale = jnp.sqrt(jnp.float32(dout) / rank)
    weight_step = (step_scale * contract(orthonormal, right_next, 1, 1, HIGH)).astype(jnp.bfloat16)
    return (input_sums.astype(jnp.bfloat16), momentum_next, right_next, weight_step)


def remote(source, target, send_sem, recv_sem, device):
    return pltpu.make_async_remote_copy(
        src_ref=source,
        dst_ref=target,
        send_sem=send_sem,
        recv_sem=recv_sem,
        device_id=device,
        device_id_type=MESH,
    )


def greet(devices):
    barrier = pltpu.get_barrier_semaphore()
    for device in devices:
        pl.semaphore_signal(barrier, inc=1, device_id=device, device_id_type=MESH)
    pl.semaphore_wait(barrier, len(devices))


def factor_kernel(
    n_row,
    n_col,
    ridge,
    act_ref,
    cot_ref,
    weight_hbm,
    momentum_hbm,
    factor_ref,
    input_ref,
    buffer_hbm,
    orthonormal_hbm,
    right_high_hbm,
    right_low_hbm,
    right_turned_hbm,
    scale_ref,
    act_all,
    cot_all,
    cot_flat,
    cot_turned,
    chunks,
    chunk_high,
    chunk_low,
    weight,
    factor_high,
    factor_low,
    token_send,
    token_recv,
    token_high,
    token_low,
    send_inner,
    recv_inner,
    totals,
    recv_outer,
    left_ref,
    gram_ref,
    projected_ref,
    input_send,
    input_recv,
    gram_in,
    gram_out,
    gram_all,
    proj_in,
    proj_out,
    proj_all,
    inverse,
    diagonal,
    work,
    corner,
    squares_all,
    orthonormal,
    right_high,
    right_low,
    right_turned,
    load_sem,
    store_sem,
    weight_sem,
    act_sem,
    cot_sem,
    token_sem,
    inner_sem,
    chain_sem,
    chain_in_sem,
    gather_send_sem,
    gather_outer_sem,
    gather_inner_sem,
    input_sem,
    gram_in_sem,
    gram_out_sem,
    gram_all_sem,
    proj_in_sem,
    proj_out_sem,
    proj_all_sem,
    squares_sem,
    result_sem,
):
    inner, outer = two_stages(n_col)
    row_inner, row_outer = two_stages(n_row)
    row, col = lax.axis_index("row"), lax.axis_index("col")
    me_in, me_out = lax.rem(col, inner), lax.div(col, inner)
    row_in, row_out = lax.rem(row, row_inner), lax.div(row, row_inner)
    piece, cols = chunks.shape[1], chunks.shape[2]
    halves, width = left_ref.shape[0], left_ref.shape[3]
    rank = halves * width
    din = cols * n_col
    act_rows = act_ref.shape[0]
    tokens = act_rows * n_row
    flip = lax.div(2 * me_out, outer)
    near = me_out + flip * (outer - 1 - 2 * me_out)

    def lanes_of(h):
        return slice(h * width, (h + 1) * width)

    def turned_back(position):
        return position + flip * (outer - 1 - 2 * position)

    def target(k):
        last = k // (outer - 1)
        return turned_back(outer - 1 - k - (k + near + 1) // outer + last * (near + 1))

    def chunk_at(j):
        return target(j % outer) * inner + (me_in + 1 + j // outer) % inner

    def load(q):
        return pltpu.make_async_copy(
            momentum_hbm.at[pl.ds(pl.multiple_of(q * piece, SUBLANES), piece), :], chunks.at[q], load_sem.at[q]
        )

    def store(q):
        return pltpu.make_async_copy(
            chunks.at[q], buffer_hbm.at[pl.ds(pl.multiple_of(q * piece, SUBLANES), piece), :], store_sem.at[q]
        )

    for j in range(n_col):
        load(chunk_at(j)).start()
    weight_copy = pltpu.make_async_copy(weight_hbm, weight, weight_sem)
    weight_copy.start()
    factor_high[...], factor_low[...] = split(factor_ref[...])

    row_peers = [lax.rem(row + d, n_row) for d in range(1, n_row)]
    col_peers = [lax.rem(col + d, n_col) for d in range(1, n_col)]
    greet([(peer, col) for peer in row_peers] + [(row, peer) for peer in col_peers])

    cot_copies = [
        remote(cot_ref, cot_all.at[col], cot_sem.at[0, d], cot_sem.at[1, d], (row, peer))
        for d, peer in enumerate(col_peers)
    ]
    act_copies = [
        remote(act_ref, act_all.at[row], act_sem.at[0, d], act_sem.at[1, d], (peer, col))
        for d, peer in enumerate(row_peers)
    ]
    for copy in cot_copies + act_copies:
        copy.start()
    act_all[row] = act_ref[...]
    cot_all[col] = cot_ref[...]

    def held_part(j):
        q = chunk_at(j)
        load(q).wait()
        return contract_split(split(chunks[q]), (factor_high[...], factor_low[...]), 1, 0)

    def turned_rows(q):
        return cot_turned[pl.ds(pl.multiple_of(q * piece, 2 * SUBLANES), piece), :]

    def token_part(j):
        rows = turned_rows(chunk_at(j))
        return contract(rows, token_high[...], 1, 0) + contract(rows, token_low[...], 1, 0)

    def inner_copy(h, d, k):
        peer = me_out * inner + (me_in + 1 + d) % inner
        return remote(
            send_inner.at[h, d, k],
            recv_inner.at[h, d, k],
            inner_sem.at[0, h, d, k],
            inner_sem.at[1, h, d, k],
            (row, peer),
        )

    def push(d, k):
        value = held_part(d * outer + k)
        for h in range(halves):
            send_inner[h, d, k] = value[:, lanes_of(h)]
        inner_copy(0, d, k).start()

    push(0, 0)
    for copy in act_copies:
        copy.wait()
    acts = act_all[...].reshape(tokens, cols)
    token_send[...] = contract(acts, factor_high[...], 1, 0) + contract(acts, factor_low[...], 1, 0)
    token_copies = [
        remote(
            token_send,
            token_recv.at[d],
            token_sem.at[0, d],
            token_sem.at[1, d],
            (row, me_out * inner + (me_in + 1 + d) % inner),
        )
        for d in range(inner - 1)
    ]
    for copy in token_copies:
        copy.start()
    for d in range(inner - 1):

        def push_next(k, carry, d=d):
            push(d, k)
            return carry

        lax.fori_loop(1 if d == 0 else 0, outer, push_next, 0)
    for h in range(1, halves):
        for d in range(inner - 1):

            def push_half(k, carry, h=h, d=d):
                inner_copy(h, d, k).start()
                return carry

            lax.fori_loop(0, outer, push_half, 0)
    for copy in cot_copies:
        copy.wait()

    def turn(b, carry):
        lanes = pl.ds(pl.multiple_of(b * LANES, LANES), LANES)
        slab = cot_all[:, :, lanes].astype(jnp.float32).reshape(tokens, LANES)
        cot_flat[:, lanes] = slab.astype(jnp.bfloat16)
        cot_turned[lanes, :] = slab.T.astype(jnp.bfloat16)
        return carry

    lax.fori_loop(0, cot_ref.shape[1] // LANES, turn, 0)

    token_sums = token_send[...]
    for d, copy in enumerate(token_copies):
        copy.wait()
        token_sums = token_sums + token_recv[d]
    token_high[...], token_low[...] = split(token_sums)

    def form(q):
        value = chunks[q] + contract(turned_rows(q), act_all[...].reshape(tokens, cols), 1, 0)
        chunks[q] = value
        chunk_high[q], chunk_low[q] = split(value)
        store(q).start()

    def own_part(k):
        j = (inner - 1) * outer + k
        value = held_part(j) + token_part(j)
        for h in range(halves):
            totals[h, k] = value[:, lanes_of(h)]

    def toward(q):
        return 2 * ((q - me_out + outer - 1) // outer) - 1

    def chain_copy(h, k):
        q = target(k)
        up = (q - me_out + outer - 1) // outer
        ending = (outer - (me_out - q)) // (outer - 1) * (1 - up)
        slot = q + ending * (outer - q)
        peer = (me_out + toward(q)) * inner + me_in
        return remote(
            totals.at[h, k], recv_outer.at[h, slot], chain_sem.at[h, k], chain_in_sem.at[h, slot], (row, peer)
        )

    def chain_arrival(h, slot):
        return remote(
            totals.at[h, 0], recv_outer.at[h, slot], chain_sem.at[h, 0], chain_in_sem.at[h, slot], (row, col)
        )

    def add_inner(h, k):
        for d in range(inner - 1):
            inner_copy(h, d, k).wait_recv()
            totals[h, k] = totals[h, k] + recv_inner[h, d, k]

    def chain(h, k):
        add_inner(h, k)
        q = target(k)

        @pl.when(jnp.logical_and(me_out - toward(q) >= 0, me_out - toward(q) < outer))
        def _():
            chain_arrival(h, q).wait_recv()
            totals[h, k] = totals[h, k] + recv_outer[h, q]

        chain_copy(h, k).start()

    def gather_outer(h, q, up):
        piece_ref = left_ref.at[h, q * inner + me_in]
        peer = (me_out + 2 * up - 1) * inner + me_in
        return remote(piece_ref, piece_ref, gather_send_sem.at[h, up, q], gather_outer_sem.at[h, q], (row, peer))

    def gather_inner(h, d, q):
        piece_ref = left_ref.at[h, q * inner + me_in]
        peer = me_out * inner + (me_in + 1 + d) % inner
        return remote(
            piece_ref, piece_ref, gather_inner_sem.at[0, h, d, q], gather_inner_sem.at[1, h, d, q], (row, peer)
        )

    def onward(h, q, start):
        up = 1 - (q - me_out + outer - 1) // outer

        @pl.when(jnp.logical_and(me_out + 2 * up - 1 >= 0, me_out + 2 * up - 1 < outer))
        def _():
            copy = gather_outer(h, q, up)
            copy.start() if start else copy.wait_send()

    def own_outward(h, start):
        for up in range(2):

            @pl.when(jnp.logical_and(me_out + 2 * up - 1 >= 0, me_out + 2 * up - 1 < outer))
            def _():
                copy = gather_outer(h, me_out, up)
                copy.start() if start else copy.wait_send()

    def settle(h):
        add_inner(h, outer - 1)

        @pl.when(me_out > 0)
        def _():
            chain_arrival(h, me_out).wait_recv()
            totals[h, outer - 1] = totals[h, outer - 1] + recv_outer[h, me_out]

        @pl.when(me_out < outer - 1)
        def _():
            chain_arrival(h, outer).wait_recv()
            totals[h, outer - 1] = totals[h, outer - 1] + recv_outer[h, outer]

        left_ref[h, col] = totals[h, outer - 1] / jnp.sqrt(jnp.float32(din))
        own_outward(h, True)
        for d in range(inner - 1):
            gather_inner(h, d, me_out).start()

    def arrival(n):
        paired = (2 * near - n - 1 + 2 * outer) // (2 * outer)
        step = (n // 2 + 1) * (1 - 2 * (n % 2))
        return turned_back(paired * (near + step) + (1 - paired) * (n + 1))

    def forward(h, n):
        q = arrival(n)
        piece_ref = left_ref.at[h, q * inner + me_in]
        remote(
            piece_ref, piece_ref, gather_send_sem.at[h, 0, q], gather_outer_sem.at[h, q], (row, col)
        ).wait_recv()
        onward(h, q, True)
        for d in range(inner - 1):
            gather_inner(h, d, q).start()

    def absorb(h, q):
        value = left_ref[h, q]
        for g in range(h + 1):
            gram_ref[h, :, lanes_of(g)] = gram_ref[h, :, lanes_of(g)] + contract(value, left_ref[g, q], 0, 0, HIGHEST)
        projected_ref[h] = projected_ref[h] + contract_split(split(value), (chunk_high[q], chunk_low[q]), 0, 0)

    def absorb_outer(h, n):
        absorb(h, arrival(n) * inner + me_in)

    def absorb_inner(h, q):
        for d in range(inner - 1):
            gather_inner(h, d, q).wait_recv()
            absorb(h, q * inner + (me_in - 1 - d + inner) % inner)

    part = width // row_inner
    inner_peers = [lax.rem(row_in + 1 + d, row_inner) for d in range(row_inner - 1)]
    outer_peers = [lax.rem(row_out + 1 + d, row_outer) for d in range(row_outer - 1)]

    def rows_at(index):
        return pl.ds(pl.multiple_of(index * part, SUBLANES), part)

    class RowSum:
        def __init__(self, source, buffer_in, buffer_out, whole, sems, h, span):
            self.source, self.whole, self.h = source, whole, h
            self.buffer_in, self.buffer_out, self.lanes = buffer_in, buffer_out, pl.ds(0, span)
            self.sems = sems

        def view(self, ref, index, rows=None):
            if rows is None:
                return ref.at[self.h, index, :, self.lanes]
            return ref.at[self.h, rows, self.lanes]

        def begin(self):
            sem = self.sems[0]
            self.first = [
                remote(
                    self.view(self.source, None, rows_at(peer)),
                    self.view(self.buffer_in, d),
                    sem.at[0, self.h, d],
                    sem.at[1, self.h, d],
                    (row_out * row_inner + peer, col),
                )
                for d, peer in enumerate(inner_peers)
            ]
            for copy in self.first:
                copy.start()

        def cross(self):
            sem = self.sems[1]
            total = self.source[self.h, rows_at(row_in), self.lanes]
            for d, copy in enumerate(self.first):
                copy.wait()
                total = total + self.buffer_in[self.h, d, :, self.lanes]
            self.buffer_out[self.h, row_out, :, self.lanes] = total
            mine = self.view(self.buffer_out, row_out)
            self.second = [
                remote(mine, mine, sem.at[0, self.h, d], sem.at[1, self.h, d], (peer * row_inner + row_in, col))
                for d, peer in enumerate(outer_peers)
            ]
            for copy in self.second:
                copy.start()

        def spread(self):
            sem = self.sems[2]
            for copy in self.second:
                copy.wait()
            total = self.buffer_out[self.h, 0, :, self.lanes]
            for o in range(1, row_outer):
                total = total + self.buffer_out[self.h, o, :, self.lanes]
            self.whole[self.h, rows_at(row_in), self.lanes] = total
            mine = self.view(self.whole, None, rows_at(row_in))
            self.third = [
                remote(mine, mine, sem.at[0, self.h, d], sem.at[1, self.h, d], (row_out * row_inner + peer, col))
                for d, peer in enumerate(inner_peers)
            ]
            for copy in self.third:
                copy.start()

        def end(self):
            for copy in self.third:
                copy.wait()

    gram_sums = [
        RowSum(gram_ref, gram_in, gram_out, gram_all, (gram_in_sem, gram_out_sem, gram_all_sem), h, (h + 1) * width)
        for h in range(halves)
    ]
    proj_sums = [
        RowSum(projected_ref, proj_in, proj_out, proj_all, (proj_in_sem, proj_out_sem, proj_all_sem), h, cols)
        for h in range(halves)
    ]
    block = corner.shape[0]

    def prepare_half(h):
        known = h * width
        shift = ridge * identity(width)
        gram = gram_all[h, :, known : known + width]
        if h == 0:
            inverse[...] = jnp.zeros_like(inverse)
            rest = None
        else:
            before = inverse[:known, :known]
            solved = contract(before, gram_all[h, :, :known], 1, 1, HIGHEST)
            gram = gram - contract(solved, solved, 0, 0, HIGHEST)
            rest = contract(solved, before, 0, 0, HIGHEST)
        work[:, :width] = gram + shift
        work[:, width:] = identity(width)
        return rest

    def finish_half(h, rest):
        known = h * width
        inverse[known : known + width, known : known + width] = diagonal[...]
        if h > 0:
            inverse[known : known + width, :known] = -contract(diagonal[...], rest, 1, 0, HIGHEST)

    def right_half(h):
        known = (h + 1) * width
        projected = proj_all[: h + 1].reshape(known, cols)
        factor = split(inverse[h * width : known, :known])
        right = contract_split(factor, split(projected), 1, 0)
        right_high[lanes_of(h), :], right_low[lanes_of(h), :] = split(right)
        squares = jnp.sum(right * right, axis=1, keepdims=True)
        squares_all[col, :, lanes_of(h)] = jnp.broadcast_to(squares, (width, LANES)).T[:SUBLANES, :]
        return right

    gram_ref[...] = jnp.zeros_like(gram_ref)
    projected_ref[...] = jnp.zeros_like(projected_ref)

    def open_chain(k, carry):
        own_part(k)
        chain(0, k)
        return carry

    lax.fori_loop(0, outer - 1, open_chain, 0)
    own_part(outer - 1)

    def form_some(q, carry):
        form(q)
        return carry

    lax.fori_loop(0, n_col // 2, form_some, 0)

    @pl.when(near == 0)
    def _():
        chain(1, 0)

    settle(0)
    weight_copy.wait()
    input_part = contract(cot_flat[...], weight[...], 1, 0)
    input_send[...] = input_part.reshape(n_row, act_rows, cols)
    input_copies = [
        remote(input_send.at[peer], input_recv.at[d], input_sem.at[0, d], input_sem.at[1, d], (peer, col))
        for d, peer in enumerate(row_peers)
    ]
    for copy in input_copies:
        copy.start()
    lax.fori_loop(n_col // 2, n_col, form_some, 0)

    def next_chain(k, carry):
        chain(1, k)
        return carry

    def next_forward(n, carry):
        forward(0, n)
        return carry

    def next_both(k, carry):
        chain(1, k)
        forward(0, k - 1)
        return carry

    @pl.when(near == 0)
    def _():
        lax.fori_loop(1, outer - 1, next_chain, 0)
        lax.fori_loop(0, outer - 2, next_forward, 0)

    @pl.when(near > 0)
    def _():
        chain(1, 0)
        lax.fori_loop(1, outer - 1, next_both, 0)

    absorb(0, col)
    settle(1)

    @pl.when(near > 0)
    def _():
        forward(0, outer - 2)


    def absorb_first(n, carry):
        absorb_outer(0, n)
        return carry

    lax.fori_loop(0, outer - 2, absorb_first, 0)
    absorb_inner(0, me_out)
    absorb(1, col)

    @pl.when(near == 0)
    def _():
        forward(0, outer - 2)

    absorb_outer(0, outer - 2)

    def absorb_second(n, carry):
        forward(1, n)
        absorb_inner(0, arrival(n))
        absorb_outer(1, n)
        return carry

    lax.fori_loop(0, outer - 2, absorb_second, 0)
    absorb_inner(0, arrival(outer - 2))
    gram_sums[0].begin()
    proj_sums[0].begin()
    absorb_inner(1, me_out)
    gram_sums[0].cross()
    proj_sums[0].cross()
    forward(1, outer - 2)
    absorb_outer(1, outer - 2)
    absorb_inner(1, arrival(0))
    gram_sums[0].spread()

    def absorb_third(n, carry):
        absorb_inner(1, arrival(n))
        return carry

    lax.fori_loop(1, outer - 1, absorb_third, 0)
    gram_sums[1].begin()
    proj_sums[1].begin()
    gram_sums[0].end()
    gram_sums[1].cross()
    proj_sums[1].cross()
    rest = prepare_half(0)
    for low in range(0, width, block):
        invert_block(low, block, work, corner, diagonal)
        if low == 0:
            gram_sums[1].spread()
            proj_sums[0].spread()
    finish_half(0, rest)
    proj_sums[0].end()
    right_turned_parts = [right_half(0)]
    gram_sums[1].end()
    rest = prepare_half(1)
    for low in range(0, width, block):
        invert_block(low, block, work, corner, diagonal)
        if low == 0:
            proj_sums[1].spread()
    finish_half(1, rest)
    proj_sums[1].end()
    right_turned_parts.append(right_half(1))

    copies = [
        remote(squares_all.at[col], squares_all.at[col], squares_sem.at[0, d], squares_sem.at[1, d], (row, peer))
        for d, peer in enumerate(col_peers)
    ]
    for copy in copies:
        copy.start()

    for h in range(halves):
        right_turned[:, lanes_of(h)] = right_turned_parts[h].T

    def result(q):
        return pltpu.make_async_copy(orthonormal.at[q], orthonormal_hbm.at[q], result_sem.at[q])

    right_copies = [
        pltpu.make_async_copy(right_high, right_high_hbm, result_sem.at[n_col]),
        pltpu.make_async_copy(right_low, right_low_hbm, result_sem.at[n_col + 1]),
        pltpu.make_async_copy(right_turned, right_turned_hbm, result_sem.at[n_col + 2]),
    ]
    for copy in right_copies:
        copy.start()

    def orthonormalise(q, carry):
        total = contract_split(split(left_ref[0, q]), split(inverse[:, :width]), 1, 1)
        for h in range(1, halves):
            total = total + contract_split(split(left_ref[h, q]), split(inverse[:, lanes_of(h)]), 1, 1)
        orthonormal[q] = total
        result(q).start()
        return carry

    lax.fori_loop(0, n_col, orthonormalise, 0)
    total = input_send[row]
    for d, copy in enumerate(input_copies):
        copy.wait()
        total = total + input_recv[d]
    input_ref[...] = total.astype(jnp.bfloat16)
    for q in range(n_col):
        store(q).wait()

    for h in range(halves):

        def drain(k, carry, h=h):
            for d in range(inner - 1):
                inner_copy(h, d, k).wait_send()
                gather_inner(h, d, k).wait_send()
            return carry

        lax.fori_loop(0, outer, drain, 0)

        def drain_chain(k, carry, h=h):
            chain_copy(h, k).wait_send()
            onward(h, arrival(k), False)
            return carry

        lax.fori_loop(0, outer - 1, drain_chain, 0)
        own_outward(h, False)

    for copy in copies:
        copy.wait()
    total = squares_all[0]
    for q in range(1, n_col):
        total = total + squares_all[q]
    scale_ref[...] = lax.rsqrt(total / din + 1e-06)
    for copy in right_copies:
        copy.wait()
    for q in range(n_col):
        result(q).wait()


def factor_call(n_row, n_col, ridge, activations, cotangent, weight, momentum, right_factor):
    inner, outer = two_stages(n_col)
    row_inner, row_outer = two_stages(n_row)
    rows, cols = momentum.shape
    rank = right_factor.shape[1]
    halves, width = 2, rank // 2
    piece = rows // n_col
    part = width // row_inner
    block = min(64, width)
    act_rows, cot_rows = activations.shape[0], cotangent.shape[0]
    tokens = act_rows * n_row
    f32, bf16 = jnp.float32, jnp.bfloat16
    vmem = pl.BlockSpec(memory_space=pltpu.VMEM)
    hbm = pl.BlockSpec(memory_space=pl.ANY)
    dma = pltpu.SemaphoreType.DMA
    return pl.pallas_call(
        functools.partial(factor_kernel, n_row, n_col, ridge),
        out_shape=(
            jax.ShapeDtypeStruct((act_rows, cols), bf16),
            jax.ShapeDtypeStruct((rows, cols), f32),
            jax.ShapeDtypeStruct((n_col, piece, rank), f32),
            jax.ShapeDtypeStruct((rank, cols), bf16),
            jax.ShapeDtypeStruct((rank, cols), bf16),
            jax.ShapeDtypeStruct((cols, rank), f32),
            jax.ShapeDtypeStruct((SUBLANES, rank), f32),
        ),
        in_specs=[vmem, vmem, hbm, hbm, vmem],
        out_specs=(vmem, hbm, hbm, hbm, hbm, hbm, vmem),
        scratch_shapes=[
            pltpu.VMEM((n_row, act_rows, cols), bf16),
            pltpu.VMEM((n_col, cot_rows, rows), bf16),
            pltpu.VMEM((tokens, rows), bf16),
            pltpu.VMEM((rows, tokens), bf16),
            pltpu.VMEM((n_col, piece, cols), f32),
            pltpu.VMEM((n_col, piece, cols), bf16),
            pltpu.VMEM((n_col, piece, cols), bf16),
            pltpu.VMEM((rows, cols), bf16),
            pltpu.VMEM((cols, rank), bf16),
            pltpu.VMEM((cols, rank), bf16),
            pltpu.VMEM((tokens, rank), f32),
            pltpu.VMEM((inner - 1, tokens, rank), f32),
            pltpu.VMEM((tokens, rank), bf16),
            pltpu.VMEM((tokens, rank), bf16),
            pltpu.VMEM((halves, inner - 1, outer, piece, width), f32),
            pltpu.VMEM((halves, inner - 1, outer, piece, width), f32),
            pltpu.VMEM((halves, outer, piece, width), f32),
            pltpu.VMEM((halves, outer + 1, piece, width), f32),
            pltpu.VMEM((halves, n_col, piece, width), f32),
            pltpu.VMEM((halves, width, rank), f32),
            pltpu.VMEM((halves, width, cols), f32),
            pltpu.VMEM((n_row, act_rows, cols), f32),
            pltpu.VMEM((n_row - 1, act_rows, cols), f32),
            pltpu.VMEM((halves, row_inner - 1, part, rank), f32),
            pltpu.VMEM((halves, row_outer, part, rank), f32),
            pltpu.VMEM((halves, width, rank), f32),
            pltpu.VMEM((halves, row_inner - 1, part, cols), f32),
            pltpu.VMEM((halves, row_outer, part, cols), f32),
            pltpu.VMEM((halves, width, cols), f32),
            pltpu.VMEM((rank, rank), f32),
            pltpu.VMEM((width, width), f32),
            pltpu.VMEM((width, 2 * width), f32),
            pltpu.VMEM((block, 2 * block), f32),
            pltpu.VMEM((n_col, SUBLANES, rank), f32),
            pltpu.VMEM((n_col, piece, rank), f32),
            pltpu.VMEM((rank, cols), bf16),
            pltpu.VMEM((rank, cols), bf16),
            pltpu.VMEM((cols, rank), f32),
            dma((n_col,)),
            dma((n_col,)),
            dma,
            dma((2, n_row - 1)),
            dma((2, n_col - 1)),
            dma((2, inner - 1)),
            dma((2, halves, inner - 1, outer)),
            dma((halves, outer)),
            dma((halves, outer + 1)),
            dma((halves, 2, outer)),
            dma((halves, outer)),
            dma((2, halves, inner - 1, outer)),
            dma((2, n_row - 1)),
            dma((2, halves, row_inner - 1)),
            dma((2, halves, row_outer - 1)),
            dma((2, halves, row_inner - 1)),
            dma((2, halves, row_inner - 1)),
            dma((2, halves, row_outer - 1)),
            dma((2, halves, row_inner - 1)),
            dma((2, n_col - 1)),
            dma((n_col + 3,)),
        ],
        compiler_params=pltpu.CompilerParams(
            collective_id=1, has_side_effects=True, vmem_limit_bytes=60 * 1024 * 1024
        ),
        name="factors",
    )(activations, cotangent, weight, momentum, right_factor)


def output_kernel(
    step_scale,
    buffer_ref,
    orthonormal_ref,
    right_high_ref,
    right_low_ref,
    right_turned_ref,
    scale_ref,
    sums_ref,
    momentum_ref,
    step_ref,
    next_ref,
    input_ref,
):
    input_ref[...] = sums_ref[...]
    right = jnp.concatenate([right_high_ref[...], right_high_ref[...], right_low_ref[...]], axis=0)

    def product(value):
        high, low = split(value)
        return contract(jnp.concatenate([high, low, high], axis=1), right, 1, 0)

    orthonormal = orthonormal_ref[...]
    momentum_ref[...] = buffer_ref[...] - (1.0 - momentum_decay) * product(orthonormal)
    step_ref[...] = (step_scale * product(orthonormal * scale_ref[:1, :])).astype(jnp.bfloat16)
    next_ref[...] = right_turned_ref[...] * scale_ref[:1, :]


def output_tile(rows, cols):
    fits = [t for t in range(16, min(rows // 4, 576) + 1, 16) if rows % t == 0 and cols % (rows // t * SUBLANES) == 0]
    return max(fits, default=0)


def output_call(step_scale, buffer, orthonormal, right_high, right_low, right_turned, scale, sums):
    rows, cols = buffer.shape
    rank = right_high.shape[0]
    tile = output_tile(rows, cols)
    steps = rows // tile
    f32 = jnp.float32
    whole = pl.BlockSpec((rank, cols), lambda i: (0, 0))
    return pl.pallas_call(
        functools.partial(output_kernel, step_scale),
        grid=(steps,),
        out_shape=(
            jax.ShapeDtypeStruct((rows, cols), f32),
            jax.ShapeDtypeStruct((rows, cols), jnp.bfloat16),
            jax.ShapeDtypeStruct((cols, rank), f32),
            jax.ShapeDtypeStruct(sums.shape, sums.dtype),
        ),
        in_specs=[
            pl.BlockSpec((tile, cols), lambda i: (i, 0)),
            pl.BlockSpec((tile, rank), lambda i: (i, 0)),
            whole,
            whole,
            pl.BlockSpec((cols // steps, rank), lambda i: (i, 0)),
            pl.BlockSpec(scale.shape, lambda i: (0, 0)),
            pl.BlockSpec(sums.shape, lambda i: (0, 0)),
        ],
        out_specs=(
            pl.BlockSpec((tile, cols), lambda i: (i, 0)),
            pl.BlockSpec((tile, cols), lambda i: (i, 0)),
            pl.BlockSpec((cols // steps, rank), lambda i: (i, 0)),
            pl.BlockSpec(sums.shape, lambda i: (0, 0)),
        ),
        compiler_params=pltpu.CompilerParams(
            dimension_semantics=("arbitrary",), vmem_limit_bytes=60 * 1024 * 1024
        ),
        name="outputs",
    )(buffer, orthonormal, right_high, right_low, right_turned, scale, sums)


def kernel_shards(n_row, n_col, activations, cotangent, weight, momentum, right_factor):
    rows, cols = momentum.shape
    rank = right_factor.shape[1]
    dout = rows * n_row
    input_sums, buffer, orthonormal, right_high, right_low, right_turned, scale = factor_call(
        n_row, n_col, ridge_weight * dout, activations, cotangent, weight, momentum, right_factor
    )
    step_scale = (dout / rank) ** 0.5
    momentum_next, weight_step, right_next, input_grad = output_call(
        step_scale, buffer, orthonormal.reshape(rows, rank), right_high, right_low, right_turned, scale, input_sums
    )
    return input_grad, momentum_next, right_next, weight_step


def shards(n_row, n_col, activations, cotangent, weight, momentum, right_factor):
    rows, cols = momentum.shape
    rank = right_factor.shape[1]
    aligned = (
        rows % (n_col * 2 * SUBLANES) == 0
        and rows % LANES == 0
        and cols % LANES == 0
        and rank % (2 * LANES) == 0
        and output_tile(rows, cols) > 0
        and activations.shape[0] % (2 * SUBLANES) == 0
        and cotangent.shape[0] % SUBLANES == 0
        and two_stages(n_row)[0] > 1
        and two_stages(n_col)[0] > 1
        and n_col % 2 == 0
        and rank % (2 * two_stages(n_row)[0] * SUBLANES) == 0
    )
    chosen = kernel_shards if aligned else plain_shards
    return chosen(n_row, n_col, activations, cotangent, weight, momentum, right_factor)


def solution(mesh):
    placed = (P("row", "col"), P("col", "row"), P("row", "col"), P("row", "col"), P("col", None))
    return jax.shard_map(
        functools.partial(shards, mesh.shape["row"], mesh.shape["col"]),
        mesh=mesh,
        in_specs=placed,
        out_specs=(P("row", "col"), P("row", "col"), P("col", None), P("row", "col")),
        check_vma=False,
    )
```
